32 devices in a mesh: ctx: 8 (over z, y), fsdp: 4 (over x, core).
Axes of the slice: x: 2, y: 2, z: 4, core: 2. Of those that a mesh axis runs over, the one named last changes fastest.
Arguments:
- tokens: bfloat16 [4, 1024, 768], P('fsdp', 'ctx'), may hold values from -6 to 6
- first_gain: bfloat16 [768], P('fsdp'), may hold values from 0.5 to 1.5
- first_bias: bfloat16 [768], P('fsdp'), may hold values from -4 to 4
- attn_weight: bfloat16 [768, 2304], P('fsdp'), may hold values from -0.3125 to 0.3125
- query_bias: bfloat16 [768], P('fsdp'), may hold values from -4 to 4
- value_bias: bfloat16 [768], P('fsdp'), may hold values from -4 to 4
- proj_weight: bfloat16 [768, 768], P('fsdp'), may hold values from -6 to 6
- proj_bias: bfloat16 [768], P('fsdp'), may hold values from -6 to 6
- second_gain: bfloat16 [768], P('fsdp'), may hold values from 0.5 to 1.5
- second_bias: bfloat16 [768], P('fsdp'), may hold values from -4 to 4
- fc_weight: bfloat16 [768, 3072], P('fsdp'), may hold values from -0.21875 to 0.21875
- fc_bias: bfloat16 [3072], P('fsdp'), may hold values from -6 to 6
- out_weight: bfloat16 [3072, 768], P('fsdp'), may hold values from -0.3125 to 0.3125
- out_bias: bfloat16 [768], P('fsdp'), may hold values from -6 to 6
- cotangent: bfloat16 [4, 1024, 768], P('fsdp', 'ctx'), may hold values from -6 to 6
Outputs:
- block_out: bfloat16 [4, 1024, 768], P('fsdp', 'ctx')
- input_grad: bfloat16 [4, 1024, 768], P('fsdp', 'ctx')
- first_gain_grad: float32 [768], P('fsdp')
- first_bias_grad: float32 [768], P('fsdp')
- attn_weight_grad: float32 [768, 2304], P('fsdp')
- query_bias_grad: float32 [768], P('fsdp')
- value_bias_grad: float32 [768], P('fsdp')
- proj_weight_grad: float32 [768, 768], P('fsdp')
- proj_bias_grad: float32 [768], P('fsdp')
- second_gain_grad: float32 [768], P('fsdp')
- second_bias_grad: float32 [768], P('fsdp')
- fc_weight_grad: float32 [768, 3072], P('fsdp')
- fc_bias_grad: float32 [3072], P('fsdp')
- out_weight_grad: float32 [3072, 768], P('fsdp')
- out_bias_grad: float32 [768], P('fsdp')
The draws below stay inside these ranges and needn't reach their ends.
All inputs are finite; a program needn't handle non-finite values.
Results may differ from the reference program's by a relative error of at most 0.017.
Values may be sent and summed in bfloat16 or wider, within the bound.
No kernel may reach another device: no remote copies, remote signals or barrier semaphores. Data moves between devices by JAX's collectives and lax.ppermute only.
A program may use at most 320 MiB of HBM per device.

```python
import jax
import jax.numpy as jnp
from jax import lax

D = 768
H = 12
HD = 64
FF = 3072
LAYERS = 12
LENGTH = 1024
SEQS = 4


def block_scale(own_key, extent, split, low, high):
    factor_of, own = 1.0, jax.random.fold_in(own_key, 6)
    for position, blocks in split:
        steps = jnp.exp(jax.random.uniform(jax.random.fold_in(own, position), (blocks,), jnp.float32, low / len(split), high / len(split)))
        factor_of = factor_of * jnp.repeat(steps, extent[position] // blocks).reshape([-1 if axis == position else 1 for axis in range(len(extent))])
    return factor_of


def scatter_about(stream_key, extent, scale, reach, cuts=(), kind=jnp.bfloat16):
    array = jax.random.normal(stream_key, extent, jnp.float32) * scale
    if len(cuts) > 0:
        array = block_scale(stream_key, extent, cuts, -0.22, 0.18) * array
    return jnp.clip(array, min=-reach, max=reach).astype(kind)


def setup_inputs(seed: int = 0) -> dict:
    key_list = jax.random.split(jax.random.key(seed), 16)
    return {
        "tokens": scatter_about(key_list[0], (SEQS, LENGTH, D), 1.0, 6.0, ((0, 4), (1, 8))),
        "first_gain": jnp.clip(1.0 + 0.1 * jax.random.normal(key_list[1], (D,), jnp.float32), 0.5, 1.5).astype(jnp.bfloat16),
        "first_bias": scatter_about(key_list[2], (D,), 0.3, 4.0, ((0, 4),)),
        "attn_weight": scatter_about(key_list[3], (D, 3 * D), (D // 2) ** -0.5, 0.3125, ((0, 4),)),
        "query_bias": scatter_about(key_list[4], (D,), 0.3, 4.0, ((0, 4),)),
        "value_bias": scatter_about(key_list[5], (D,), 0.3, 4.0, ((0, 4),)),
        "proj_weight": scatter_about(key_list[6], (D, D), (max(1, D // 512)) ** -0.5, 6.0, ((0, 4),)),
        "proj_bias": scatter_about(key_list[7], (D,), 0.5, 6.0, ((0, 4),)),
        "second_gain": jnp.clip(1.0 + 0.1 * jax.random.normal(key_list[8], (D,), jnp.float32), 0.5, 1.5).astype(jnp.bfloat16),
        "second_bias": scatter_about(key_list[9], (D,), 0.3, 4.0, ((0, 4),)),
        "fc_weight": scatter_about(key_list[10], (D, FF), D ** -0.5, 0.21875, ((0, 4),)),
        "fc_bias": scatter_about(key_list[11], (FF,), 0.5, 6.0, ((0, 4),)),
        "out_weight": scatter_about(key_list[12], (FF, D), (FF // 8) ** -0.5, 0.3125, ((0, 4),)),
        "out_bias": scatter_about(key_list[13], (D,), 0.5, 6.0, ((0, 4),)),
        "cotangent": scatter_about(key_list[14], (SEQS, LENGTH, D), 1.0, 6.0, ((0, 4), (1, 8))),
    }


EPSILON = 1e-05
HIGHEST = lax.Precision.HIGHEST

@jax.custom_vjp
def low(v):
    return lax.optimization_barrier(v.astype(jnp.bfloat16)).astype(jnp.float32)

@jax.custom_vjp
def low_back(v):
    return v

def low_keep(v):
    return (low(v), None)

def low_pass(kept, grad):
    return (grad,)

def back_keep(v):
    return (v, None)

def back_low(kept, grad):
    return (low(grad),)
low.defvjp(low_keep, low_pass)
low_back.defvjp(back_keep, back_low)

def layer_norm(values_in, norm_gain, norm_shift):
    center = lax.optimization_barrier(jnp.mean(values_in, axis=-1, keepdims=True))
    centered = values_in - center
    spread = lax.optimization_barrier(jnp.mean(centered * centered, axis=-1, keepdims=True))
    return centered * lax.rsqrt(spread + EPSILON) * norm_gain + norm_shift

def attend(queries, key_rows, value_rows):
    seq_len = queries.shape[0]
    block_rows = min(512, seq_len)
    key_index = jnp.arange(seq_len, dtype=jnp.int32)

    def one_block(number):
        offset = number * block_rows
        query_rows = lax.dynamic_slice_in_dim(queries, offset, block_rows, 0)
        scores = jnp.einsum('qhd,khd->hqk', query_rows, key_rows, precision=HIGHEST) * HD ** (-0.5)
        scores = low_back(scores)
        query_index = offset + jnp.arange(block_rows, dtype=jnp.int32)
        visible = key_index[None, :] <= query_index[:, None]
        scores = jnp.where(visible[None], scores, -1e+30)
        highest = lax.optimization_barrier(jnp.max(scores, axis=-1, keepdims=True))
        log_total = highest + jnp.log(lax.optimization_barrier(jnp.sum(jnp.exp(scores - highest), axis=-1, keepdims=True)))
        weights = low(jnp.exp(scores - log_total))
        return jnp.einsum('hqk,khd->qhd', weights, value_rows, precision=HIGHEST)
    blocks = lax.map(jax.checkpoint(one_block), jnp.arange(seq_len // block_rows, dtype=jnp.int32))
    return blocks.reshape(seq_len, H * HD)

def block_forward(sequence, params):
    gain_one, shift_one, attn_matrix, query_shift, value_shift, proj_matrix, proj_shift, gain_two, shift_two, fc_matrix, fc_shift, out_matrix, out_shift = params
    seq_len = sequence.shape[0]
    normed = low(layer_norm(sequence, gain_one, shift_one))
    mixed_rows = jnp.dot(normed, attn_matrix, precision=HIGHEST)
    queries = low(low_back(mixed_rows[:, :D] + query_shift))
    key_rows = low(low_back(mixed_rows[:, D:2 * D]))
    value_rows = low(low_back(mixed_rows[:, 2 * D:] + value_shift))
    attended = attend(queries.reshape(seq_len, H, HD), key_rows.reshape(seq_len, H, HD), value_rows.reshape(seq_len, H, HD))
    attended = low(low_back(attended))
    branch = low_back(jnp.dot(attended, proj_matrix, precision=HIGHEST) + proj_shift)
    middle = sequence + LAYERS ** (-0.5) * branch
    normed_two = low(layer_norm(middle, gain_two, shift_two))
    hidden = low_back(jnp.dot(normed_two, fc_matrix, precision=HIGHEST) + fc_shift)
    active = low(jax.nn.gelu(hidden, approximate=True))
    output = low_back(jnp.dot(active, out_matrix, precision=HIGHEST) + out_shift)
    return middle + LAYERS ** (-0.5) * output

def reference(tokens, first_gain, first_bias, attn_weight, query_bias, value_bias, proj_weight, proj_bias, second_gain, second_bias, fc_weight, fc_bias, out_weight, out_bias, cotangent):
    params = tuple((weight_arg.astype(jnp.float32) for weight_arg in (first_gain, first_bias, attn_weight, query_bias, value_bias, proj_weight, proj_bias, second_gain, second_bias, fc_weight, fc_bias, out_weight, out_bias)))

    def forward(inputs, param_set):
        return lax.map(lambda sequence: block_forward(sequence, param_set), inputs)
    result, pullback = jax.vjp(forward, tokens.astype(jnp.float32), params)
    input_grad, param_grads = pullback(cotangent.astype(jnp.float32))
    return (result.astype(jnp.bfloat16), input_grad.astype(jnp.bfloat16), param_grads[0], param_grads[1], param_grads[2], param_grads[3], param_grads[4], param_grads[5], param_grads[6], param_grads[7], param_grads[8], param_grads[9], param_grads[10], param_grads[11], param_grads[12])
```

```python
from functools import partial

import jax
import jax.numpy as jnp
from jax import lax
from jax.experimental import pallas as pl
from jax.experimental.pallas import tpu as pltpu
from jax.sharding import PartitionSpec as P

HD = 64
LAYERS = 12
EPSILON = 1e-05
BF = jnp.bfloat16
F32 = jnp.float32
RESIDUAL = LAYERS ** (-0.5)
SCORE = HD ** (-0.5)
NEVER = -1e30
VMEM_BYTES = 50 * 1024 * 1024


def shape(dims, kind):
    return jax.ShapeDtypeStruct(dims, kind)


def call(body, name, outs, *args, scratch=()):
    vmem = pl.BlockSpec(memory_space=pltpu.VMEM)
    smem = pl.BlockSpec(memory_space=pltpu.SMEM)
    return pl.pallas_call(
        body,
        name=name,
        out_shape=outs,
        in_specs=[smem] + [vmem] * (len(args) - 1),
        out_specs=[vmem] * len(outs),
        scratch_shapes=list(scratch),
        compiler_params=pltpu.CompilerParams(vmem_limit_bytes=VMEM_BYTES),
    )(*args)


def rows_at(index, size):
    return pl.ds(pl.multiple_of(index * size, size), size)


def dot(first, second):
    return jnp.dot(first, second, preferred_element_type=F32)


def dot_rows(first, second):
    return lax.dot_general(first, second, (((0,), (0,)), ((), ())), preferred_element_type=F32)


def dot_columns(first, second):
    return lax.dot_general(first, second, (((1,), (1,)), ((), ())), preferred_element_type=F32)


def normalize(values):
    center = jnp.mean(values, axis=-1, keepdims=True)
    centered = values - center
    spread = jnp.mean(centered * centered, axis=-1, keepdims=True)
    scale = lax.rsqrt(spread + EPSILON)
    return centered * scale, scale


def norm_back(grad, unit, scale, gain):
    inner = grad * gain
    mean_inner = jnp.mean(inner, axis=-1, keepdims=True)
    mean_along = jnp.mean(inner * unit, axis=-1, keepdims=True)
    return scale * (inner - mean_inner - unit * mean_along)


def join_body(at, *refs):
    pieces, (whole,) = refs[:-1], refs[-1:]
    size = pieces[0].shape[0]
    for k, piece in enumerate(pieces):
        whole[rows_at(at[2] ^ k, size), :] = piece[...]


def mixed_body(parts, rows, at, gathered, bias, *refs):
    weights, (normed, matrix, vectors), outs = refs[:parts], refs[parts : parts + 3], refs[parts + 3 : -1]
    kept = refs[-1]
    width = weights[0].shape[0]
    features = parts * width
    for k, piece in enumerate(weights):
        matrix[rows_at(at[2] ^ k, width), :] = piece[...]
    small = jnp.concatenate([gathered[j, rows : rows + 8, :width] for j in range(parts)], axis=1).astype(F32)
    vectors[...] = small
    for j in range(parts):
        unit, _ = normalize(gathered[j, :rows, :].astype(F32))
        normed[j * rows : (j + 1) * rows, :] = (unit * small[0:1] + small[1:2]).astype(BF)
    kept[...] = (dot(normed[...], matrix[...]) + bias[...]).astype(BF)
    count = len(outs) // 2
    for k in range(count):
        block = rows_at(at[0] ^ k, rows)
        outs[k][...] = kept[block, :256]
        outs[count + k][...] = kept[block, 256:]


def place(at, count, blocks, rows, queries, pairs, partners, q_all, kv_all):
    for k in range(count):
        row = at[0] ^ k
        q_all[rows_at(row, rows), :] = queries[k][...]
        kv_all[rows_at(row * blocks + at[1], rows), :] = pairs[k][...]
        for j, partner in enumerate(partners):
            side = row * blocks + (at[1] ^ (j + 1))
            kv_all[rows_at(side, rows), :] = partner[k * rows : (k + 1) * rows, :]


def head_views(tile_one, tile_two, scale):
    low = lax.broadcasted_iota(jnp.int32, tile_one.shape, 1) < HD
    zero = jnp.zeros_like(tile_one)
    tile_one = tile_one * scale if scale is not None else tile_one
    tile_two = tile_two * scale if scale is not None else tile_two
    return (jnp.where(low, tile_one, zero), jnp.where(low, zero, tile_one), tile_two)


def visible_keys(at, i, blocks, rows, keys):
    query = (i * blocks + at[1]) * rows + lax.broadcasted_iota(jnp.int32, (rows, keys), 0)
    return lax.broadcasted_iota(jnp.int32, (rows, keys), 1) <= query


def attend_body(count, blocks, rows, at, *refs):
    queries, pairs = refs[:count], refs[count : 2 * count]
    partners = refs[2 * count : 2 * count + blocks - 1]
    outs = refs[2 * count + blocks - 1 :]
    pieces, (exact, totals, q_all, kv_all) = outs[:count], outs[count:]
    place(at, count, blocks, rows, queries, pairs, partners, q_all, kv_all)
    low = lax.broadcasted_iota(jnp.int32, (rows, 128), 1) < HD
    for i in range(count):
        keys = (i + 1) * blocks * rows
        mine = slice(i * rows, (i + 1) * rows)
        heads = head_views(q_all[mine, :128], q_all[mine, 128:], SCORE)
        seen = visible_keys(at, i, blocks, rows, keys)
        found = []
        for h, query in enumerate(heads):
            key_cols = slice(0, 128) if h < 2 else slice(256, 384)
            value_cols = slice(128, 256) if h < 2 else slice(256, 384)
            scores = jnp.where(seen, dot_columns(query, kv_all[:keys, key_cols]), NEVER)
            highest = jnp.max(scores, axis=-1, keepdims=True)
            weights = jnp.exp(scores - highest)
            total = jnp.sum(weights, axis=-1, keepdims=True)
            totals[mine, h : h + 1] = highest + jnp.log(total)
            weights = (weights * (1.0 / total)).astype(BF)
            found.append(dot(weights, kv_all[:keys, value_cols]))
        exact[mine, :128] = jnp.where(low, found[0], found[1])
        exact[mine, 128:] = jnp.where(low, 0.0, found[2])
    for k in range(count):
        pieces[k][...] = exact[rows_at(at[0] ^ k, rows), :].astype(BF)


def attend_back_body(count, blocks, rows, at, *refs):
    grads, (q_all, kv_all, exact, totals) = refs[:count], refs[count : count + 4]
    outs = refs[count + 4 :]
    pieces, (own, away), (g_all, dq_all, acc) = outs[:count], outs[count : count + 2], outs[count + 2 :]
    for k in range(count):
        g_all[rows_at(at[0] ^ k, rows), :] = grads[k][...]
    acc[...] = jnp.zeros_like(acc)
    low = lax.broadcasted_iota(jnp.int32, (rows, 128), 1) < HD
    for i in range(count):
        keys = (i + 1) * blocks * rows
        mine = slice(i * rows, (i + 1) * rows)
        q_heads = head_views(q_all[mine, :128], q_all[mine, 128:], SCORE)
        g_heads = head_views(g_all[mine, :128], g_all[mine, 128:], None)
        seen = visible_keys(at, i, blocks, rows, keys)
        found = []
        for h in range(3):
            key_cols = slice(0, 128) if h < 2 else slice(256, 384)
            value_cols = slice(128, 256) if h < 2 else slice(256, 384)
            kept = exact[mine, :128] if h < 2 else exact[mine, 128:]
            delta = jnp.sum(g_heads[h].astype(F32) * kept, axis=-1, keepdims=True)
            scores = dot_columns(q_heads[h], kv_all[:keys, key_cols]) - totals[mine, h : h + 1]
            weights = jnp.exp(jnp.where(seen, scores, NEVER))
            g_weights = dot_columns(g_heads[h], kv_all[:keys, value_cols])
            g_scores = (weights * (g_weights - delta)).astype(BF)
            found.append(dot(g_scores, kv_all[:keys, key_cols]))
            acc[:keys, key_cols] += dot_rows(g_scores, q_heads[h])
            acc[:keys, value_cols] += dot_rows(weights.astype(BF), g_heads[h])
        dq_all[mine, :128] = (jnp.where(low, found[0], found[1]) * SCORE).astype(BF)
        dq_all[mine, 128:] = (jnp.where(low, found[2], 0.0) * SCORE).astype(BF)
    for k in range(count):
        row = at[0] ^ k
        pieces[k][...] = dq_all[rows_at(row, rows), :]
        into = slice(k * rows, (k + 1) * rows)
        own[into, :] = acc[rows_at(row * blocks + at[1], rows), :]
        for j in range(1, blocks):
            from_rows = slice((j - 1) * count * rows + k * rows, (j - 1) * count * rows + (k + 1) * rows)
            away[from_rows, :] = acc[rows_at(row * blocks + (at[1] ^ j), rows), :].astype(BF)


def plain_heads(values):
    zero = jnp.zeros_like(values[:, :HD])
    first = jnp.concatenate([values[:, :HD], zero], 1)
    second = jnp.concatenate([zero, values[:, HD:128]], 1)
    return (first, second, values[:, 128:])


def plain_terms(at, count, blocks, rows):
    q_pos = (jnp.arange(count)[:, None] * blocks + at[1]) * rows + jnp.arange(rows)[None]
    k_pos = jnp.arange(count * blocks * rows)
    return k_pos[None] <= q_pos.reshape(-1)[:, None]


def plain_attend(count, blocks, rows, at, queries, pairs, partners):
    width = pairs[0].shape[1]
    q_all = jnp.zeros((count, rows, queries[0].shape[1]), BF)
    kv_all = jnp.zeros((count, blocks, rows, width), BF)
    for k in range(count):
        row = at[0] ^ k
        q_all = q_all.at[row].set(queries[k])
        kv_all = kv_all.at[row, at[1]].set(pairs[k])
        for j, partner in enumerate(partners):
            kv_all = kv_all.at[row, at[1] ^ (j + 1)].set(partner[k * rows : (k + 1) * rows])
    q_all, kv_all = q_all.reshape(count * rows, -1), kv_all.reshape(-1, width)
    seen = plain_terms(at, count, blocks, rows)
    found, totals = [], []
    for h, query in enumerate(plain_heads(q_all)):
        key = kv_all[:, :128] if h < 2 else kv_all[:, 256:]
        value = kv_all[:, 128:256] if h < 2 else kv_all[:, 256:]
        scores = jnp.where(seen, dot_columns(query, key) * SCORE, NEVER)
        total = jax.nn.logsumexp(scores, axis=-1, keepdims=True)
        found.append(dot(jnp.exp(scores - total).astype(BF), value))
        totals.append(total)
    exact = jnp.concatenate([found[0][:, :HD], found[1][:, HD:], jnp.zeros_like(found[2][:, :HD]), found[2][:, HD:]], 1)
    grid = exact.astype(BF).reshape(count, rows, -1)
    pieces = [grid[at[0] ^ k] for k in range(count)]
    totals = jnp.concatenate(totals + [jnp.zeros((count * rows, 125), F32)], 1)
    return (*pieces, exact, totals, q_all, kv_all)


def plain_attend_back(count, blocks, rows, at, grads, q_all, kv_all, exact, totals):
    g_all = jnp.zeros((count, rows, grads[0].shape[1]), BF)
    for k in range(count):
        g_all = g_all.at[at[0] ^ k].set(grads[k])
    g_all = g_all.reshape(count * rows, -1)
    seen = plain_terms(at, count, blocks, rows)
    dq, parts = [], []
    for h, (query, grad, kept) in enumerate(zip(plain_heads(q_all), plain_heads(g_all), plain_heads(exact))):
        key = kv_all[:, :128] if h < 2 else kv_all[:, 256:]
        value = kv_all[:, 128:256] if h < 2 else kv_all[:, 256:]
        delta = jnp.sum(grad.astype(F32) * kept, axis=-1, keepdims=True)
        scores = dot_columns(query, key) * SCORE - totals[:, h : h + 1]
        weights = jnp.exp(jnp.where(seen, scores, NEVER))
        g_scores = (weights * (dot_columns(grad, value) - delta)).astype(BF)
        dq.append(dot(g_scores, key) * SCORE)
        parts.append((dot_rows(g_scores, query) * SCORE, dot_rows(weights.astype(BF), grad)))
    dq = jnp.concatenate([dq[0][:, :HD], dq[1][:, HD:], dq[2][:, :HD], jnp.zeros_like(dq[2][:, :HD])], 1)
    dq = dq.astype(BF).reshape(count, rows, -1)
    acc = jnp.concatenate([parts[0][0] + parts[1][0], parts[0][1] + parts[1][1], parts[2][0] + parts[2][1]], 1)
    acc = acc.reshape(count, blocks, rows, -1)
    pieces = [dq[at[0] ^ k] for k in range(count)]
    own = jnp.concatenate([acc[at[0] ^ k, at[1]] for k in range(count)], 0)
    away = [acc[at[0] ^ k, at[1] ^ j].astype(BF) for j in range(1, blocks) for k in range(count)]
    return (*pieces, own, jnp.concatenate(away, 0))


def merge_body(count, rows, at, own, *refs):
    arrived, outs = refs[:-count], refs[-count:]
    for k in range(count):
        part = slice(k * rows, (k + 1) * rows)
        total = own[part, :]
        for ref in arrived:
            total = total + ref[part, :].astype(F32)
        outs[k][...] = total.astype(BF)


def gelu_terms(hidden):
    root = 0.7978845608028654
    square = hidden * hidden
    bend = jnp.tanh(root * hidden * (1.0 + 0.044715 * square))
    half = 0.5 * (1.0 + bend)
    slope = half + 0.5 * hidden * (1.0 - bend * bend) * root * (1.0 + 3.0 * 0.044715 * square)
    return hidden * half, slope


def middle_body(parts, rows, at, attended, tok, extra, vectors, fc, fc_bias, out, *refs):
    gn_mine, gn_other, mid_mine, normed, active, g_hidden, att_all, proj, mid = refs
    width = extra.shape[1] - rows
    zero = jnp.zeros((HD, proj.shape[1]), BF)
    for j in range(parts):
        weight = extra[j, rows:, :]
        proj[j * 256 : j * 256 + 128, :] = weight[:128]
        proj[j * 256 + 128 : j * 256 + 128 + HD, :] = zero
        proj[j * 256 + 128 + HD : (j + 1) * 256, :] = weight[128:width]
        for k in range(parts):
            att_all[rows_at(at[0] ^ k, rows), j * 256 : (j + 1) * 256] = attended[j, k * rows : (k + 1) * rows, :]
    branch = dot(att_all[...], proj[...]) + vectors[4:5]
    for j in range(parts):
        part = slice(j * rows, (j + 1) * rows)
        value = tok[j, :rows, :].astype(F32) + RESIDUAL * branch[part]
        mid[part, :] = value
        unit, _ = normalize(value)
        normed[part, :] = (unit * vectors[2:3] + vectors[3:4]).astype(BF)
    hidden = dot(normed[...], fc[...]) + fc_bias[...].astype(F32)
    value, slope = gelu_terms(hidden)
    active[...] = value.astype(BF)
    g_out = jnp.concatenate([(RESIDUAL * extra[j, :rows, :].astype(F32)).astype(BF) for j in range(parts)], axis=0)
    g_hidden[...] = (dot_columns(g_out, out[...]) * slope).astype(BF)
    grad = dot_columns(g_hidden[...], fc[...])
    core = at[3]
    for s in range(parts):
        part = slice(s * rows, (s + 1) * rows)
        into = slice((s // 2) * rows, (s // 2 + 1) * rows)

        @pl.when(core == s % 2)
        def _():
            gn_mine[into, :] = grad[part]
            mid_mine[into, :] = mid[part, :]

        @pl.when(core != s % 2)
        def _():
            gn_other[into, :] = grad[part]


def weights_body(parts, rows, ways, at, extra, normed, active, g_hidden, out, *refs):
    mine, other, out_grad, fc_grad, sums = refs
    g_out = jnp.concatenate([(RESIDUAL * extra[j, :rows, :].astype(F32)).astype(BF) for j in range(parts)], axis=0)
    result = dot(active[...], out[...])
    core = at[3]
    for s in range(parts):
        part = slice(s * rows, (s + 1) * rows)
        into = slice((s // 2) * rows, (s // 2 + 1) * rows)

        @pl.when(core == s % 2)
        def _():
            mine[into, :] = result[part]

        @pl.when(core != s % 2)
        def _():
            other[into, :] = result[part]

    grad = dot_rows(active[...], g_out)
    size = grad.shape[0] // ways
    for c in range(ways):
        out_grad[c, :, :] = grad[c * size : (c + 1) * size].astype(BF)
    grad = dot_rows(normed[...], g_hidden[...])
    size = grad.shape[0] // (ways * parts)
    for c in range(ways):
        for j in range(parts):
            at_row = (j * ways + c) * size
            fc_grad[c, j, :, :] = grad[at_row : at_row + size].astype(BF)
    sums[...] = jnp.zeros_like(sums)
    sums[0:1, :] = jnp.sum(g_out.astype(F32), axis=0, keepdims=True)
    sums[1:2, :] = jnp.sum(g_hidden[...].astype(F32), axis=0, keepdims=True)


def second_norm_body(rows, at, chip_sum, arrived, mid, extra, vectors, g_branch, own_middle, sums):
    grad = chip_sum[...] + arrived[...].astype(F32)
    unit, scale = normalize(mid[...])
    back = norm_back(grad, unit, scale, vectors[2:3])
    sums[...] = jnp.zeros_like(sums)
    sums[0:1, :] = jnp.sum(grad * unit, axis=0, keepdims=True)
    sums[1:2, :] = jnp.sum(grad, axis=0, keepdims=True)
    core = at[3]
    for j in range(2):
        part = slice(j * rows, (j + 1) * rows)
        g_middle = back[part] + extra[2 * j + core, :rows, :].astype(F32)
        g_branch[part, :] = (RESIDUAL * g_middle).astype(BF)

        @pl.when(at[2] == 2 * j + core)
        def _():
            own_middle[...] = g_middle


def attended_grad_body(parts, rows, at, mine, other, proj, *refs):
    outs, (kept, g_all) = refs[:parts], refs[parts:]
    core = at[3]
    for j in range(2):
        part = slice(j * rows, (j + 1) * rows)
        kept[rows_at(2 * j + core, rows), :] = mine[part, :]
        kept[rows_at(2 * j + 1 - core, rows), :] = other[part, :]
    zero = jnp.zeros((HD, proj.shape[1]), BF)
    weight = jnp.concatenate([proj[:128, :], zero, proj[128:, :]], axis=0)
    g_all[...] = dot_columns(kept[...], weight).astype(BF)
    for k in range(parts):
        outs[k][...] = g_all[rows_at(at[0] ^ k, rows), :]


def proj_grad_body(parts, rows, ways, at, attended, g_branch, proj_grad, sums):
    grad = jnp.zeros((256, g_branch.shape[1]), F32)
    for k in range(parts):
        grad = grad + dot_rows(attended[k * rows : (k + 1) * rows, :], g_branch[rows_at(at[0] ^ k, rows), :])
    grad = jnp.concatenate([grad[:128], grad[128 + HD :]], axis=0)
    size = grad.shape[0] // ways
    for c in range(ways):
        proj_grad[c, :, :] = grad[c * size : (c + 1) * size].astype(BF)
    sums[...] = jnp.zeros_like(sums)
    sums[0:1, :] = jnp.sum(g_branch[...].astype(F32), axis=0, keepdims=True)


def first_grad_body(parts, rows, ways, at, normed, matrix, *refs):
    queries, pairs = refs[:parts], refs[parts : 2 * parts]
    mine, other, grads, sums, mixed = refs[2 * parts :]
    for k in range(parts):
        block = rows_at(at[0] ^ k, rows)
        mixed[block, :256] = queries[k][...]
        mixed[block, 256:] = pairs[k][...]
    back = dot_columns(mixed[...], matrix[...])
    core = at[3]
    for s in range(parts):
        part = slice(s * rows, (s + 1) * rows)
        into = slice((s // 2) * rows, (s // 2 + 1) * rows)

        @pl.when(core == s % 2)
        def _():
            mine[into, :] = back[part]

        @pl.when(core != s % 2)
        def _():
            other[into, :] = back[part]

    grad = dot_rows(normed[...], mixed[...])
    size = grad.shape[0] // (ways * parts)
    for c in range(ways):
        for j in range(parts):
            at_row = (j * ways + c) * size
            grads[c, j, :, :] = grad[at_row : at_row + size].astype(BF)
    sums[...] = jnp.zeros_like(sums)
    sums[0:1, :] = jnp.sum(mixed[...].astype(F32), axis=0, keepdims=True)


def first_norm_body(at, own, arrived, tokens, own_middle, vectors, input_grad, sums):
    grad = own[...] + arrived[...].astype(F32)
    unit, scale = normalize(tokens[...].astype(F32))
    back = norm_back(grad, unit, scale, vectors[0:1])
    input_grad[...] = (back + own_middle[...]).astype(BF)
    sums[...] = jnp.zeros_like(sums)
    sums[0:1, :] = jnp.sum(grad * unit, axis=0, keepdims=True)
    sums[1:2, :] = jnp.sum(grad, axis=0, keepdims=True)


def shards(
    parts,
    ways,
    tokens,
    first_gain,
    first_bias,
    attn_weight,
    query_bias,
    value_bias,
    proj_weight,
    proj_bias,
    second_gain,
    second_bias,
    fc_weight,
    fc_bias,
    out_weight,
    out_bias,
    cotangent,
):
    rows, features = tokens.shape[1], tokens.shape[2]
    width = features // parts
    count = parts
    blocks = ways // count
    hidden = fc_weight.shape[1] // parts
    f = lax.axis_index("fsdp").astype(jnp.int32)
    c = lax.axis_index("ctx").astype(jnp.int32)
    a, b, core = c // blocks, c % blocks, f % 2
    at = jnp.stack([a, b, f, core])

    def over_fsdp(value, k):
        return lax.ppermute(value, "fsdp", [(i, i ^ k) for i in range(parts)])

    def over_ctx(value, k):
        return lax.ppermute(value, "ctx", [(i, i ^ k) for i in range(ways)])

    tok, cot = tokens[0], cotangent[0]

    small = jnp.stack([first_gain, first_bias, second_gain, second_bias, proj_bias, out_bias])
    small = jnp.pad(small, ((0, 2), (0, features - width)))
    tok_all = lax.all_gather(jnp.concatenate([tok, small], 0), "fsdp")
    split = attn_weight.reshape(width, 3, parts, width)
    zero = jnp.zeros((width, HD), BF)

    def head_columns(owner):
        q, k, v = (lax.dynamic_index_in_dim(split[:, i], owner, 1, keepdims=False) for i in range(3))
        return jnp.concatenate([q, zero, k[:, :128], v[:, :128], k[:, 128:], v[:, 128:]], 1)

    attn_pieces = [head_columns(f)] + [over_fsdp(head_columns(f ^ k), k) for k in range(1, parts)]
    fc_split = fc_weight.reshape(width, parts, hidden)

    def fc_columns(owner):
        return lax.dynamic_index_in_dim(fc_split, owner, 1, keepdims=False)

    fc_pieces = [fc_columns(f)] + [over_fsdp(fc_columns(f ^ k), k) for k in range(1, parts)]
    extra = lax.all_gather(jnp.concatenate([cot, proj_weight], 0), "fsdp")

    none = jnp.zeros((128,), F32)
    vb = value_bias.astype(F32)
    bias = jnp.concatenate([query_bias.astype(F32), none[:HD], none, vb[:128], none[:HD], vb[128:]])[None]
    columns = bias.shape[1]
    mixed = call(
        partial(mixed_body, parts, rows),
        "mixed",
        [shape((parts * rows, features), BF), shape((features, columns), BF), shape((8, features), F32)]
        + [shape((rows, 256), BF)] * count
        + [shape((rows, 384), BF)] * count,
        at,
        tok_all,
        bias,
        *attn_pieces,
        scratch=[pltpu.VMEM((parts * rows, columns), BF)],
    )
    normed, attn_matrix, vectors = mixed[:3]
    queries, pairs = mixed[3 : 3 + count], mixed[3 + count :]

    pairs = [pairs[0]] + [over_ctx(pairs[k], k * blocks) for k in range(1, count)]
    queries = [queries[0]] + [over_ctx(queries[k], k * blocks) for k in range(1, count)]
    joined = jnp.concatenate(pairs, 0)
    partners = [over_ctx(joined, j) for j in range(1, blocks)]
    small_blocks = blocks * count * rows <= 1024
    if small_blocks:
        kept = call(
            partial(attend_body, count, blocks, rows),
            "attend",
            [shape((rows, 256), BF)] * count
            + [
                shape((count * rows, 256), F32),
                shape((count * rows, 128), F32),
                shape((count * rows, 256), BF),
                shape((count * blocks * rows, 384), BF),
            ],
            at,
            *queries,
            *pairs,
            *partners,
        )
    else:
        kept = plain_attend(count, blocks, rows, at, queries, pairs, partners)
    att_pieces, state = kept[:count], kept[count:]
    att_pieces = [att_pieces[0]] + [over_ctx(att_pieces[k], k * blocks) for k in range(1, count)]
    attended = jnp.concatenate(att_pieces, 0)
    attended_all = lax.all_gather(attended, "fsdp")
    fc_matrix = call(join_body, "join", [shape((features, hidden), BF)], at, *fc_pieces)[0]

    half = parts * rows // 2
    gn_mine, gn_other, mid_mine, normed_two, active, g_hidden = call(
        partial(middle_body, parts, rows),
        "middle",
        [shape((half, features), F32)] * 3
        + [shape((parts * rows, features), BF), shape((parts * rows, hidden), BF), shape((parts * rows, hidden), BF)],
        at,
        attended_all,
        tok_all,
        extra,
        vectors,
        fc_matrix,
        fc_bias[None],
        out_weight,
        scratch=[
            pltpu.VMEM((parts * rows, parts * 256), BF),
            pltpu.VMEM((parts * 256, features), BF),
            pltpu.VMEM((parts * rows, features), F32),
        ],
    )
    chip_sum = gn_mine + over_fsdp(gn_other, 1)
    arrived = over_fsdp(chip_sum.astype(BF), 2)
    size = features // (ways * parts)
    mine, other, out_grad, fc_grad, sums_mlp = call(
        partial(weights_body, parts, rows, ways),
        "mlp_weights",
        [
            shape((half, features), F32),
            shape((half, features), F32),
            shape((ways, hidden // ways, features), BF),
            shape((ways, parts, size, hidden), BF),
            shape((8, features), F32),
        ],
        at,
        extra,
        normed_two,
        active,
        g_hidden,
        out_weight,
    )
    g_branch, own_middle, sums_two = call(
        partial(second_norm_body, rows),
        "second_norm",
        [shape((half, features), BF), shape((rows, features), F32), shape((8, features), F32)],
        at,
        chip_sum,
        arrived,
        mid_mine,
        extra,
        vectors,
    )
    other_branch = over_fsdp(g_branch, 1)
    grads = call(
        partial(attended_grad_body, parts, rows),
        "attended_grad",
        [shape((rows, 256), BF)] * parts + [shape((parts * rows, features), BF)],
        at,
        g_branch,
        other_branch,
        proj_weight,
        scratch=[pltpu.VMEM((parts * rows, 256), BF)],
    )
    g_pieces, g_branch_all = grads[:parts], grads[parts]
    g_pieces = [g_pieces[0]] + [over_ctx(g_pieces[k], k * blocks) for k in range(1, count)]
    proj_grad, sums_proj = call(
        partial(proj_grad_body, parts, rows, ways),
        "proj_weight_grad",
        [shape((ways, width // ways, features), BF), shape((8, features), F32)],
        at,
        attended,
        g_branch_all,
    )
    if small_blocks:
        back = call(
            partial(attend_back_body, count, blocks, rows),
            "attend_back",
            [shape((rows, 256), BF)] * count
            + [shape((count * rows, 384), F32), shape(((blocks - 1) * count * rows, 384), BF)],
            at,
            *g_pieces,
            state[2],
            state[3],
            state[0],
            state[1],
            scratch=[
                pltpu.VMEM((count * rows, 256), BF),
                pltpu.VMEM((count * rows, 256), BF),
                pltpu.VMEM((count * blocks * rows, 384), F32),
            ],
        )
    else:
        back = plain_attend_back(count, blocks, rows, at, g_pieces, state[2], state[3], state[0], state[1])
    dq, own, away = back[:count], back[count], back[count + 1]
    stack = count * rows
    from_partners = [over_ctx(away[(j - 1) * stack : j * stack], j) for j in range(1, blocks)]
    dkv = call(partial(merge_body, count, rows), "merge", [shape((rows, 384), BF)] * count, at, own, *from_partners)
    dq = [dq[0]] + [over_ctx(dq[k], k * blocks) for k in range(1, count)]
    dkv = [dkv[0]] + [over_ctx(dkv[k], k * blocks) for k in range(1, count)]
    g1_mine, g1_other, attn_grad, sums_attn = call(
        partial(first_grad_body, parts, rows, ways),
        "first_grad",
        [
            shape((half, features), F32),
            shape((half, features), F32),
            shape((ways, parts, size, columns), BF),
            shape((8, columns), F32),
        ],
        at,
        normed,
        attn_matrix,
        *dq,
        *dkv,
        scratch=[pltpu.VMEM((parts * rows, columns), BF)],
    )

    def own_rows(values, place):
        return lax.dynamic_slice_in_dim(values, place * rows, rows, 0)

    x = f // 2
    first_sum = g1_mine + over_fsdp(g1_other, 1)
    first_arrived = over_fsdp(own_rows(first_sum, 1 - x).astype(BF), 2)
    input_grad, sums_one = call(
        first_norm_body,
        "first_norm",
        [shape((rows, features), BF), shape((8, features), F32)],
        at,
        own_rows(first_sum, x),
        first_arrived,
        tok,
        own_middle,
        vectors,
    )
    out_sum = mine + over_fsdp(other, 1)
    out_arrived = over_fsdp(own_rows(out_sum, 1 - x).astype(BF), 2)
    output = own_rows(out_sum, x) + out_arrived.astype(F32) + vectors[5:6]
    block_out = (own_rows(mid_mine, x) + RESIDUAL * output).astype(BF)

    sums_one = sums_one[:2] + over_fsdp(sums_one[:2], 1)
    sums_one = sums_one + over_fsdp(sums_one, 2)
    sums_two = sums_two[:2] + over_fsdp(sums_two[:2], 1)

    def own_slice(row):
        return lax.dynamic_slice_in_dim(row, f * width, width, 0)

    sums_q = sums_attn[0, :width]
    sums_v = jnp.concatenate([sums_attn[0, 384:512], sums_attn[0, 512 + HD :]])
    vector_sums = jnp.concatenate(
        [
            own_slice(sums_one[0]),
            own_slice(sums_one[1]),
            sums_q,
            sums_v,
            own_slice(sums_proj[0]),
            own_slice(sums_two[0]),
            own_slice(sums_two[1]),
            own_slice(sums_mlp[0]),
            sums_mlp[1],
        ]
    )
    vector_sums = lax.psum(vector_sums.reshape(-1, 128), "ctx").reshape(-1)
    slices = [vector_sums[i * width : (i + 1) * width] for i in range(8)]
    fc_bias_grad = vector_sums[8 * width :]

    def reduce_ctx(value):
        return lax.psum_scatter(value, "ctx", scatter_dimension=0, tiled=False)

    def turn(value):
        return lax.all_to_all(value, "fsdp", split_axis=0, concat_axis=0, tiled=False)

    def gather_ctx(value):
        return lax.all_gather(value, "ctx")

    mlp_sum = reduce_ctx(jnp.concatenate([out_grad, fc_grad.reshape(ways, parts * size, hidden)], 1))
    out_size = hidden // ways
    fc_turned = turn(mlp_sum[out_size:].reshape(parts, size, hidden))
    mlp_all = gather_ctx(jnp.concatenate([mlp_sum[:out_size], fc_turned.reshape(parts * size, hidden)], 0))
    out_weight_grad = mlp_all[:, :out_size].reshape(hidden, features).astype(F32)
    fc_all = mlp_all[:, out_size:].reshape(ways, parts, size, hidden)
    fc_weight_grad = fc_all.transpose(0, 2, 1, 3).reshape(width, parts * hidden).astype(F32)
    proj_all = gather_ctx(reduce_ctx(proj_grad))
    proj_weight_grad = proj_all.reshape(width, features).astype(F32)
    attn_all = gather_ctx(turn(reduce_ctx(attn_grad)))
    attn_all = attn_all.transpose(0, 2, 1, 3).reshape(width, parts, columns)
    q = attn_all[:, :, :width]
    k = jnp.concatenate([attn_all[:, :, 256:384], attn_all[:, :, 512 : 512 + HD]], 2)
    v = jnp.concatenate([attn_all[:, :, 384:512], attn_all[:, :, 512 + HD :]], 2)
    attn_weight_grad = jnp.stack([q, k, v], 1).reshape(width, 3 * features).astype(F32)
    return (
        block_out[None],
        input_grad[None],
        slices[0],
        slices[1],
        attn_weight_grad,
        slices[2],
        slices[3],
        proj_weight_grad,
        slices[4],
        slices[5],
        slices[6],
        fc_weight_grad,
        fc_bias_grad,
        out_weight_grad,
        slices[7],
    )


def solution(mesh):
    rows, row, matrix = P("fsdp", "ctx", None), P("fsdp"), P("fsdp", None)
    return jax.shard_map(
        partial(shards, mesh.shape["fsdp"], mesh.shape["ctx"]),
        mesh=mesh,
        in_specs=(
            rows, row, row, matrix, row, row, matrix, row, row, row, matrix, row, matrix, row, rows,
        ),
        out_specs=(
            rows, rows, row, row, matrix, row, row, matrix, row, row, row, matrix, row, matrix, row,
        ),
        check_vma=False,
    )
```

```python
from functools import partial

import jax
import jax.numpy as jnp
from jax import lax
from jax.experimental import pallas as pl
from jax.experimental.pallas import tpu as pltpu
from jax.sharding import PartitionSpec as P

HD = 64
LAYERS = 12
EPSILON = 1e-05
BF = jnp.bfloat16
F32 = jnp.float32
RESIDUAL = LAYERS ** (-0.5)
SCORE = HD ** (-0.5)
NEVER = -1e30
VMEM_BYTES = 50 * 1024 * 1024


def shape(dims, kind):
    return jax.ShapeDtypeStruct(dims, kind)


def call(body, name, outs, *args, scratch=(), after=()):
    vmem = pl.BlockSpec(memory_space=pltpu.VMEM)
    smem = pl.BlockSpec(memory_space=pltpu.SMEM)
    held = pl.BlockSpec(memory_space=pl.ANY)
    count, waits = len(args), len(after)

    def run(*refs):
        body(*refs[:count], *refs[count + waits :])

    return pl.pallas_call(
        run,
        name=name,
        out_shape=outs,
        in_specs=[smem] + [vmem] * (count - 1) + [held] * waits,
        out_specs=[vmem] * len(outs),
        scratch_shapes=list(scratch),
        compiler_params=pltpu.CompilerParams(vmem_limit_bytes=VMEM_BYTES),
    )(*args, *after)


def rows_at(index, size):
    return pl.ds(pl.multiple_of(index * size, size), size)


def dot(first, second):
    return jnp.dot(first, second, preferred_element_type=F32)


def dot_rows(first, second):
    return lax.dot_general(first, second, (((0,), (0,)), ((), ())), preferred_element_type=F32)


def dot_columns(first, second):
    return lax.dot_general(first, second, (((1,), (1,)), ((), ())), preferred_element_type=F32)


def normalize(values):
    center = jnp.mean(values, axis=-1, keepdims=True)
    centered = values - center
    spread = jnp.mean(centered * centered, axis=-1, keepdims=True)
    scale = lax.rsqrt(spread + EPSILON)
    return centered * scale, scale


def norm_back(grad, unit, scale, gain):
    inner = grad * gain
    mean_inner = jnp.mean(inner, axis=-1, keepdims=True)
    mean_along = jnp.mean(inner * unit, axis=-1, keepdims=True)
    return scale * (inner - mean_inner - unit * mean_along)


def join(at, pieces, whole):
    size = pieces[0].shape[0]
    for k, piece in enumerate(pieces):
        whole[rows_at(at[2] ^ k, size), :] = piece[...]


def join_body(at, *refs):
    join(at, refs[:-1], refs[-1])


def columns_body(parts, at, attn, fc, small, *refs):
    attn_pieces, fc_pieces = refs[:parts], refs[parts:]
    features = attn.shape[1] // 3
    width = features // parts
    hidden = fc.shape[1] // parts
    unit = (
        lax.broadcasted_iota(jnp.int32, (8, HD), 0) == lax.broadcasted_iota(jnp.int32, (8, HD), 1)
    ).astype(BF)
    spare = dot_rows(small[...], unit).astype(BF)
    for owner in range(parts):

        @pl.when(at[2] == owner)
        def _():
            for k in range(parts):
                first = (owner ^ k) * width
                piece = attn_pieces[k]
                piece[:, :width] = attn[:, first : first + width]
                piece[:, width:256] = spare
                key = attn[:, features + first : features + first + width]
                value = attn[:, 2 * features + first : 2 * features + first + width]
                piece[:, 256:384] = key[:, :128]
                piece[:, 384:512] = value[:, :128]
                piece[:, 512 : 512 + HD] = key[:, 128:]
                piece[:, 512 + HD :] = value[:, 128:]
                fc_pieces[k][...] = fc[:, (owner ^ k) * hidden : ((owner ^ k) + 1) * hidden]


def block_of(at, k, rows):
    return rows_at(at[2] ^ at[0] ^ k, rows)


def mixed_body(parts, count, at, bias, *refs):
    tokens, weights = refs[:parts], refs[parts : 2 * parts]
    normed, matrix, vectors, *outs, kept = refs[2 * parts :]
    rows = tokens[0].shape[0]
    join(at, weights, matrix)
    columns = matrix.shape[1]
    width = weights[0].shape[0]
    pick = lax.broadcasted_iota(jnp.int32, (8, columns), 1) == width + lax.broadcasted_iota(
        jnp.int32, (8, columns), 0
    )
    small = dot_columns(pick.astype(BF), matrix[...])
    vectors[...] = small
    for k in range(parts):
        unit, _ = normalize(tokens[k][...].astype(F32))
        normed[k * rows : (k + 1) * rows, :] = (unit * small[0:1] + small[1:2]).astype(BF)
    lane = lax.broadcasted_iota(jnp.int32, (1, columns), 1)
    spare = (lane >= width) & (lane < 256)
    kept[...] = jnp.where(spare, 0.0, dot(normed[...], matrix[...]) + bias[...]).astype(BF)
    for k in range(count):
        block = block_of(at, k, rows)
        outs[k][...] = kept[block, :256]
        outs[count + k][...] = kept[block, 256:]


def place(at, count, blocks, rows, queries, pairs, partners, q_all, kv_all):
    for k in range(count):
        row = at[0] ^ k
        q_all[rows_at(row, rows), :] = queries[k][...]
        kv_all[rows_at(row * blocks + at[1], rows), :] = pairs[k][...]
        for j, partner in enumerate(partners):
            side = row * blocks + (at[1] ^ (j + 1))
            kv_all[rows_at(side, rows), :] = partner[k * rows : (k + 1) * rows, :]


def head_views(tile_one, tile_two, scale):
    low = lax.broadcasted_iota(jnp.int32, tile_one.shape, 1) < HD
    zero = jnp.zeros_like(tile_one)
    tile_one = tile_one * scale if scale is not None else tile_one
    tile_two = tile_two * scale if scale is not None else tile_two
    return (jnp.where(low, tile_one, zero), jnp.where(low, zero, tile_one), tile_two)


def visible_keys(at, i, blocks, rows, keys):
    query = (i * blocks + at[1]) * rows + lax.broadcasted_iota(jnp.int32, (rows, keys), 0)
    return lax.broadcasted_iota(jnp.int32, (rows, keys), 1) <= query


def attend_body(count, blocks, rows, at, *refs):
    queries, pairs = refs[:count], refs[count : 2 * count]
    partners = refs[2 * count : 2 * count + blocks - 1]
    fc_pieces = refs[2 * count + blocks - 1 : 3 * count + blocks - 1]
    outs = refs[3 * count + blocks - 1 :]
    pieces, (exact, totals, q_all, kv_all, fc) = outs[:count], outs[count:]
    join(at, fc_pieces, fc)
    place(at, count, blocks, rows, queries, pairs, partners, q_all, kv_all)
    low = lax.broadcasted_iota(jnp.int32, (rows, 128), 1) < HD
    for i in range(count):
        keys = (i + 1) * blocks * rows
        mine = slice(i * rows, (i + 1) * rows)
        heads = head_views(q_all[mine, :128], q_all[mine, 128:], SCORE)
        seen = visible_keys(at, i, blocks, rows, keys)
        found = []
        for h, query in enumerate(heads):
            key_cols = slice(0, 128) if h < 2 else slice(256, 384)
            value_cols = slice(128, 256) if h < 2 else slice(256, 384)
            scores = jnp.where(seen, dot_columns(query, kv_all[:keys, key_cols]), NEVER)
            highest = jnp.max(scores, axis=-1, keepdims=True)
            weights = jnp.exp(scores - highest)
            total = jnp.sum(weights, axis=-1, keepdims=True)
            totals[mine, h : h + 1] = highest + jnp.log(total)
            weights = (weights * (1.0 / total)).astype(BF)
            found.append(dot(weights, kv_all[:keys, value_cols]))
        exact[mine, :128] = jnp.where(low, found[0], found[1])
        exact[mine, 128:] = jnp.where(low, 0.0, found[2])
    half = rows // 2
    for k in range(count):
        block = rows_at(at[0] ^ k, rows)
        pieces[k][:rows, :] = exact[block, :128].astype(BF)
        last = exact[block, 128:]
        pair = jnp.where(low[:half], pltpu.roll(last[:half], HD, 1), last[half:])
        pieces[k][rows:, :] = pair.astype(BF)


def attend_back_body(count, blocks, rows, at, *refs):
    grads, (q_all, kv_all, exact, totals) = refs[:count], refs[count : count + 4]
    outs = refs[count + 4 :]
    pieces, (own, away), (g_all, dq_all, acc) = outs[:count], outs[count : count + 2], outs[count + 2 :]
    for k in range(count):
        g_all[rows_at(at[0] ^ k, rows), :] = grads[k][...]
    acc[...] = jnp.zeros_like(acc)
    low = lax.broadcasted_iota(jnp.int32, (rows, 128), 1) < HD
    for i in range(count):
        keys = (i + 1) * blocks * rows
        mine = slice(i * rows, (i + 1) * rows)
        q_heads = head_views(q_all[mine, :128], q_all[mine, 128:], SCORE)
        g_heads = head_views(g_all[mine, :128], g_all[mine, 128:], None)
        seen = visible_keys(at, i, blocks, rows, keys)
        found = []
        for h in range(3):
            key_cols = slice(0, 128) if h < 2 else slice(256, 384)
            value_cols = slice(128, 256) if h < 2 else slice(256, 384)
            kept = exact[mine, :128] if h < 2 else exact[mine, 128:]
            delta = jnp.sum(g_heads[h].astype(F32) * kept, axis=-1, keepdims=True)
            scores = dot_columns(q_heads[h], kv_all[:keys, key_cols]) - totals[mine, h : h + 1]
            weights = jnp.exp(jnp.where(seen, scores, NEVER))
            g_weights = dot_columns(g_heads[h], kv_all[:keys, value_cols])
            g_scores = (weights * (g_weights - delta)).astype(BF)
            found.append(dot(g_scores, kv_all[:keys, key_cols]))
            acc[:keys, key_cols] += dot_rows(g_scores, q_heads[h])
            acc[:keys, value_cols] += dot_rows(weights.astype(BF), g_heads[h])
        dq_all[mine, :128] = (jnp.where(low, found[0], found[1]) * SCORE).astype(BF)
        dq_all[mine, 128:] = (jnp.where(low, found[2], 0.0) * SCORE).astype(BF)
    for k in range(count):
        row = at[0] ^ k
        pieces[k][...] = dq_all[rows_at(row, rows), :]
        into = slice(k * rows, (k + 1) * rows)
        own[into, :] = acc[rows_at(row * blocks + at[1], rows), :]
        for j in range(1, blocks):
            from_rows = slice((j - 1) * count * rows + k * rows, (j - 1) * count * rows + (k + 1) * rows)
            away[from_rows, :] = acc[rows_at(row * blocks + (at[1] ^ j), rows), :].astype(BF)


def plain_heads(values):
    zero = jnp.zeros_like(values[:, :HD])
    first = jnp.concatenate([values[:, :HD], zero], 1)
    second = jnp.concatenate([zero, values[:, HD:128]], 1)
    return (first, second, values[:, 128:])


def plain_terms(at, count, blocks, rows):
    q_pos = (jnp.arange(count)[:, None] * blocks + at[1]) * rows + jnp.arange(rows)[None]
    k_pos = jnp.arange(count * blocks * rows)
    return k_pos[None] <= q_pos.reshape(-1)[:, None]


def plain_attend(count, blocks, rows, at, queries, pairs, partners):
    width = pairs[0].shape[1]
    q_all = jnp.zeros((count, rows, queries[0].shape[1]), BF)
    kv_all = jnp.zeros((count, blocks, rows, width), BF)
    for k in range(count):
        row = at[0] ^ k
        q_all = q_all.at[row].set(queries[k])
        kv_all = kv_all.at[row, at[1]].set(pairs[k])
        for j, partner in enumerate(partners):
            kv_all = kv_all.at[row, at[1] ^ (j + 1)].set(partner[k * rows : (k + 1) * rows])
    q_all, kv_all = q_all.reshape(count * rows, -1), kv_all.reshape(-1, width)
    seen = plain_terms(at, count, blocks, rows)
    found, totals = [], []
    for h, query in enumerate(plain_heads(q_all)):
        key = kv_all[:, :128] if h < 2 else kv_all[:, 256:]
        value = kv_all[:, 128:256] if h < 2 else kv_all[:, 256:]
        scores = jnp.where(seen, dot_columns(query, key) * SCORE, NEVER)
        total = jax.nn.logsumexp(scores, axis=-1, keepdims=True)
        found.append(dot(jnp.exp(scores - total).astype(BF), value))
        totals.append(total)
    exact = jnp.concatenate([found[0][:, :HD], found[1][:, HD:], jnp.zeros_like(found[2][:, :HD]), found[2][:, HD:]], 1)
    grid = exact.astype(BF).reshape(count, rows, -1)
    half = rows // 2
    pair = jnp.concatenate([grid[:, :half, 128 + HD :], grid[:, half:, 128 + HD :]], 2)
    grid = jnp.concatenate([grid[:, :, :128], pair], 1)
    pieces = [grid[at[0] ^ k] for k in range(count)]
    totals = jnp.concatenate(totals + [jnp.zeros((count * rows, 125), F32)], 1)
    return (*pieces, exact, totals, q_all, kv_all)


def plain_attend_back(count, blocks, rows, at, grads, q_all, kv_all, exact, totals):
    g_all = jnp.zeros((count, rows, grads[0].shape[1]), BF)
    for k in range(count):
        g_all = g_all.at[at[0] ^ k].set(grads[k])
    g_all = g_all.reshape(count * rows, -1)
    seen = plain_terms(at, count, blocks, rows)
    dq, parts = [], []
    for h, (query, grad, kept) in enumerate(zip(plain_heads(q_all), plain_heads(g_all), plain_heads(exact))):
        key = kv_all[:, :128] if h < 2 else kv_all[:, 256:]
        value = kv_all[:, 128:256] if h < 2 else kv_all[:, 256:]
        delta = jnp.sum(grad.astype(F32) * kept, axis=-1, keepdims=True)
        scores = dot_columns(query, key) * SCORE - totals[:, h : h + 1]
        weights = jnp.exp(jnp.where(seen, scores, NEVER))
        g_scores = (weights * (dot_columns(grad, value) - delta)).astype(BF)
        dq.append(dot(g_scores, key) * SCORE)
        parts.append((dot_rows(g_scores, query) * SCORE, dot_rows(weights.astype(BF), grad)))
    dq = jnp.concatenate([dq[0][:, :HD], dq[1][:, HD:], dq[2][:, :HD], jnp.zeros_like(dq[2][:, :HD])], 1)
    dq = dq.astype(BF).reshape(count, rows, -1)
    acc = jnp.concatenate([parts[0][0] + parts[1][0], parts[0][1] + parts[1][1], parts[2][0] + parts[2][1]], 1)
    acc = acc.reshape(count, blocks, rows, -1)
    pieces = [dq[at[0] ^ k] for k in range(count)]
    own = jnp.concatenate([acc[at[0] ^ k, at[1]] for k in range(count)], 0)
    away = [acc[at[0] ^ k, at[1] ^ j].astype(BF) for j in range(1, blocks) for k in range(count)]
    return (*pieces, own, jnp.concatenate(away, 0))


def merge_body(count, rows, at, own, *refs):
    arrived, outs = refs[:-count], refs[-count:]
    for k in range(count):
        part = slice(k * rows, (k + 1) * rows)
        total = own[part, :]
        for ref in arrived:
            total = total + ref[part, :].astype(F32)
        outs[k][...] = total.astype(BF)


def gelu_terms(hidden):
    root = 0.7978845608028654
    square = hidden * hidden
    bend = jnp.tanh(root * hidden * (1.0 + 0.044715 * square))
    half = 0.5 * (1.0 + bend)
    slope = half + 0.5 * hidden * (1.0 - bend * bend) * root * (1.0 + 3.0 * 0.044715 * square)
    return hidden * half, slope


def g_output(extras, rows):
    return jnp.concatenate([(RESIDUAL * ref[:rows, :].astype(F32)).astype(BF) for ref in extras], axis=0)


def split_rows(values, rows, mine, other):
    mine[:rows, :] = values[:rows]
    mine[rows:, :] = values[2 * rows : 3 * rows]
    other[:rows, :] = values[rows : 2 * rows]
    other[rows:, :] = values[3 * rows :]


def middle_body(parts, rows, at, attended, vectors, fc, fc_bias, out, *refs):
    tokens, extras = refs[:parts], refs[parts : 2 * parts]
    gn_mine, gn_other, mid_mine, normed, active, g_hidden, own, att_all, proj = refs[2 * parts :]
    zero = jnp.zeros((HD, proj.shape[1]), BF)
    half = rows // 2
    low = lax.broadcasted_iota(jnp.int32, (half, 128), 1) < HD
    for k in range(parts):
        weight = extras[k][rows:, :]
        owner = at[2] ^ k
        packed = jnp.concatenate([weight[:128], zero, weight[128:]], axis=0)
        proj[rows_at(owner, 256), :] = packed
    size = rows + half
    for j in range(parts):
        for k in range(parts):
            piece = attended[j, k * size : (k + 1) * size, :]
            pair = piece[rows:].astype(F32)
            upper = jnp.where(low, 0.0, pltpu.roll(pair, HD, 1)).astype(BF)
            lower = jnp.where(low, 0.0, pair).astype(BF)
            block = block_of(at, k, rows)
            att_all[block, j * 256 : j * 256 + 128] = piece[:rows]
            att_all[block, j * 256 + 128 : (j + 1) * 256] = jnp.concatenate([upper, lower], axis=0)
    own[...] = att_all[:, pl.ds(pl.multiple_of(at[2] * 256, 256), 256)]
    branch = dot(att_all[...], proj[...]) + vectors[4:5]
    for k in range(parts):
        part = slice(k * rows, (k + 1) * rows)
        value = tokens[k][...].astype(F32) + RESIDUAL * branch[part]
        if k % 2 == 0:
            mid_mine[(k // 2) * rows : (k // 2 + 1) * rows, :] = value
        unit, _ = normalize(value)
        normed[part, :] = (unit * vectors[2:3] + vectors[3:4]).astype(BF)
    hidden = dot(normed[...], fc[...]) + fc_bias[...].astype(F32)
    value, slope = gelu_terms(hidden)
    active[...] = value.astype(BF)
    g_hidden[...] = (dot_columns(g_output(extras, rows), out[...]) * slope).astype(BF)
    split_rows(dot_columns(g_hidden[...], fc[...]), rows, gn_mine, gn_other)


def chunk_rows(at, owner, owner_rows, blocks, count, side, k):
    size = owner_rows // (blocks * count)
    return pl.ds(pl.multiple_of(owner * owner_rows + (side * count + (at[0] ^ k)) * size, 8), size)


def weights_body(parts, rows, blocks, at, normed, active, g_hidden, out, *refs):
    extras = refs[:parts]
    mine, other, *grads, sums, out_all, fc_all = refs[parts:]
    g_out = g_output(extras, rows)
    split_rows(dot(active[...], out[...]), rows, mine, other)
    out_all[...] = dot_rows(active[...], g_out)
    fc_all[...] = dot_rows(normed[...], g_hidden[...])
    sums[...] = jnp.zeros_like(sums)
    sums[0:1, :] = jnp.sum(g_out.astype(F32), axis=0, keepdims=True)
    sums[1:2, :] = jnp.sum(g_hidden[...].astype(F32), axis=0, keepdims=True)
    if blocks != 2:
        grads[0][...] = out_all[...].astype(BF)
        grads[1][...] = fc_all[...].astype(BF)
        return
    kept, away = grads
    out_rows, fc_rows = out_all.shape[0], fc_all.shape[0] // parts
    out_size, fc_size = out_rows // (2 * parts), fc_rows // (2 * parts)
    start = 0
    for k in range(parts):
        rows_kept = chunk_rows(at, 0, out_rows, 2, parts, at[1], k)
        rows_away = chunk_rows(at, 0, out_rows, 2, parts, 1 - at[1], k)
        kept[start : start + out_size, :] = out_all[rows_kept, :]
        away[start : start + out_size, :] = out_all[rows_away, :].astype(BF)
        start += out_size
        for j in range(parts):
            rows_kept = chunk_rows(at, at[2] ^ j, fc_rows, 2, parts, at[1], k)
            rows_away = chunk_rows(at, at[2] ^ j, fc_rows, 2, parts, 1 - at[1], k)
            kept[start : start + fc_size, :] = fc_all[rows_kept, :]
            away[start : start + fc_size, :] = fc_all[rows_away, :].astype(BF)
            start += fc_size


def second_norm_body(rows, at, chip_sum, arrived, mid, own_extra, x_extra, vectors, g_branch, own_middle, sums):
    add = arrived[...].astype(F32)
    grad = chip_sum[...] + jnp.concatenate([add[rows:], add[:rows]], axis=0)
    unit, scale = normalize(mid[...])
    back = norm_back(grad, unit, scale, vectors[2:3])
    sums[...] = jnp.zeros_like(sums)
    sums[0:1, :] = jnp.sum(grad * unit, axis=0, keepdims=True)
    sums[1:2, :] = jnp.sum(grad, axis=0, keepdims=True)
    g_own = back[:rows] + own_extra[:rows, :].astype(F32)
    own_middle[...] = g_own
    g_branch[:rows, :] = (RESIDUAL * g_own).astype(BF)
    g_branch[rows:, :] = (RESIDUAL * (back[rows:] + x_extra[:rows, :].astype(F32))).astype(BF)


def attended_grad_body(parts, rows, at, mine, other, proj, *refs):
    outs, (kept, g_all) = refs[:parts], refs[parts:]
    kept[:rows, :] = mine[:rows, :]
    kept[rows : 2 * rows, :] = other[:rows, :]
    kept[2 * rows : 3 * rows, :] = mine[rows:, :]
    kept[3 * rows :, :] = other[rows:, :]
    zero = jnp.zeros((HD, proj.shape[1]), BF)
    weight = jnp.concatenate([proj[:128, :], zero, proj[128:, :]], axis=0)
    g_all[...] = dot_columns(kept[...], weight).astype(BF)
    for k in range(parts):
        outs[k][...] = g_all[block_of(at, k, rows), :]


def proj_grad_body(at, attended, g_branch, proj_grad, sums):
    grad = dot_rows(attended[...], g_branch[...])
    proj_grad[...] = jnp.concatenate([grad[:128], grad[128 + HD :]], axis=0)
    sums[...] = jnp.zeros_like(sums)
    sums[0:1, :] = jnp.sum(g_branch[...].astype(F32), axis=0, keepdims=True)


def pack_wide(values, lanes):
    third = values.shape[0] // 3
    rest = values[:, lanes:]
    low = [rest[i * third : (i + 1) * third] for i in range(3)]
    low.append(jnp.zeros((third, lanes - 384), values.dtype))
    return jnp.concatenate([values[:, :lanes], jnp.concatenate(low, axis=1)], axis=0)


def first_grad_body(parts, rows, blocks, at, normed, matrix, proj_grad, *refs):
    queries, pairs = refs[:parts], refs[parts : 2 * parts]
    mine, other, *grads, sums, mixed, attn_all = refs[2 * parts :]
    for k in range(parts):
        block = block_of(at, k, rows)
        mixed[block, :256] = queries[k][...]
        mixed[block, 256:] = pairs[k][...]
    split_rows(dot_columns(mixed[...], matrix[...]), rows, mine, other)
    attn_all[...] = dot_rows(normed[...], mixed[...])
    sums[...] = jnp.zeros_like(sums)
    sums[0:1, :] = jnp.sum(mixed[...].astype(F32), axis=0, keepdims=True)
    if blocks != 2:
        grads[0][...] = attn_all[...].astype(BF)
        grads[1][...] = proj_grad[...].astype(BF)
        return
    kept, away = grads
    lanes = attn_all.shape[1]
    owner_rows = attn_all.shape[0] // parts
    size = owner_rows // (2 * parts)
    start = 0
    for k in range(parts):
        for j in range(parts):
            kept[start : start + size, :] = attn_all[chunk_rows(at, at[2] ^ j, owner_rows, 2, parts, at[1], k), :]
            part = attn_all[chunk_rows(at, at[2] ^ j, owner_rows, 2, parts, 1 - at[1], k), :]
            away[start : start + size, :] = part.astype(BF)
            start += size
        packed = size + size // 3
        part = proj_grad[chunk_rows(at, 0, owner_rows, 2, parts, at[1], k), :]
        kept[start : start + packed, :] = pack_wide(part, lanes)
        part = proj_grad[chunk_rows(at, 0, owner_rows, 2, parts, 1 - at[1], k), :]
        away[start : start + packed, :] = pack_wide(part, lanes).astype(BF)
        start += packed


def first_norm_body(rows, at, own, arrived, tokens, own_middle, vectors, input_grad, sums):
    grad = own[:rows, :] + arrived[...].astype(F32)
    unit, scale = normalize(tokens[...].astype(F32))
    back = norm_back(grad, unit, scale, vectors[0:1])
    input_grad[...] = (back + own_middle[...]).astype(BF)
    sums[...] = jnp.zeros_like(sums)
    sums[0:1, :] = jnp.sum(grad * unit, axis=0, keepdims=True)
    sums[1:2, :] = jnp.sum(grad, axis=0, keepdims=True)


def pair_sum_body(count, at, kept, arrived, *outs):
    size = kept.shape[0] // count
    for k in range(count):
        part = slice(k * size, (k + 1) * size)
        outs[k][...] = (kept[part, :] + arrived[part, :].astype(F32)).astype(outs[k].dtype)


def total_body(count, at, *refs):
    total = refs[0][...]
    for ref in refs[1:count]:
        total = total + ref[...].astype(F32)
    start = 0
    for out in refs[count:]:
        out[...] = total[start : start + out.shape[0]].astype(BF)
        start += out.shape[0]


def mlp_final_body(parts, at, *refs):
    own, away, (out_grad, fc_grad) = refs[:parts], refs[parts], refs[parts + 1 :]
    out_rows, fc_rows = out_grad.shape[0], fc_grad.shape[0]
    hidden = fc_grad.shape[1] // parts
    out_size, fc_size = out_rows // (2 * parts), fc_rows // (2 * parts)
    size = out_size + parts * fc_size
    for side in range(2):
        block = at[1] if side == 0 else 1 - at[1]
        for k in range(parts):
            piece = own[k][...] if side == 0 else away[k * size : (k + 1) * size, :]
            piece = piece.astype(F32)
            out_grad[chunk_rows(at, 0, out_rows, 2, parts, block, k), :] = piece[:out_size]
            rows = chunk_rows(at, 0, fc_rows, 2, parts, block, k)
            for j in range(parts):
                start = out_size + j * fc_size
                lanes = pl.ds(pl.multiple_of((at[2] ^ j) * hidden, 128), hidden)
                fc_grad[rows, lanes] = piece[start : start + fc_size]


def attn_final_body(parts, at, *refs):
    own, away, (attn_grad, proj_grad, kept) = refs[:parts], refs[parts], refs[parts + 1 :]
    rows_all, features = proj_grad.shape
    width = features // parts
    lanes = kept.shape[2]
    size = rows_all // (2 * parts)
    third = size // 3
    total = parts * size + size + third
    for side in range(2):
        block = at[1] if side == 0 else 1 - at[1]
        for k in range(parts):
            piece = own[k][...] if side == 0 else away[k * total : (k + 1) * total, :]
            piece = piece.astype(F32)
            rows = chunk_rows(at, 0, rows_all, 2, parts, block, k)
            for j in range(parts):
                kept[at[2] ^ j, rows, :] = piece[j * size : (j + 1) * size]
            start = parts * size
            proj_grad[rows, :lanes] = piece[start : start + size]
            low = piece[start + size :]
            proj_grad[rows, lanes:] = jnp.concatenate([low[:, i * 128 : (i + 1) * 128] for i in range(3)], axis=0)
    for g in range(parts):
        first = g * width
        attn_grad[:, first : first + width] = kept[g, :, :width]
        first += features
        attn_grad[:, first : first + width] = jnp.concatenate([kept[g, :, 256:384], kept[g, :, 512 : 512 + HD]], axis=1)
        first += features
        attn_grad[:, first : first + width] = jnp.concatenate([kept[g, :, 384:512], kept[g, :, 512 + HD :]], axis=1)


def shards(
    parts,
    ways,
    tokens,
    first_gain,
    first_bias,
    attn_weight,
    query_bias,
    value_bias,
    proj_weight,
    proj_bias,
    second_gain,
    second_bias,
    fc_weight,
    fc_bias,
    out_weight,
    out_bias,
    cotangent,
):
    rows, features = tokens.shape[1], tokens.shape[2]
    width = features // parts
    count = parts
    blocks = ways // count
    hidden = fc_weight.shape[1] // parts
    all_rows, half_rows = parts * rows, parts * rows // 2
    f = lax.axis_index("fsdp").astype(jnp.int32)
    c = lax.axis_index("ctx").astype(jnp.int32)
    a, b = c // blocks, c % blocks
    at = jnp.stack([a, b, f])

    def over_fsdp(value, k):
        return lax.ppermute(value, "fsdp", [(i, i ^ k) for i in range(parts)])

    def over_ctx(value, k):
        return lax.ppermute(value, "ctx", [(i, i ^ k) for i in range(ways)])

    def spread(value):
        across = over_fsdp(value, 2)
        return [value, over_fsdp(value, 1), across, over_fsdp(across, 1)]

    def turn_fsdp(pieces):
        return [pieces[0]] + [over_fsdp(pieces[k], k) for k in range(1, parts)]

    def turn_ctx(pieces):
        return [pieces[0]] + [over_ctx(pieces[k], k * blocks) for k in range(1, count)]

    tok = tokens[0]
    tok_all = spread(tok)
    small = jnp.stack([first_gain, first_bias, second_gain, second_bias, proj_bias, out_bias, out_bias, out_bias])
    columns = 256 + 2 * width
    pieces = call(
        partial(columns_body, parts),
        "columns",
        [shape((width, columns), BF)] * parts + [shape((width, hidden), BF)] * parts,
        at,
        attn_weight,
        fc_weight,
        small,
    )
    attn_pieces = turn_fsdp(pieces[:parts])
    fc_pieces = turn_fsdp(pieces[parts:])
    extra = spread(jnp.concatenate([cotangent[0], proj_weight], 0))

    none = jnp.zeros((128,), F32)
    vb = value_bias.astype(F32)
    bias = jnp.concatenate([query_bias.astype(F32), none[:HD], none, vb[:128], none[:HD], vb[128:]])[None]
    mixed = call(
        partial(mixed_body, parts, count),
        "mixed",
        [shape((all_rows, features), BF), shape((features, columns), BF), shape((8, features), F32)]
        + [shape((rows, 256), BF)] * count
        + [shape((rows, 384), BF)] * count,
        at,
        bias,
        *tok_all,
        *attn_pieces,
        scratch=[pltpu.VMEM((all_rows, columns), BF)],
    )
    normed, attn_matrix, vectors = mixed[:3]

    pairs = turn_ctx(mixed[3 + count :])
    queries = turn_ctx(mixed[3 : 3 + count])
    joined = jnp.concatenate(pairs, 0)
    partners = [over_ctx(joined, j) for j in range(1, blocks)]
    small_blocks = blocks * count * rows <= 1024
    if small_blocks:
        kept = call(
            partial(attend_body, count, blocks, rows),
            "attend",
            [shape((rows + rows // 2, 128), BF)] * count
            + [
                shape((count * rows, 256), F32),
                shape((count * rows, 128), F32),
                shape((count * rows, 256), BF),
                shape((count * blocks * rows, 384), BF),
                shape((features, hidden), BF),
            ],
            at,
            *queries,
            *pairs,
            *partners,
            *fc_pieces,
        )
        kept, fc_matrix = kept[:-1], kept[-1]
    else:
        kept = plain_attend(count, blocks, rows, at, queries, pairs, partners)
        fc_matrix = call(join_body, "join", [shape((features, hidden), BF)], at, *fc_pieces)[0]
    att_pieces, state = turn_ctx(kept[:count]), kept[count:]
    attended_all = lax.all_gather(jnp.concatenate(att_pieces, 0), "fsdp")

    gn_mine, gn_other, mid_mine, normed_two, active, g_hidden, attended = call(
        partial(middle_body, parts, rows),
        "middle",
        [shape((half_rows, features), F32)] * 3
        + [shape((all_rows, features), BF), shape((all_rows, hidden), BF), shape((all_rows, hidden), BF)]
        + [shape((all_rows, 256), BF)],
        at,
        attended_all,
        vectors,
        fc_matrix,
        fc_bias[None],
        out_weight,
        *tok_all,
        *extra,
        scratch=[pltpu.VMEM((all_rows, parts * 256), BF), pltpu.VMEM((parts * 256, features), BF)],
    )
    chip_sum = gn_mine + over_fsdp(gn_other, 1)
    chip_low = chip_sum.astype(BF)
    arrived = over_fsdp(chip_low, 2)
    if blocks == 2:
        chunk = hidden // (2 * count) + features // (2 * count)
        mlp_grads = [shape((count * chunk, features), F32), shape((count * chunk, features), BF)]
    else:
        mlp_grads = [shape((hidden, features), BF), shape((features, hidden), BF)]
    mine, other, *mlp_grads, sums_mlp = call(
        partial(weights_body, parts, rows, blocks),
        "mlp_weights",
        [shape((half_rows, features), F32)] * 2 + mlp_grads + [shape((8, features), F32)],
        at,
        normed_two,
        active,
        g_hidden,
        out_weight,
        *extra,
        scratch=[pltpu.VMEM((hidden, features), F32), pltpu.VMEM((features, hidden), F32)],
        after=[chip_low],
    )
    g_branch, own_middle, sums_two = call(
        partial(second_norm_body, rows),
        "second_norm",
        [shape((half_rows, features), BF), shape((rows, features), F32), shape((8, features), F32)],
        at,
        chip_sum,
        arrived,
        mid_mine,
        extra[0],
        extra[2],
        vectors,
    )
    grads = call(
        partial(attended_grad_body, parts, rows),
        "attended_grad",
        [shape((rows, 256), BF)] * parts + [shape((all_rows, features), BF)],
        at,
        g_branch,
        over_fsdp(g_branch, 1),
        proj_weight,
        scratch=[pltpu.VMEM((all_rows, 256), BF)],
    )
    g_pieces, g_branch_all = turn_ctx(grads[:parts]), grads[parts]
    proj_grad, sums_proj = call(
        proj_grad_body,
        "proj_weight_grad",
        [shape((width, features), F32), shape((8, features), F32)],
        at,
        attended,
        g_branch_all,
    )
    if small_blocks:
        back = call(
            partial(attend_back_body, count, blocks, rows),
            "attend_back",
            [shape((rows, 256), BF)] * count
            + [shape((count * rows, 384), F32), shape(((blocks - 1) * count * rows, 384), BF)],
            at,
            *g_pieces,
            state[2],
            state[3],
            state[0],
            state[1],
            scratch=[
                pltpu.VMEM((count * rows, 256), BF),
                pltpu.VMEM((count * rows, 256), BF),
                pltpu.VMEM((count * blocks * rows, 384), F32),
            ],
        )
    else:
        back = plain_attend_back(count, blocks, rows, at, g_pieces, state[2], state[3], state[0], state[1])
    dq, own, away = back[:count], back[count], back[count + 1]
    stack = count * rows
    from_partners = [over_ctx(away[(j - 1) * stack : j * stack], j) for j in range(1, blocks)]
    dkv = call(partial(merge_body, count, rows), "merge", [shape((rows, 384), BF)] * count, at, own, *from_partners)
    dq, dkv = turn_ctx(dq), turn_ctx(dkv)
    if blocks == 2:
        size = width // (2 * count)
        chunk = parts * size + size + size // 3
        attn_grads = [shape((count * chunk, columns), F32), shape((count * chunk, columns), BF)]
    else:
        attn_grads = [shape((features, columns), BF), shape((width, features), BF)]
    g1_mine, g1_other, *attn_grads, sums_attn = call(
        partial(first_grad_body, parts, rows, blocks),
        "first_grad",
        [shape((half_rows, features), F32)] * 2 + attn_grads + [shape((8, columns), F32)],
        at,
        normed,
        attn_matrix,
        proj_grad,
        *dq,
        *dkv,
        scratch=[pltpu.VMEM((all_rows, columns), BF), pltpu.VMEM((features, columns), F32)],
    )
    first_sum = g1_mine + over_fsdp(g1_other, 1)
    input_grad, sums_one = call(
        partial(first_norm_body, rows),
        "first_norm",
        [shape((rows, features), BF), shape((8, features), F32)],
        at,
        first_sum,
        over_fsdp(first_sum[rows:].astype(BF), 2),
        tok,
        own_middle,
        vectors,
    )
    out_sum = mine + over_fsdp(other, 1)
    output = out_sum[:rows] + over_fsdp(out_sum[rows:].astype(BF), 2).astype(F32) + vectors[5:6]
    block_out = (mid_mine[:rows] + RESIDUAL * output).astype(BF)

    sums_one = sums_one[:2] + over_fsdp(sums_one[:2], 1)
    sums_one = sums_one + over_fsdp(sums_one, 2)
    sums_two = sums_two[:2] + over_fsdp(sums_two[:2], 1)

    def own_slice(row):
        return lax.dynamic_slice_in_dim(row, f * width, width, 0)

    vector_sums = jnp.concatenate(
        [
            own_slice(sums_one[0]),
            own_slice(sums_one[1]),
            sums_attn[0, :width],
            jnp.concatenate([sums_attn[0, 384:512], sums_attn[0, 512 + HD :]]),
            own_slice(sums_proj[0]),
            own_slice(sums_two[0]),
            own_slice(sums_two[1]),
            own_slice(sums_mlp[0]),
            sums_mlp[1],
        ]
    ).reshape(-1, 128)
    if blocks == 2:
        vector_sums = vector_sums + over_ctx(vector_sums, 1)
        vector_sums = sum((over_ctx(vector_sums, 2 * k) for k in range(1, count)), vector_sums)
    else:
        vector_sums = lax.psum(vector_sums, "ctx")
    vector_sums = vector_sums.reshape(-1)
    slices = [vector_sums[i * width : (i + 1) * width] for i in range(8)]
    fc_bias_grad = vector_sums[8 * width :]

    if blocks == 2:

        def summed(name, kept, away, cuts):
            size, lanes = kept.shape[0] // count, kept.shape[1]
            sent = call(
                partial(pair_sum_body, count),
                name + "_pair",
                [shape((size, lanes), F32)] + [shape((size, lanes), BF)] * (count - 1),
                at,
                kept,
                over_ctx(away, 1),
            )
            return call(
                partial(total_body, count),
                name + "_total",
                [shape((cut, lanes), BF) for cut in cuts],
                at,
                *turn_ctx(sent),
            )

        def gathered(piece):
            pieces = [piece] + [over_ctx(piece, 2 * k) for k in range(1, count)]
            return (*pieces, over_ctx(jnp.concatenate(pieces, 0), 1))

        out_size, fc_size = hidden // (2 * count), width // (2 * count)
        out_part, *fc_parts = summed("mlp", *mlp_grads, [out_size] + [fc_size] * parts)
        out_weight_grad, fc_weight_grad = call(
            partial(mlp_final_body, parts),
            "mlp_final",
            [shape((hidden, features), F32), shape((width, parts * hidden), F32)],
            at,
            *gathered(jnp.concatenate([out_part, *turn_fsdp(fc_parts)], 0)),
        )
        *attn_parts, proj_part = summed("attn", *attn_grads, [size] * parts + [size + size // 3])
        attn_weight_grad, proj_weight_grad = call(
            partial(attn_final_body, parts),
            "attn_final",
            [shape((width, 3 * features), F32), shape((width, features), F32)],
            at,
            *gathered(jnp.concatenate([*turn_fsdp(attn_parts), proj_part], 0)),
            scratch=[pltpu.VMEM((parts, width, columns), F32)],
        )
    else:

        def over_all(value):
            part = lax.psum_scatter(value, "ctx", scatter_dimension=1, tiled=True)
            return lax.all_gather(part, "ctx", axis=1, tiled=True)

        out_weight_grad = over_all(mlp_grads[0]).astype(F32)
        fc_grad = over_all(mlp_grads[1]).reshape(parts, width, hidden)
        fc_grad = lax.all_to_all(fc_grad, "fsdp", split_axis=0, concat_axis=0)
        fc_weight_grad = fc_grad.transpose(1, 0, 2).reshape(width, parts * hidden).astype(F32)
        proj_weight_grad = over_all(attn_grads[1]).astype(F32)
        attn_all = over_all(attn_grads[0]).reshape(parts, width, columns)
        attn_all = lax.all_to_all(attn_all, "fsdp", split_axis=0, concat_axis=0).transpose(1, 0, 2)
        q = attn_all[:, :, :width]
        k = jnp.concatenate([attn_all[:, :, 256:384], attn_all[:, :, 512 : 512 + HD]], 2)
        v = jnp.concatenate([attn_all[:, :, 384:512], attn_all[:, :, 512 + HD :]], 2)
        attn_weight_grad = jnp.stack([q, k, v], 1).reshape(width, 3 * features).astype(F32)
    return (
        block_out[None],
        input_grad[None],
        slices[0],
        slices[1],
        attn_weight_grad,
        slices[2],
        slices[3],
        proj_weight_grad,
        slices[4],
        slices[5],
        slices[6],
        fc_weight_grad,
        fc_bias_grad,
        out_weight_grad,
        slices[7],
    )


def solution(mesh):
    rows, row, matrix = P("fsdp", "ctx", None), P("fsdp"), P("fsdp", None)
    return jax.shard_map(
        partial(shards, mesh.shape["fsdp"], mesh.shape["ctx"]),
        mesh=mesh,
        in_specs=(
            rows, row, row, matrix, row, row, matrix, row, row, row, matrix, row, matrix, row, rows,
        ),
        out_specs=(
            rows, rows, row, row, matrix, row, row, matrix, row, row, row, matrix, row, matrix, row,
        ),
        check_vma=False,
    )
```

```python
from functools import partial

import jax
import jax.numpy as jnp
from jax import lax
from jax.experimental import pallas as pl
from jax.experimental.pallas import tpu as pltpu
from jax.sharding import PartitionSpec as P

HD = 64
LAYERS = 12
EPSILON = 1e-05
BF = jnp.bfloat16
F32 = jnp.float32
RESIDUAL = LAYERS ** (-0.5)
SCORE = HD ** (-0.5)
NEVER = -1e30
VMEM_BYTES = 50 * 1024 * 1024


def shape(dims, kind):
    return jax.ShapeDtypeStruct(dims, kind)


class Direct:
    def __init__(self, array):
        self.array = array


def call(body, name, outs, *args, scratch=(), after=()):
    vmem = pl.BlockSpec(memory_space=pltpu.VMEM)
    smem = pl.BlockSpec(memory_space=pltpu.SMEM)
    held = pl.BlockSpec(memory_space=pl.ANY)
    count, waits = len(args), len(after)
    specs = [pl.BlockSpec() if isinstance(arg, Direct) else vmem for arg in args[1:]]
    args = [arg.array if isinstance(arg, Direct) else arg for arg in args]

    def run(*refs):
        body(*refs[:count], *refs[count + waits :])

    return pl.pallas_call(
        run,
        name=name,
        out_shape=outs,
        in_specs=[smem] + specs + [held] * waits,
        out_specs=[vmem] * len(outs),
        scratch_shapes=list(scratch),
        compiler_params=pltpu.CompilerParams(vmem_limit_bytes=VMEM_BYTES),
    )(*args, *after)


def rows_at(index, size):
    return pl.ds(pl.multiple_of(index * size, size), size)


def dot(first, second):
    return jnp.dot(first, second, preferred_element_type=F32)


def dot_rows(first, second):
    return lax.dot_general(first, second, (((0,), (0,)), ((), ())), preferred_element_type=F32)


def dot_columns(first, second):
    return lax.dot_general(first, second, (((1,), (1,)), ((), ())), preferred_element_type=F32)


def normalize(values):
    center = jnp.mean(values, axis=-1, keepdims=True)
    centered = values - center
    spread = jnp.mean(centered * centered, axis=-1, keepdims=True)
    scale = lax.rsqrt(spread + EPSILON)
    return centered * scale, scale


def norm_back(grad, unit, scale, gain):
    inner = grad * gain
    mean_inner = jnp.mean(inner, axis=-1, keepdims=True)
    mean_along = jnp.mean(inner * unit, axis=-1, keepdims=True)
    return scale * (inner - mean_inner - unit * mean_along)


def join(at, pieces, whole):
    size = pieces[0].shape[0]
    for k, piece in enumerate(pieces):
        whole[rows_at(at[2] ^ k, size), :] = piece[...]


def as_row(ref):
    return ref[...].astype(F32).reshape(1, ref.shape[0])


def attn_columns_body(parts, at, attn, *refs):
    vectors, pieces = refs[:6], refs[6:]
    features = attn.shape[1] // 3
    width = features // parts
    unit = (
        lax.broadcasted_iota(jnp.int32, (8, HD), 0) == lax.broadcasted_iota(jnp.int32, (8, HD), 1)
    ).astype(BF)
    small = jnp.concatenate([as_row(ref) for ref in vectors] + [jnp.zeros((2, width), F32)], axis=0)
    spare = dot_rows(small.astype(BF), unit).astype(BF)
    for owner in range(parts):

        @pl.when(at[2] == owner)
        def _():
            for k in range(parts):
                first = (owner ^ k) * width
                piece = pieces[k]
                piece[:, :width] = attn[:, first : first + width]
                piece[:, width:256] = spare
                key = attn[:, features + first : features + first + width]
                value = attn[:, 2 * features + first : 2 * features + first + width]
                piece[:, 256:384] = key[:, :128]
                piece[:, 384:512] = value[:, :128]
                piece[:, 512 : 512 + HD] = key[:, 128:]
                piece[:, 512 + HD :] = value[:, 128:]


def fc_columns_body(at, fc, *pieces):
    for k, piece in enumerate(pieces):
        hidden = piece.shape[1]
        piece[...] = fc[:, pl.ds(pl.multiple_of((at[2] ^ k) * hidden, 128), hidden)]


def stack_body(count, at, *refs):
    pairs, fc_pieces, (joined, fc) = refs[:count], refs[count:-2], refs[-2:]
    size = pairs[0].shape[0]
    for k, pair in enumerate(pairs):
        joined[k * size : (k + 1) * size, :] = pair[...]
    join(at, fc_pieces, fc)


def block_of(at, k, rows):
    return rows_at(at[2] ^ at[0] ^ k, rows)


def mixed_body(parts, count, at, query_bias, value_bias, *refs):
    tokens, weights = refs[:parts], refs[parts : 2 * parts]
    normed, matrix, vectors, *outs, kept = refs[2 * parts :]
    rows = tokens[0].shape[0]
    join(at, weights, matrix)
    columns = matrix.shape[1]
    width = weights[0].shape[0]
    pick = lax.broadcasted_iota(jnp.int32, (8, columns), 1) == width + lax.broadcasted_iota(
        jnp.int32, (8, columns), 0
    )
    small = dot_columns(pick.astype(BF), matrix[...])
    vectors[...] = small
    for k in range(parts):
        unit, _ = normalize(tokens[k][...].astype(F32))
        normed[k * rows : (k + 1) * rows, :] = (unit * small[0:1] + small[1:2]).astype(BF)
    lane = lax.broadcasted_iota(jnp.int32, (1, columns), 1)
    spare = (lane >= width) & (lane < 256)
    query, value = as_row(query_bias), as_row(value_bias)
    none = jnp.zeros((1, 128), F32)
    bias = [query, none[:, :HD], none, value[:, :128], none[:, :HD], value[:, 128:]]
    bias = jnp.concatenate(bias, axis=1)
    kept[...] = jnp.where(spare, 0.0, dot(normed[...], matrix[...]) + bias).astype(BF)
    for k in range(count):
        block = block_of(at, k, rows)
        outs[k][...] = kept[block, :256]
        outs[count + k][...] = kept[block, 256:]


def place(at, count, blocks, rows, queries, pairs, partners, q_all, kv_all):
    for k in range(count):
        row = at[0] ^ k
        q_all[rows_at(row, rows), :] = queries[k][...]
        kv_all[rows_at(row * blocks + at[1], rows), :] = pairs[k][...]
        for j, partner in enumerate(partners):
            side = row * blocks + (at[1] ^ (j + 1))
            kv_all[rows_at(side, rows), :] = partner[k * rows : (k + 1) * rows, :]


def head_views(tile_one, tile_two, scale):
    low = lax.broadcasted_iota(jnp.int32, tile_one.shape, 1) < HD
    zero = jnp.zeros_like(tile_one)
    tile_one = tile_one * scale if scale is not None else tile_one
    tile_two = tile_two * scale if scale is not None else tile_two
    return (jnp.where(low, tile_one, zero), jnp.where(low, zero, tile_one), tile_two)


def visible_keys(at, i, blocks, rows, keys):
    query = (i * blocks + at[1]) * rows + lax.broadcasted_iota(jnp.int32, (rows, keys), 0)
    return lax.broadcasted_iota(jnp.int32, (rows, keys), 1) <= query


def attend_body(count, blocks, rows, at, *refs):
    queries, pairs = refs[:count], refs[count : 2 * count]
    partners = refs[2 * count : 2 * count + blocks - 1]
    outs = refs[2 * count + blocks - 1 :]
    pieces, (exact, totals, q_all, kv_all) = outs[:count], outs[count:]
    place(at, count, blocks, rows, queries, pairs, partners, q_all, kv_all)
    low = lax.broadcasted_iota(jnp.int32, (rows, 128), 1) < HD
    for i in range(count):
        keys = (i + 1) * blocks * rows
        mine = slice(i * rows, (i + 1) * rows)
        heads = head_views(q_all[mine, :128], q_all[mine, 128:], SCORE)
        seen = visible_keys(at, i, blocks, rows, keys)
        found = []
        for h, query in enumerate(heads):
            key_cols = slice(0, 128) if h < 2 else slice(256, 384)
            value_cols = slice(128, 256) if h < 2 else slice(256, 384)
            scores = jnp.where(seen, dot_columns(query, kv_all[:keys, key_cols]), NEVER)
            highest = jnp.max(scores, axis=-1, keepdims=True)
            weights = jnp.exp(scores - highest)
            total = jnp.sum(weights, axis=-1, keepdims=True)
            totals[mine, h : h + 1] = highest + jnp.log(total)
            weights = (weights * (1.0 / total)).astype(BF)
            found.append(dot(weights, kv_all[:keys, value_cols]))
        exact[mine, :128] = jnp.where(low, found[0], found[1])
        exact[mine, 128:] = jnp.where(low, 0.0, found[2])
    half = rows // 2
    for k in range(count):
        block = rows_at(at[0] ^ k, rows)
        pieces[k][:rows, :] = exact[block, :128].astype(BF)
        last = exact[block, 128:]
        pair = jnp.where(low[:half], pltpu.roll(last[:half], HD, 1), last[half:])
        pieces[k][rows:, :] = pair.astype(BF)


def attend_back_body(count, blocks, rows, at, *refs):
    grads, (q_all, kv_all, exact, totals) = refs[:count], refs[count : count + 4]
    outs = refs[count + 4 :]
    pieces, (own, away), (g_all, dq_all, acc) = outs[:count], outs[count : count + 2], outs[count + 2 :]
    for k in range(count):
        g_all[rows_at(at[0] ^ k, rows), :] = grads[k][...]
    acc[...] = jnp.zeros_like(acc)
    low = lax.broadcasted_iota(jnp.int32, (rows, 128), 1) < HD
    for i in range(count):
        keys = (i + 1) * blocks * rows
        mine = slice(i * rows, (i + 1) * rows)
        q_heads = head_views(q_all[mine, :128], q_all[mine, 128:], SCORE)
        g_heads = head_views(g_all[mine, :128], g_all[mine, 128:], None)
        seen = visible_keys(at, i, blocks, rows, keys)
        found = []
        for h in range(3):
            key_cols = slice(0, 128) if h < 2 else slice(256, 384)
            value_cols = slice(128, 256) if h < 2 else slice(256, 384)
            kept = exact[mine, :128] if h < 2 else exact[mine, 128:]
            delta = jnp.sum(g_heads[h].astype(F32) * kept, axis=-1, keepdims=True)
            scores = dot_columns(q_heads[h], kv_all[:keys, key_cols]) - totals[mine, h : h + 1]
            weights = jnp.exp(jnp.where(seen, scores, NEVER))
            g_weights = dot_columns(g_heads[h], kv_all[:keys, value_cols])
            g_scores = (weights * (g_weights - delta)).astype(BF)
            found.append(dot(g_scores, kv_all[:keys, key_cols]))
            acc[:keys, key_cols] += dot_rows(g_scores, q_heads[h])
            acc[:keys, value_cols] += dot_rows(weights.astype(BF), g_heads[h])
        dq_all[mine, :128] = (jnp.where(low, found[0], found[1]) * SCORE).astype(BF)
        dq_all[mine, 128:] = (jnp.where(low, found[2], 0.0) * SCORE).astype(BF)
    for k in range(count):
        row = at[0] ^ k
        pieces[k][...] = dq_all[rows_at(row, rows), :]
        into = slice(k * rows, (k + 1) * rows)
        own[into, :] = acc[rows_at(row * blocks + at[1], rows), :]
        for j in range(1, blocks):
            from_rows = slice((j - 1) * count * rows + k * rows, (j - 1) * count * rows + (k + 1) * rows)
            away[from_rows, :] = acc[rows_at(row * blocks + (at[1] ^ j), rows), :].astype(BF)


def plain_heads(values):
    zero = jnp.zeros_like(values[:, :HD])
    first = jnp.concatenate([values[:, :HD], zero], 1)
    second = jnp.concatenate([zero, values[:, HD:128]], 1)
    return (first, second, values[:, 128:])


def plain_terms(at, count, blocks, rows):
    q_pos = (jnp.arange(count)[:, None] * blocks + at[1]) * rows + jnp.arange(rows)[None]
    k_pos = jnp.arange(count * blocks * rows)
    return k_pos[None] <= q_pos.reshape(-1)[:, None]


def plain_attend(count, blocks, rows, at, queries, pairs, partners):
    width = pairs[0].shape[1]
    q_all = jnp.zeros((count, rows, queries[0].shape[1]), BF)
    kv_all = jnp.zeros((count, blocks, rows, width), BF)
    for k in range(count):
        row = at[0] ^ k
        q_all = q_all.at[row].set(queries[k])
        kv_all = kv_all.at[row, at[1]].set(pairs[k])
        for j, partner in enumerate(partners):
            kv_all = kv_all.at[row, at[1] ^ (j + 1)].set(partner[k * rows : (k + 1) * rows])
    q_all, kv_all = q_all.reshape(count * rows, -1), kv_all.reshape(-1, width)
    seen = plain_terms(at, count, blocks, rows)
    found, totals = [], []
    for h, query in enumerate(plain_heads(q_all)):
        key = kv_all[:, :128] if h < 2 else kv_all[:, 256:]
        value = kv_all[:, 128:256] if h < 2 else kv_all[:, 256:]
        scores = jnp.where(seen, dot_columns(query, key) * SCORE, NEVER)
        total = jax.nn.logsumexp(scores, axis=-1, keepdims=True)
        found.append(dot(jnp.exp(scores - total).astype(BF), value))
        totals.append(total)
    exact = jnp.concatenate([found[0][:, :HD], found[1][:, HD:], jnp.zeros_like(found[2][:, :HD]), found[2][:, HD:]], 1)
    grid = exact.astype(BF).reshape(count, rows, -1)
    half = rows // 2
    pair = jnp.concatenate([grid[:, :half, 128 + HD :], grid[:, half:, 128 + HD :]], 2)
    grid = jnp.concatenate([grid[:, :, :128], pair], 1)
    pieces = [grid[at[0] ^ k] for k in range(count)]
    totals = jnp.concatenate(totals + [jnp.zeros((count * rows, 125), F32)], 1)
    return (*pieces, exact, totals, q_all, kv_all)


def plain_attend_back(count, blocks, rows, at, grads, q_all, kv_all, exact, totals):
    g_all = jnp.zeros((count, rows, grads[0].shape[1]), BF)
    for k in range(count):
        g_all = g_all.at[at[0] ^ k].set(grads[k])
    g_all = g_all.reshape(count * rows, -1)
    seen = plain_terms(at, count, blocks, rows)
    dq, parts = [], []
    for h, (query, grad, kept) in enumerate(zip(plain_heads(q_all), plain_heads(g_all), plain_heads(exact))):
        key = kv_all[:, :128] if h < 2 else kv_all[:, 256:]
        value = kv_all[:, 128:256] if h < 2 else kv_all[:, 256:]
        delta = jnp.sum(grad.astype(F32) * kept, axis=-1, keepdims=True)
        scores = dot_columns(query, key) * SCORE - totals[:, h : h + 1]
        weights = jnp.exp(jnp.where(seen, scores, NEVER))
        g_scores = (weights * (dot_columns(grad, value) - delta)).astype(BF)
        dq.append(dot(g_scores, key) * SCORE)
        parts.append((dot_rows(g_scores, query) * SCORE, dot_rows(weights.astype(BF), grad)))
    dq = jnp.concatenate([dq[0][:, :HD], dq[1][:, HD:], dq[2][:, :HD], jnp.zeros_like(dq[2][:, :HD])], 1)
    dq = dq.astype(BF).reshape(count, rows, -1)
    acc = jnp.concatenate([parts[0][0] + parts[1][0], parts[0][1] + parts[1][1], parts[2][0] + parts[2][1]], 1)
    acc = acc.reshape(count, blocks, rows, -1)
    pieces = [dq[at[0] ^ k] for k in range(count)]
    own = jnp.concatenate([acc[at[0] ^ k, at[1]] for k in range(count)], 0)
    away = [acc[at[0] ^ k, at[1] ^ j].astype(BF) for j in range(1, blocks) for k in range(count)]
    return (*pieces, own, jnp.concatenate(away, 0))


def merge_body(count, rows, at, own, *refs):
    arrived, outs = refs[:-count], refs[-count:]
    for k in range(count):
        part = slice(k * rows, (k + 1) * rows)
        total = own[part, :]
        for ref in arrived:
            total = total + ref[part, :].astype(F32)
        outs[k][...] = total.astype(BF)


def gelu_terms(hidden):
    root = 0.7978845608028654
    square = hidden * hidden
    bend = jnp.tanh(root * hidden * (1.0 + 0.044715 * square))
    half = 0.5 * (1.0 + bend)
    slope = half + 0.5 * hidden * (1.0 - bend * bend) * root * (1.0 + 3.0 * 0.044715 * square)
    return hidden * half, slope


def g_output(extras, rows):
    return jnp.concatenate([(RESIDUAL * ref[:rows, :].astype(F32)).astype(BF) for ref in extras], axis=0)


def split_rows(values, rows, mine, other):
    mine[:rows, :] = values[:rows]
    mine[rows:, :] = values[2 * rows : 3 * rows]
    other[:rows, :] = values[rows : 2 * rows]
    other[rows:, :] = values[3 * rows :]


def middle_body(parts, rows, at, attended, vectors, fc, fc_bias, out, *refs):
    tokens, extras = refs[:parts], refs[parts : 2 * parts]
    gn_mine, gn_other, mid_mine, normed, active, g_hidden, own, att_all, proj = refs[2 * parts :]
    zero = jnp.zeros((HD, proj.shape[1]), BF)
    half = rows // 2
    low = lax.broadcasted_iota(jnp.int32, (half, 128), 1) < HD
    for k in range(parts):
        weight = extras[k][rows:, :]
        owner = at[2] ^ k
        packed = jnp.concatenate([weight[:128], zero, weight[128:]], axis=0)
        proj[rows_at(owner, 256), :] = packed
    size = rows + half
    for j in range(parts):
        for k in range(parts):
            piece = attended[j, k * size : (k + 1) * size, :]
            pair = piece[rows:].astype(F32)
            upper = jnp.where(low, 0.0, pltpu.roll(pair, HD, 1)).astype(BF)
            lower = jnp.where(low, 0.0, pair).astype(BF)
            block = block_of(at, k, rows)
            att_all[block, j * 256 : j * 256 + 128] = piece[:rows]
            att_all[block, j * 256 + 128 : (j + 1) * 256] = jnp.concatenate([upper, lower], axis=0)
    own[...] = att_all[:, pl.ds(pl.multiple_of(at[2] * 256, 256), 256)]
    branch = dot(att_all[...], proj[...]) + vectors[4:5]
    for k in range(parts):
        part = slice(k * rows, (k + 1) * rows)
        value = tokens[k][...].astype(F32) + RESIDUAL * branch[part]
        if k % 2 == 0:
            mid_mine[(k // 2) * rows : (k // 2 + 1) * rows, :] = value
        unit, _ = normalize(value)
        normed[part, :] = (unit * vectors[2:3] + vectors[3:4]).astype(BF)
    hidden = dot(normed[...], fc[...]) + as_row(fc_bias)
    value, slope = gelu_terms(hidden)
    active[...] = value.astype(BF)
    g_hidden[...] = (dot_columns(g_output(extras, rows), out[...]) * slope).astype(BF)
    split_rows(dot_columns(g_hidden[...], fc[...]), rows, gn_mine, gn_other)


def fill_half(half, count, bit, kept, away, chunk):
    size = kept.shape[0] // half
    for i in range(half):
        into = slice(i * size, (i + 1) * size)
        kept[into, :] = chunk(bit * half + i)
        away[into, :] = chunk((1 - bit) * half + i).astype(BF)


def out_weights_body(rows, step, at, active, *refs):
    extras = refs[:-4]
    kept, away, sums, grad = refs[-4:]
    g_out = g_output(extras, rows)
    grad[...] = dot_rows(active[...], g_out)
    sums[...] = jnp.zeros_like(sums)
    sums[0:1, :] = jnp.sum(g_out[:rows].astype(F32), axis=0, keepdims=True)
    half = kept.shape[0]
    bit = (at[3] // step) % 2
    kept[...] = grad[rows_at(bit, half), :]
    away[...] = grad[rows_at(1 - bit, half), :].astype(BF)


def fc_weights_body(parts, rows, half, step, at, normed, active, g_hidden, out, mine, other, kept, away, sums, grad):
    grad[...] = dot_rows(normed[...], g_hidden[...])
    size = grad.shape[0] // (parts * 2 * half)

    def chunk(i):
        blocks = [((at[2] ^ j) * 2 * half + i) * size for j in range(parts)]
        return jnp.concatenate([grad[pl.ds(pl.multiple_of(start, 8), size), :] for start in blocks], axis=0)

    fill_half(half, parts, (at[3] // step) % 2, kept, away, chunk)
    split_rows(dot(active[...], out[...]), rows, mine, other)
    sums[...] = jnp.zeros_like(sums)
    sums[0:1, :] = jnp.sum(g_hidden[...].astype(F32), axis=0, keepdims=True)


def plain_weights_body(rows, at, normed, active, g_hidden, out, *refs):
    extras = refs[:-6]
    mine, other, out_grad, fc_grad, out_sums, fc_sums = refs[-6:]
    g_out = g_output(extras, rows)
    split_rows(dot(active[...], out[...]), rows, mine, other)
    out_grad[...] = dot_rows(active[...], g_out).astype(BF)
    fc_grad[...] = dot_rows(normed[...], g_hidden[...]).astype(BF)
    out_sums[...] = jnp.zeros_like(out_sums)
    out_sums[0:1, :] = jnp.sum(g_out[:rows].astype(F32), axis=0, keepdims=True)
    fc_sums[...] = jnp.zeros_like(fc_sums)
    fc_sums[0:1, :] = jnp.sum(g_hidden[...].astype(F32), axis=0, keepdims=True)


def second_norm_body(rows, at, chip_sum, arrived, mid, own_extra, x_extra, vectors, g_branch, own_middle, sums):
    add = arrived[...].astype(F32)
    grad = chip_sum[...] + jnp.concatenate([add[rows:], add[:rows]], axis=0)
    unit, scale = normalize(mid[...])
    back = norm_back(grad, unit, scale, vectors[2:3])
    sums[...] = jnp.zeros_like(sums)
    sums[0:1, :] = jnp.sum(grad[:rows] * unit[:rows], axis=0, keepdims=True)
    sums[1:2, :] = jnp.sum(grad[:rows], axis=0, keepdims=True)
    g_own = back[:rows] + own_extra[:rows, :].astype(F32)
    own_middle[...] = g_own
    g_branch[:rows, :] = (RESIDUAL * g_own).astype(BF)
    g_branch[rows:, :] = (RESIDUAL * (back[rows:] + x_extra[:rows, :].astype(F32))).astype(BF)


def attended_grad_body(parts, rows, at, mine, other, proj, *refs):
    outs, (kept, g_all) = refs[:parts], refs[parts:]
    kept[:rows, :] = mine[:rows, :]
    kept[rows : 2 * rows, :] = other[:rows, :]
    kept[2 * rows : 3 * rows, :] = mine[rows:, :]
    kept[3 * rows :, :] = other[rows:, :]
    zero = jnp.zeros((HD, proj.shape[1]), BF)
    weight = jnp.concatenate([proj[:128, :], zero, proj[128:, :]], axis=0)
    g_all[...] = dot_columns(kept[...], weight).astype(BF)
    for k in range(parts):
        outs[k][...] = g_all[block_of(at, k, rows), :]


def proj_grad_body(rows, at, attended, g_branch, proj_grad, sums):
    grad = dot_rows(attended[...], g_branch[...])
    proj_grad[...] = jnp.concatenate([grad[:128], grad[128 + HD :]], axis=0)
    sums[...] = jnp.zeros_like(sums)
    sums[0:1, :] = jnp.sum(g_branch[:rows, :].astype(F32), axis=0, keepdims=True)


def pack_wide(values, lanes):
    third = values.shape[0] // 3
    rest = values[:, lanes:]
    low = [rest[i * third : (i + 1) * third] for i in range(3)]
    low.append(jnp.zeros((third, lanes - 384), values.dtype))
    return jnp.concatenate([values[:, :lanes], jnp.concatenate(low, axis=1)], axis=0)


def first_grad_body(parts, rows, half, step, at, normed, matrix, proj_grad, *refs):
    queries, pairs = refs[:parts], refs[parts : 2 * parts]
    mine, other, *grads, sums, mixed, attn_all = refs[2 * parts :]
    for k in range(parts):
        block = block_of(at, k, rows)
        mixed[block, :256] = queries[k][...]
        mixed[block, 256:] = pairs[k][...]
    split_rows(dot_columns(mixed[...], matrix[...]), rows, mine, other)
    attn_all[...] = dot_rows(normed[...], mixed[...])
    sums[...] = jnp.zeros_like(sums)
    sums[0:1, :] = jnp.sum(mixed[...].astype(F32), axis=0, keepdims=True)
    if not half:
        grads[0][...] = attn_all[...].astype(BF)
        grads[1][...] = proj_grad[...].astype(BF)
        return
    lanes = attn_all.shape[1]
    size = attn_all.shape[0] // (parts * 2 * half)

    def chunk(i):
        blocks = [((at[2] ^ j) * 2 * half + i) * size for j in range(parts)]
        found = [attn_all[pl.ds(pl.multiple_of(start, 8), size), :] for start in blocks]
        found.append(pack_wide(proj_grad[pl.ds(pl.multiple_of(i * size, 8), size), :], lanes))
        return jnp.concatenate(found, axis=0)

    fill_half(half, parts, (at[3] // step) % 2, *grads, chunk)


def first_norm_body(rows, at, own, arrived, tokens, own_middle, vectors, two, proj, out_sums, fc_sums, attn, input_grad, whole, local):
    grad = own[:rows, :] + arrived[...].astype(F32)
    unit, scale = normalize(tokens[...].astype(F32))
    back = norm_back(grad, unit, scale, vectors[0:1])
    input_grad[...] = (back + own_middle[...]).astype(BF)
    whole[0:1, :] = jnp.sum(grad * unit, axis=0, keepdims=True)
    whole[1:2, :] = jnp.sum(grad, axis=0, keepdims=True)
    whole[2:4, :] = two[0:2, :]
    whole[4:5, :] = proj[0:1, :]
    whole[5:6, :] = out_sums[0:1, :]
    whole[6:8, :] = jnp.zeros_like(whole[6:8, :])
    local[0:1, :] = fc_sums[0:1, :]
    local[1:2, :] = jnp.zeros_like(local[1:2, :])
    local[1:2, :256] = attn[0:1, :256]
    local[1:2, 256:384] = attn[0:1, 384:512]
    local[1:2, 384:512] = attn[0:1, 512:]
    local[2:, :] = jnp.zeros_like(local[2:, :])


def vector_pack_body(parts, at, mine, across, local, out):
    total = mine[...] + across[...]
    width = total.shape[1] // parts
    out[...] = jnp.zeros_like(out)
    for owner in range(parts):

        @pl.when(at[2] == owner)
        def _():
            out[0:6, :width] = total[0:6, owner * width : (owner + 1) * width]

    out[6:8, :] = local[0:2, :]


def vector_final_body(at, *refs):
    count = len(refs) - 9
    total = refs[0][...]
    for ref in refs[1:count]:
        total = total + ref[...]
    outs = refs[count:]
    width = outs[0].shape[0]
    for row in range(6):
        outs[row][...] = total[row : row + 1, :width].reshape(width)
    outs[6][...] = total[7:8, :width].reshape(width)
    value = jnp.concatenate([total[7:8, 256:384], total[7:8, 384 + HD : 512]], axis=1)
    outs[7][...] = value.reshape(width)
    outs[8][...] = total[6:7, :].reshape(total.shape[1])


def halve_body(step, at, held, arrived, kept, away, total):
    total[...] = held[...] + arrived[...].astype(F32)
    half = kept.shape[0]
    bit = (at[3] // step) % 2
    kept[...] = total[rows_at(bit, half), :]
    away[...] = total[rows_at(1 - bit, half), :].astype(BF)


def last_sum_body(at, held, arrived, *outs):
    total = held[...] + arrived[...].astype(F32)
    start = 0
    for out in outs:
        out[...] = total[start : start + out.shape[0]].astype(BF)
        start += out.shape[0]


def stack_rows_body(at, *refs):
    out = refs[-1]
    start = 0
    for ref in refs[:-1]:
        out[start : start + ref.shape[0], :] = ref[...]
        start += ref.shape[0]


def chunk_number(at, mask, steps):
    number = 0
    for step in steps:
        number = number * 2 + ((at[3] ^ mask) // step) % 2
    return number


def chunks_of(at, steps, refs):
    masks = [0]
    found = [(0, refs[0], 0)]
    for step, ref in zip(reversed(steps), refs[1:]):
        found += [(mask ^ step, ref, i) for i, mask in enumerate(masks)]
        masks = masks + [mask ^ step for mask in masks]
    size = refs[0].shape[0]
    for mask, ref, i in found:
        yield chunk_number(at, mask, steps), ref[i * size : (i + 1) * size, :].astype(F32)


def out_final_body(steps, at, *refs):
    for place, piece in chunks_of(at, steps, refs[:-1]):
        refs[-1][rows_at(place, piece.shape[0]), :] = piece


def fc_final_body(parts, steps, at, *refs):
    out = refs[-1]
    hidden = out.shape[1] // parts
    for place, piece in chunks_of(at, steps, refs[:-1]):
        size = piece.shape[0] // parts
        for j in range(parts):
            lanes = pl.ds(pl.multiple_of((at[2] ^ j) * hidden, 128), hidden)
            out[rows_at(place, size), lanes] = piece[j * size : (j + 1) * size]


def attn_final_body(parts, steps, at, *refs):
    attn_grad, proj_grad, kept = refs[-3:]
    features = proj_grad.shape[1]
    width = features // parts
    lanes = kept.shape[2]
    for place, piece in chunks_of(at, steps, refs[:-3]):
        size = proj_grad.shape[0] // 2 ** len(steps)
        rows = rows_at(place, size)
        for j in range(parts):
            kept[at[2] ^ j, rows, :] = piece[j * size : (j + 1) * size]
        start = parts * size
        proj_grad[rows, :lanes] = piece[start : start + size]
        low = piece[start + size :]
        proj_grad[rows, lanes:] = jnp.concatenate([low[:, i * 128 : (i + 1) * 128] for i in range(3)], axis=0)
    for g in range(parts):
        first = g * width
        attn_grad[:, first : first + width] = kept[g, :, :width]
        first += features
        attn_grad[:, first : first + width] = jnp.concatenate([kept[g, :, 256:384], kept[g, :, 512 : 512 + HD]], axis=1)
        first += features
        attn_grad[:, first : first + width] = jnp.concatenate([kept[g, :, 384:512], kept[g, :, 512 + HD :]], axis=1)


def shards(
    parts,
    ways,
    tokens,
    first_gain,
    first_bias,
    attn_weight,
    query_bias,
    value_bias,
    proj_weight,
    proj_bias,
    second_gain,
    second_bias,
    fc_weight,
    fc_bias,
    out_weight,
    out_bias,
    cotangent,
):
    rows, features = tokens.shape[1], tokens.shape[2]
    width = features // parts
    count = parts
    blocks = ways // count
    hidden = fc_weight.shape[1] // parts
    all_rows, half_rows = parts * rows, parts * rows // 2
    f = lax.axis_index("fsdp").astype(jnp.int32)
    c = lax.axis_index("ctx").astype(jnp.int32)
    a, b = c // blocks, c % blocks
    at = jnp.stack([a, b, f, c])
    halved = ways == 8
    out_steps, fc_steps, attn_steps = (1, 2, 4), (2, 1, 4), (1, 2, 4)
    chunks = 4

    def over_fsdp(value, k):
        return lax.ppermute(value, "fsdp", [(i, i ^ k) for i in range(parts)])

    def over_ctx(value, k):
        return lax.ppermute(value, "ctx", [(i, i ^ k) for i in range(ways)])

    def spread(value):
        across = over_fsdp(value, 2)
        return [value, over_fsdp(value, 1), across, over_fsdp(across, 1)]

    def turn_fsdp(pieces):
        return [pieces[0]] + [over_fsdp(pieces[k], k) for k in range(1, parts)]

    def turn_ctx(pieces):
        return [pieces[0]] + [over_ctx(pieces[k], k * blocks) for k in range(1, count)]

    def halve(name, kept, arrived, step, after=()):
        size, lanes = kept.shape[0] // 2, kept.shape[1]
        return call(
            partial(halve_body, step),
            name,
            [shape((size, lanes), F32), shape((size, lanes), BF)],
            at,
            kept,
            arrived,
            scratch=[pltpu.VMEM((2 * size, lanes), F32)],
            after=after,
        )

    def last_sum(name, kept, arrived, cuts, after=()):
        outs = [shape((cut, kept.shape[1]), BF) for cut in cuts]
        return call(last_sum_body, name, outs, at, kept, arrived, after=after)

    def stacked(name, pieces, after=()):
        total = sum(piece.shape[0] for piece in pieces)
        outs = [shape((total, pieces[0].shape[1]), BF)]
        return call(stack_rows_body, name, outs, at, *pieces, after=after)[0]

    tok = tokens[0]
    tok_all = spread(tok)
    columns = 256 + 2 * width
    attn_pieces = call(
        partial(attn_columns_body, parts),
        "attn_columns",
        [shape((width, columns), BF)] * parts,
        at,
        *map(Direct, (attn_weight, first_gain, first_bias, second_gain, second_bias, proj_bias, out_bias)),
    )
    attn_pieces = turn_fsdp(attn_pieces)
    fc_pieces = call(
        fc_columns_body,
        "fc_columns",
        [shape((width, hidden), BF)] * parts,
        at,
        Direct(fc_weight),
        after=attn_pieces[1:],
    )
    fc_pieces = turn_fsdp(fc_pieces)

    mixed = call(
        partial(mixed_body, parts, count),
        "mixed",
        [shape((all_rows, features), BF), shape((features, columns), BF), shape((8, features), F32)]
        + [shape((rows, 256), BF)] * count
        + [shape((rows, 384), BF)] * count,
        at,
        query_bias,
        value_bias,
        *tok_all,
        *attn_pieces,
        scratch=[pltpu.VMEM((all_rows, columns), BF)],
    )
    normed, attn_matrix, vectors = mixed[:3]
    extra = call(
        stack_rows_body,
        "stack_extra",
        [shape((rows + width, features), BF)],
        at,
        Direct(cotangent[0]),
        Direct(proj_weight),
        after=[vectors],
    )[0]
    extra = spread(extra)

    pairs = turn_ctx(mixed[3 + count :])
    queries = turn_ctx(mixed[3 : 3 + count])
    joined, fc_matrix = call(
        partial(stack_body, count),
        "stack_pairs",
        [shape((count * rows, pairs[0].shape[1]), BF), shape((features, hidden), BF)],
        at,
        *pairs,
        *fc_pieces,
    )
    partners = [over_ctx(joined, j) for j in range(1, blocks)]
    small_blocks = blocks * count * rows <= 1024
    if small_blocks:
        kept = call(
            partial(attend_body, count, blocks, rows),
            "attend",
            [shape((rows + rows // 2, 128), BF)] * count
            + [
                shape((count * rows, 256), F32),
                shape((count * rows, 128), F32),
                shape((count * rows, 256), BF),
                shape((count * blocks * rows, 384), BF),
            ],
            at,
            *queries,
            *pairs,
            *partners,
            after=extra,
        )
    else:
        kept = plain_attend(count, blocks, rows, at, queries, pairs, partners)
    att_pieces, state = turn_ctx(kept[:count]), kept[count:]
    attended_all = lax.all_gather(jnp.concatenate(att_pieces, 0), "fsdp")

    gn_mine, gn_other, mid_mine, normed_two, active, g_hidden, attended = call(
        partial(middle_body, parts, rows),
        "middle",
        [shape((half_rows, features), F32)] * 3
        + [shape((all_rows, features), BF), shape((all_rows, hidden), BF), shape((all_rows, hidden), BF)]
        + [shape((all_rows, 256), BF)],
        at,
        attended_all,
        vectors,
        fc_matrix,
        fc_bias,
        out_weight,
        *tok_all,
        *extra,
        scratch=[pltpu.VMEM((all_rows, parts * 256), BF), pltpu.VMEM((parts * 256, features), BF)],
    )
    chip_sum = gn_mine + over_fsdp(gn_other, 1)
    chip_low = chip_sum.astype(BF)
    arrived = over_fsdp(chip_low, 2)
    mlp_sums = [shape((8, features), F32), shape((8, hidden), F32)]
    if halved:
        out_kept, out_away, out_sums = call(
            partial(out_weights_body, rows, out_steps[0]),
            "out_weights",
            [shape((hidden // 2, features), F32), shape((hidden // 2, features), BF), mlp_sums[0]],
            at,
            active,
            *extra,
            scratch=[pltpu.VMEM((hidden, features), F32)],
            after=[chip_low],
        )
        mine, other, fc_kept, fc_away, fc_sums = call(
            partial(fc_weights_body, parts, rows, chunks, fc_steps[0]),
            "fc_weights",
            [shape((half_rows, features), F32)] * 2
            + [shape((features // 2, hidden), F32), shape((features // 2, hidden), BF), mlp_sums[1]],
            at,
            normed_two,
            active,
            g_hidden,
            out_weight,
            scratch=[pltpu.VMEM((features, hidden), F32)],
            after=[out_away],
        )
    else:
        mine, other, out_grad, fc_grad, out_sums, fc_sums = call(
            partial(plain_weights_body, rows),
            "mlp_weights",
            [shape((half_rows, features), F32)] * 2
            + [shape((hidden, features), BF), shape((features, hidden), BF)]
            + mlp_sums,
            at,
            normed_two,
            active,
            g_hidden,
            out_weight,
            *extra,
        )
    if halved:
        out_in = over_ctx(out_away, out_steps[0])
        fc_in = over_ctx(fc_away, fc_steps[0])
    g_branch, own_middle, sums_two = call(
        partial(second_norm_body, rows),
        "second_norm",
        [shape((half_rows, features), BF), shape((rows, features), F32), shape((8, features), F32)],
        at,
        chip_sum,
        arrived,
        mid_mine,
        extra[0],
        extra[2],
        vectors,
        after=[fc_sums],
    )
    grads = call(
        partial(attended_grad_body, parts, rows),
        "attended_grad",
        [shape((rows, 256), BF)] * parts + [shape((all_rows, features), BF)],
        at,
        g_branch,
        over_fsdp(g_branch, 1),
        proj_weight,
        scratch=[pltpu.VMEM((all_rows, 256), BF)],
    )
    g_pieces, g_branch_all = turn_ctx(grads[:parts]), grads[parts]
    proj_grad, sums_proj = call(
        partial(proj_grad_body, rows),
        "proj_weight_grad",
        [shape((width, features), F32), shape((8, features), F32)],
        at,
        attended,
        g_branch_all,
    )
    if halved:
        out_kept, out_away = halve("out_halve_one", out_kept, out_in, out_steps[1])
        out_in = over_ctx(out_away, out_steps[1])
    if small_blocks:
        back = call(
            partial(attend_back_body, count, blocks, rows),
            "attend_back",
            [shape((rows, 256), BF)] * count
            + [shape((count * rows, 384), F32), shape(((blocks - 1) * count * rows, 384), BF)],
            at,
            *g_pieces,
            state[2],
            state[3],
            state[0],
            state[1],
            scratch=[
                pltpu.VMEM((count * rows, 256), BF),
                pltpu.VMEM((count * rows, 256), BF),
                pltpu.VMEM((count * blocks * rows, 384), F32),
            ],
            after=[out_away] if halved else [],
        )
    else:
        back = plain_attend_back(count, blocks, rows, at, g_pieces, state[2], state[3], state[0], state[1])
    dq, own, away = back[:count], back[count], back[count + 1]
    stack = count * rows
    from_partners = [over_ctx(away[(j - 1) * stack : j * stack], j) for j in range(1, blocks)]
    if halved:
        fc_kept, fc_away = halve("fc_halve_one", fc_kept, fc_in, fc_steps[1])
        fc_in = over_ctx(fc_away, fc_steps[1])
    dkv = call(
        partial(merge_body, count, rows),
        "merge",
        [shape((rows, 384), BF)] * count,
        at,
        own,
        *from_partners,
        after=[fc_away] if halved else [],
    )
    dq, dkv = turn_ctx(dq), turn_ctx(dkv)
    if halved:
        out_kept, out_away = halve("out_halve_two", out_kept, out_in, out_steps[2])
        out_in = over_ctx(out_away, out_steps[2])
        fc_kept, fc_away = halve("fc_halve_two", fc_kept, fc_in, fc_steps[2])
        fc_in = over_ctx(fc_away, fc_steps[2])
        size = width // (2 * chunks)
        packed = size + size // 3
        chunk = parts * size + packed
        attn_grads = [shape((chunks * chunk, columns), F32), shape((chunks * chunk, columns), BF)]
    else:
        attn_grads = [shape((features, columns), BF), shape((width, features), BF)]
    g1_mine, g1_other, *attn_grads, sums_attn = call(
        partial(first_grad_body, parts, rows, chunks if halved else 0, attn_steps[0]),
        "first_grad",
        [shape((half_rows, features), F32)] * 2 + attn_grads + [shape((8, columns), F32)],
        at,
        normed,
        attn_matrix,
        proj_grad,
        *dq,
        *dkv,
        scratch=[pltpu.VMEM((all_rows, columns), BF), pltpu.VMEM((features, columns), F32)],
        after=[out_away, fc_away] if halved else [],
    )
    first_sum = g1_mine + over_fsdp(g1_other, 1)
    input_grad, vectors_whole, vectors_local = call(
        partial(first_norm_body, rows),
        "first_norm",
        [shape((rows, features), BF), shape((8, features), F32), shape((8, hidden), F32)],
        at,
        first_sum,
        over_fsdp(first_sum[rows:].astype(BF), 2),
        tok,
        own_middle,
        vectors,
        sums_two,
        sums_proj,
        out_sums,
        fc_sums,
        sums_attn,
    )
    out_sum = mine + over_fsdp(other, 1)
    output = out_sum[:rows] + over_fsdp(out_sum[rows:].astype(BF), 2).astype(F32) + vectors[5:6]
    block_out = (mid_mine[:rows] + RESIDUAL * output).astype(BF)

    vectors_whole = vectors_whole + over_fsdp(vectors_whole, 1)
    vector_sums = call(
        partial(vector_pack_body, parts),
        "vector_pack",
        [shape((8, hidden), F32)],
        at,
        vectors_whole,
        over_fsdp(vectors_whole, 2),
        vectors_local,
    )[0]
    if blocks == 2:
        vector_sums = vector_sums + over_ctx(vector_sums, 1)
        vector_sums = [vector_sums] + [over_ctx(vector_sums, 2 * k) for k in range(1, count)]
    else:
        vector_sums = [lax.psum(vector_sums, "ctx")]
    vector_grads = call(
        vector_final_body,
        "vector_final",
        [shape((width,), F32)] * 8 + [shape((hidden,), F32)],
        at,
        *vector_sums,
    )
    first_gain_grad, first_bias_grad, second_gain_grad, second_bias_grad = vector_grads[:4]
    proj_bias_grad, out_bias_grad, query_bias_grad, value_bias_grad, fc_bias_grad = vector_grads[4:]

    if halved:
        kept, away = attn_grads
        attn_in = over_ctx(away, attn_steps[0])
        out_part = last_sum("out_sum", out_kept, out_in, [hidden // (2 * chunks)])[0]
        fc_parts = last_sum("fc_sum", fc_kept, fc_in, [size] * parts)
        out_pieces = [out_part, over_ctx(out_part, out_steps[2])]
        fc_part = stacked("fc_turned", turn_fsdp(fc_parts))
        fc_pieces = [fc_part, over_ctx(fc_part, fc_steps[2])]
        kept, away = halve("attn_halve_one", kept, attn_in, attn_steps[1], after=[out_part, fc_parts[0], vectors_whole])
        attn_in = over_ctx(away, attn_steps[1])
        out_pieces.append(over_ctx(stacked("out_two", out_pieces), out_steps[1]))
        fc_message = stacked("fc_two", fc_pieces)
        fc_pieces.append(over_ctx(fc_message, fc_steps[1]))
        kept, away = halve("attn_halve_two", kept, attn_in, attn_steps[2], after=[fc_message, vector_sums[0]])
        attn_in = over_ctx(away, attn_steps[2])
        out_message = stacked("out_four", out_pieces)
        out_pieces.append(over_ctx(out_message, out_steps[0]))
        fc_message = stacked("fc_four", fc_pieces)
        fc_pieces.append(over_ctx(fc_message, fc_steps[0]))
        *attn_parts, proj_part = last_sum(
            "attn_sum", kept, attn_in, [size] * parts + [packed], after=[out_message, fc_message]
        )
        attn_part = stacked("attn_turned", [*turn_fsdp(attn_parts), proj_part])
        attn_pieces = [attn_part, over_ctx(attn_part, attn_steps[2])]
        attn_pieces.append(over_ctx(stacked("attn_two", attn_pieces), attn_steps[1]))
        out_weight_grad = call(
            partial(out_final_body, out_steps),
            "out_final",
            [shape((hidden, features), F32)],
            at,
            *out_pieces,
        )[0]
        fc_weight_grad = call(
            partial(fc_final_body, parts, fc_steps),
            "fc_final",
            [shape((width, parts * hidden), F32)],
            at,
            *fc_pieces,
        )[0]
        attn_pieces.append(over_ctx(stacked("attn_four", attn_pieces), attn_steps[0]))
        attn_weight_grad, proj_weight_grad = call(
            partial(attn_final_body, parts, attn_steps),
            "attn_final",
            [shape((width, 3 * features), F32), shape((width, features), F32)],
            at,
            *attn_pieces,
            scratch=[pltpu.VMEM((parts, width, columns), F32)],
        )
    else:

        def over_all(value):
            part = lax.psum_scatter(value, "ctx", scatter_dimension=1, tiled=True)
            return lax.all_gather(part, "ctx", axis=1, tiled=True)

        out_weight_grad = over_all(out_grad).astype(F32)
        fc_grad = over_all(fc_grad).reshape(parts, width, hidden)
        fc_grad = lax.all_to_all(fc_grad, "fsdp", split_axis=0, concat_axis=0)
        fc_weight_grad = fc_grad.transpose(1, 0, 2).reshape(width, parts * hidden).astype(F32)
        proj_weight_grad = over_all(attn_grads[1]).astype(F32)
        attn_all = over_all(attn_grads[0]).reshape(parts, width, columns)
        attn_all = lax.all_to_all(attn_all, "fsdp", split_axis=0, concat_axis=0).transpose(1, 0, 2)
        q = attn_all[:, :, :width]
        k = jnp.concatenate([attn_all[:, :, 256:384], attn_all[:, :, 512 : 512 + HD]], 2)
        v = jnp.concatenate([attn_all[:, :, 384:512], attn_all[:, :, 512 + HD :]], 2)
        attn_weight_grad = jnp.stack([q, k, v], 1).reshape(width, 3 * features).astype(F32)
    return (
        block_out[None],
        input_grad[None],
        first_gain_grad,
        first_bias_grad,
        attn_weight_grad,
        query_bias_grad,
        value_bias_grad,
        proj_weight_grad,
        proj_bias_grad,
        second_gain_grad,
        second_bias_grad,
        fc_weight_grad,
        fc_bias_grad,
        out_weight_grad,
        out_bias_grad,
    )


def solution(mesh):
    rows, row, matrix = P("fsdp", "ctx", None), P("fsdp"), P("fsdp", None)
    return jax.shard_map(
        partial(shards, mesh.shape["fsdp"], mesh.shape["ctx"]),
        mesh=mesh,
        in_specs=(
            rows, row, row, matrix, row, row, matrix, row, row, row, matrix, row, matrix, row, rows,
        ),
        out_specs=(
            rows, rows, row, row, matrix, row, row, matrix, row, row, row, matrix, row, matrix, row,
        ),
        check_vma=False,
    )
```

```python
from functools import partial

import jax
import jax.numpy as jnp
from jax import lax
from jax.experimental import pallas as pl
from jax.experimental.pallas import tpu as pltpu
from jax.sharding import PartitionSpec as P

HD = 64
LAYERS = 12
EPSILON = 1e-05
BF = jnp.bfloat16
F32 = jnp.float32
RESIDUAL = LAYERS ** (-0.5)
SCORE = HD ** (-0.5)
NEVER = -1e30
OUT_STEPS, FC_STEPS = (1, 2, 4), (2, 1, 4)
MERGE_PERMUTES = False


def shape(dims, kind):
    return jax.ShapeDtypeStruct(dims, kind)


def call(body, name, outs, *args, scratch=(), after=(), us=1.0, mib=16):
    vmem = pl.BlockSpec(memory_space=pltpu.VMEM)
    smem = pl.BlockSpec(memory_space=pltpu.SMEM)
    held = pl.BlockSpec(memory_space=pl.ANY)
    count, waits = len(args), len(after)

    def run(*refs):
        body(*refs[:count], *refs[count + waits :])

    return pl.pallas_call(
        run,
        name=name,
        out_shape=outs,
        in_specs=[smem] + [vmem] * (count - 1) + [held] * waits,
        out_specs=[vmem] * len(outs),
        scratch_shapes=list(scratch),
        cost_estimate=pl.CostEstimate(flops=int(us * 1e3), transcendentals=0, bytes_accessed=int(us * 1e3)),
        compiler_params=pltpu.CompilerParams(vmem_limit_bytes=mib * 1024 * 1024),
    )(*args, *after)


def rows_at(index, size):
    return pl.ds(pl.multiple_of(index * size, size), size)


def dot(first, second):
    return jnp.dot(first, second, preferred_element_type=F32)


def dot_rows(first, second):
    return lax.dot_general(first, second, (((0,), (0,)), ((), ())), preferred_element_type=F32)


def dot_columns(first, second):
    return lax.dot_general(first, second, (((1,), (1,)), ((), ())), preferred_element_type=F32)


def normalize(values):
    center = jnp.mean(values, axis=-1, keepdims=True)
    centered = values - center
    spread = jnp.mean(centered * centered, axis=-1, keepdims=True)
    scale = lax.rsqrt(spread + EPSILON)
    return centered * scale, scale


def norm_back(grad, unit, scale, gain):
    inner = grad * gain
    mean_inner = jnp.mean(inner, axis=-1, keepdims=True)
    mean_along = jnp.mean(inner * unit, axis=-1, keepdims=True)
    return scale * (inner - mean_inner - unit * mean_along)


def join(at, pieces, whole):
    size = pieces[0].shape[0]
    for k, piece in enumerate(pieces):
        whole[rows_at(at[2] ^ k, size), :] = piece[...]


def as_row(ref):
    return ref[...].astype(F32).reshape(1, ref.shape[0])


def attn_columns_body(parts, at, attn, *pieces):
    features = attn.shape[1] // 3
    width = features // parts
    for owner in range(parts):

        @pl.when(at[2] == owner)
        def _():
            for k in range(parts):
                first = (owner ^ k) * width
                piece = pieces[k]
                piece[:, :width] = attn[:, first : first + width]
                piece[:, width:256] = jnp.zeros((width, 256 - width), BF)
                key = attn[:, features + first : features + first + width]
                value = attn[:, 2 * features + first : 2 * features + first + width]
                piece[:, 256:384] = key[:, :128]
                piece[:, 384:512] = value[:, :128]
                piece[:, 512 : 512 + HD] = key[:, 128:]
                piece[:, 512 + HD :] = value[:, 128:]


def token_message_body(at, tokens, *refs):
    vectors, out = refs[:-1], refs[-1]
    rows, width = tokens.shape[0], vectors[0].shape[0]
    out[:rows, :] = tokens[...]
    small = jnp.concatenate([as_row(ref) for ref in vectors] + [jnp.zeros((8 - len(vectors), width), F32)], axis=0)
    rest = jnp.zeros((8, tokens.shape[1] - width), F32)
    out[rows:, :] = jnp.concatenate([small, rest], axis=1).astype(BF)


def fc_columns_body(at, fc, *pieces):
    for k, piece in enumerate(pieces):
        hidden = piece.shape[1]
        piece[...] = fc[:, pl.ds(pl.multiple_of((at[2] ^ k) * hidden, 128), hidden)]


def join_body(at, *refs):
    join(at, refs[:-1], refs[-1])


def block_of(at, k, rows):
    return rows_at(at[2] ^ at[0] ^ k, rows)


def mixed_body(parts, count, at, query_bias, value_bias, *refs):
    tokens, weights = refs[:parts], refs[parts : 2 * parts]
    normed, matrix, vectors, *outs, kept = refs[2 * parts :]
    rows = tokens[0].shape[0] - 8
    join(at, weights, matrix)
    columns = matrix.shape[1]
    width = weights[0].shape[0]
    for owner in range(parts):

        @pl.when(at[2] == owner)
        def _():
            for k in range(parts):
                lanes = slice((owner ^ k) * width, ((owner ^ k) + 1) * width)
                vectors[:, lanes] = tokens[k][rows:, :width].astype(F32)

    small = vectors[...]
    for k in range(parts):
        unit, _ = normalize(tokens[k][:rows, :].astype(F32))
        normed[k * rows : (k + 1) * rows, :] = (unit * small[0:1] + small[1:2]).astype(BF)
    query, value = as_row(query_bias), as_row(value_bias)
    none = jnp.zeros((1, 128), F32)
    bias = [query, none[:, :HD], none, value[:, :128], none[:, :HD], value[:, 128:]]
    bias = jnp.concatenate(bias, axis=1)
    kept[...] = (dot(normed[...], matrix[...]) + bias).astype(BF)
    half = rows // 2
    third = normed.shape[1] // 6
    first = (at[2] % 2) * 3 * third
    for k in range(count):
        block = block_of(at, k, rows)
        outs[k][:rows, :] = kept[block, :256]
        part = normed[block, pl.ds(pl.multiple_of(first, 128), 3 * third)]
        outs[k][rows : 2 * rows, :] = part[:, : 2 * third]
        outs[k][2 * rows :, :third] = part[:half, 2 * third :]
        outs[k][2 * rows :, third:] = part[half:, 2 * third :]
        outs[count + k][...] = kept[block, 256:]


def normed_stack_body(rows, at, *refs):
    half = rows // 2
    out = refs[-1]
    third = out.shape[1] // 3
    for k, ref in enumerate(refs[:-1]):
        part = slice(k * rows, (k + 1) * rows)
        out[part, : 2 * third] = ref[rows : 2 * rows, :]
        out[k * rows : k * rows + half, 2 * third :] = ref[2 * rows :, :third]
        out[k * rows + half : (k + 1) * rows, 2 * third :] = ref[2 * rows :, third:]


def normed_place_body(count, blocks, rows, at, *refs):
    sides, (every, own) = refs[:-2], refs[-2:]
    lanes = sides[0].shape[1]
    core = at[2] % 2
    for side in range(2):
        part = pl.ds(pl.multiple_of((core if side == 0 else 1 - core) * lanes, 128), lanes)
        for j in range(blocks):
            ref = sides[side * blocks + j]
            for k in range(count):
                row = at[0] ^ k
                piece = ref[k * rows : (k + 1) * rows, :]
                every[rows_at(row * blocks + (at[1] ^ j), rows), part] = piece
                if j == 0:
                    own[rows_at(row, rows), part] = piece


def place(at, count, blocks, rows, queries, pairs, partners, q_all, kv_all):
    for k in range(count):
        row = at[0] ^ k
        q_all[rows_at(row, rows), :] = queries[k][:rows, :]
        kv_all[rows_at(row * blocks + at[1], rows), :] = pairs[k][...]
        for j, partner in enumerate(partners):
            side = row * blocks + (at[1] ^ (j + 1))
            kv_all[rows_at(side, rows), :] = partner[k * rows : (k + 1) * rows, :]


def head_views(tile_one, tile_two, scale):
    low = lax.broadcasted_iota(jnp.int32, tile_one.shape, 1) < HD
    zero = jnp.zeros_like(tile_one)
    tile_one = tile_one * scale if scale is not None else tile_one
    tile_two = tile_two * scale if scale is not None else tile_two
    return (jnp.where(low, tile_one, zero), jnp.where(low, zero, tile_one), tile_two)


def visible_keys(at, i, blocks, rows, keys):
    query = (i * blocks + at[1]) * rows + lax.broadcasted_iota(jnp.int32, (rows, keys), 0)
    return lax.broadcasted_iota(jnp.int32, (rows, keys), 1) <= query


def attend_body(count, blocks, rows, at, *refs):
    queries, pairs = refs[:count], refs[count : 2 * count]
    partners = refs[2 * count : 2 * count + blocks - 1]
    outs = refs[2 * count + blocks - 1 :]
    pieces, (exact, totals, q_all, kv_all) = outs[:count], outs[count:]
    place(at, count, blocks, rows, queries, pairs, partners, q_all, kv_all)
    low = lax.broadcasted_iota(jnp.int32, (rows, 128), 1) < HD
    for i in range(count):
        keys = (i + 1) * blocks * rows
        mine = slice(i * rows, (i + 1) * rows)
        heads = head_views(q_all[mine, :128], q_all[mine, 128:], SCORE)
        seen = visible_keys(at, i, blocks, rows, keys)
        found = []
        for h, query in enumerate(heads):
            key_cols = slice(0, 128) if h < 2 else slice(256, 384)
            value_cols = slice(128, 256) if h < 2 else slice(256, 384)
            scores = jnp.where(seen, dot_columns(query, kv_all[:keys, key_cols]), NEVER)
            highest = jnp.max(scores, axis=-1, keepdims=True)
            weights = jnp.exp(scores - highest)
            total = jnp.sum(weights, axis=-1, keepdims=True)
            totals[mine, h : h + 1] = highest + jnp.log(total)
            weights = (weights * (1.0 / total)).astype(BF)
            found.append(dot(weights, kv_all[:keys, value_cols]))
        exact[mine, :128] = jnp.where(low, found[0], found[1])
        exact[mine, 128:] = jnp.where(low, 0.0, found[2])
    half = rows // 2
    for k in range(count):
        block = rows_at(at[0] ^ k, rows)
        pieces[k][:rows, :] = exact[block, :128].astype(BF)
        last = exact[block, 128:]
        pair = jnp.where(low[:half], pltpu.roll(last[:half], HD, 1), last[half:])
        pieces[k][rows:, :] = pair.astype(BF)


def attend_back_body(count, blocks, rows, at, *refs):
    grads, (q_all, kv_all, exact, totals) = refs[:count], refs[count : count + 4]
    outs = refs[count + 4 :]
    own, away, dq_all, summed, g_all, acc = outs
    for k in range(count):
        g_all[rows_at(at[0] ^ k, rows), :] = grads[k][...]
    acc[...] = jnp.zeros_like(acc)
    low = lax.broadcasted_iota(jnp.int32, (rows, 128), 1) < HD
    for i in range(count):
        keys = (i + 1) * blocks * rows
        mine = slice(i * rows, (i + 1) * rows)
        q_heads = head_views(q_all[mine, :128], q_all[mine, 128:], SCORE)
        g_heads = head_views(g_all[mine, :128], g_all[mine, 128:], None)
        seen = visible_keys(at, i, blocks, rows, keys)
        found = []
        for h in range(3):
            key_cols = slice(0, 128) if h < 2 else slice(256, 384)
            value_cols = slice(128, 256) if h < 2 else slice(256, 384)
            kept = exact[mine, :128] if h < 2 else exact[mine, 128:]
            delta = jnp.sum(g_heads[h].astype(F32) * kept, axis=-1, keepdims=True)
            scores = dot_columns(q_heads[h], kv_all[:keys, key_cols]) - totals[mine, h : h + 1]
            weights = jnp.exp(jnp.where(seen, scores, NEVER))
            g_weights = dot_columns(g_heads[h], kv_all[:keys, value_cols])
            g_scores = (weights * (g_weights - delta)).astype(BF)
            found.append(dot(g_scores, kv_all[:keys, key_cols]))
            acc[:keys, key_cols] += dot_rows(g_scores, q_heads[h])
            acc[:keys, value_cols] += dot_rows(weights.astype(BF), g_heads[h])
        dq_all[mine, :128] = (jnp.where(low, found[0], found[1]) * SCORE).astype(BF)
        dq_all[mine, 128:] = (jnp.where(low, found[2], 0.0) * SCORE).astype(BF)
    summed[...] = acc[...].astype(BF)
    for i in range(count):
        into = slice(i * rows, (i + 1) * rows)
        own[into, :] = acc[rows_at(i * blocks + at[1], rows), :]
        for j in range(1, blocks):
            from_rows = slice(((j - 1) * count + i) * rows, ((j - 1) * count + i + 1) * rows)
            away[from_rows, :] = acc[rows_at(i * blocks + (at[1] ^ j), rows), :].astype(BF)


def plain_heads(values):
    zero = jnp.zeros_like(values[:, :HD])
    first = jnp.concatenate([values[:, :HD], zero], 1)
    second = jnp.concatenate([zero, values[:, HD:128]], 1)
    return (first, second, values[:, 128:])


def plain_terms(at, count, blocks, rows):
    q_pos = (jnp.arange(count)[:, None] * blocks + at[1]) * rows + jnp.arange(rows)[None]
    k_pos = jnp.arange(count * blocks * rows)
    return k_pos[None] <= q_pos.reshape(-1)[:, None]


def plain_attend(count, blocks, rows, at, queries, pairs, partners):
    width = pairs[0].shape[1]
    q_all = jnp.zeros((count, rows, queries[0].shape[1]), BF)
    kv_all = jnp.zeros((count, blocks, rows, width), BF)
    for k in range(count):
        row = at[0] ^ k
        q_all = q_all.at[row].set(queries[k][:rows])
        kv_all = kv_all.at[row, at[1]].set(pairs[k])
        for j, partner in enumerate(partners):
            kv_all = kv_all.at[row, at[1] ^ (j + 1)].set(partner[k * rows : (k + 1) * rows])
    q_all, kv_all = q_all.reshape(count * rows, -1), kv_all.reshape(-1, width)
    seen = plain_terms(at, count, blocks, rows)
    found, totals = [], []
    for h, query in enumerate(plain_heads(q_all)):
        key = kv_all[:, :128] if h < 2 else kv_all[:, 256:]
        value = kv_all[:, 128:256] if h < 2 else kv_all[:, 256:]
        scores = jnp.where(seen, dot_columns(query, key) * SCORE, NEVER)
        total = jax.nn.logsumexp(scores, axis=-1, keepdims=True)
        found.append(dot(jnp.exp(scores - total).astype(BF), value))
        totals.append(total)
    exact = jnp.concatenate([found[0][:, :HD], found[1][:, HD:], jnp.zeros_like(found[2][:, :HD]), found[2][:, HD:]], 1)
    grid = exact.astype(BF).reshape(count, rows, -1)
    half = rows // 2
    pair = jnp.concatenate([grid[:, :half, 128 + HD :], grid[:, half:, 128 + HD :]], 2)
    grid = jnp.concatenate([grid[:, :, :128], pair], 1)
    pieces = [grid[at[0] ^ k] for k in range(count)]
    totals = jnp.concatenate(totals + [jnp.zeros((count * rows, 125), F32)], 1)
    return (*pieces, exact, totals, q_all, kv_all)


def plain_attend_back(count, blocks, rows, at, grads, q_all, kv_all, exact, totals):
    g_all = jnp.zeros((count, rows, grads[0].shape[1]), BF)
    for k in range(count):
        g_all = g_all.at[at[0] ^ k].set(grads[k])
    g_all = g_all.reshape(count * rows, -1)
    seen = plain_terms(at, count, blocks, rows)
    dq, parts = [], []
    for h, (query, grad, kept) in enumerate(zip(plain_heads(q_all), plain_heads(g_all), plain_heads(exact))):
        key = kv_all[:, :128] if h < 2 else kv_all[:, 256:]
        value = kv_all[:, 128:256] if h < 2 else kv_all[:, 256:]
        delta = jnp.sum(grad.astype(F32) * kept, axis=-1, keepdims=True)
        scores = dot_columns(query, key) * SCORE - totals[:, h : h + 1]
        weights = jnp.exp(jnp.where(seen, scores, NEVER))
        g_scores = (weights * (dot_columns(grad, value) - delta)).astype(BF)
        dq.append(dot(g_scores, key) * SCORE)
        parts.append((dot_rows(g_scores, query) * SCORE, dot_rows(weights.astype(BF), grad)))
    dq = jnp.concatenate([dq[0][:, :HD], dq[1][:, HD:], dq[2][:, :HD], jnp.zeros_like(dq[2][:, :HD])], 1)
    dq = dq.astype(BF).reshape(count, rows, -1)
    acc = jnp.concatenate([parts[0][0] + parts[1][0], parts[0][1] + parts[1][1], parts[2][0] + parts[2][1]], 1)
    acc = acc.reshape(count, blocks, rows, -1)
    dq_all, summed = dq.reshape(count * rows, -1), acc.reshape(-1, acc.shape[-1]).astype(BF)
    own = jnp.concatenate([acc[i, at[1]] for i in range(count)], 0)
    away = [acc[i, at[1] ^ j].astype(BF) for j in range(1, blocks) for i in range(count)]
    return (own, jnp.concatenate(away, 0), dq_all, summed)


def merge_body(at, dq, own, *refs):
    arrived, out = refs[:-1], refs[-1]
    total = own[...]
    for ref in arrived:
        total = total + ref[...].astype(F32)
    out[:, :256] = dq[...]
    out[:, 256:] = total.astype(BF)


def gelu_terms(hidden):
    root = 0.7978845608028654
    square = hidden * hidden
    bend = jnp.tanh(root * hidden * (1.0 + 0.044715 * square))
    half = 0.5 * (1.0 + bend)
    slope = half + 0.5 * hidden * (1.0 - bend * bend) * root * (1.0 + 3.0 * 0.044715 * square)
    return hidden * half, slope


def g_output(extras, rows):
    return jnp.concatenate([(RESIDUAL * ref[:rows, :].astype(F32)).astype(BF) for ref in extras], axis=0)


def split_rows(values, rows, mine, other):
    mine[:rows, :] = values[:rows]
    mine[rows:, :] = values[2 * rows : 3 * rows]
    other[:rows, :] = values[rows : 2 * rows]
    other[rows:, :] = values[3 * rows :]


def middle_body(parts, rows, at, attended, vectors, fc, fc_bias, out, *refs):
    tokens, extras = refs[:parts], refs[parts : 2 * parts]
    gn_mine, gn_other, mid_mine, normed, active, g_hidden, own, att_all, proj = refs[2 * parts :]
    zero = jnp.zeros((HD, proj.shape[1]), BF)
    half = rows // 2
    low = lax.broadcasted_iota(jnp.int32, (half, 128), 1) < HD
    for k in range(parts):
        weight = extras[k][rows:, :]
        owner = at[2] ^ k
        packed = jnp.concatenate([weight[:128], zero, weight[128:]], axis=0)
        proj[rows_at(owner, 256), :] = packed
    size = rows + half
    for j in range(parts):
        for k in range(parts):
            piece = attended[j, k * size : (k + 1) * size, :]
            pair = piece[rows:].astype(F32)
            upper = jnp.where(low, 0.0, pltpu.roll(pair, HD, 1)).astype(BF)
            lower = jnp.where(low, 0.0, pair).astype(BF)
            block = block_of(at, k, rows)
            att_all[block, j * 256 : j * 256 + 128] = piece[:rows]
            att_all[block, j * 256 + 128 : (j + 1) * 256] = jnp.concatenate([upper, lower], axis=0)
    own[...] = att_all[:, pl.ds(pl.multiple_of(at[2] * 256, 256), 256)]
    branch = dot(att_all[...], proj[...]) + vectors[4:5]
    for k in range(parts):
        part = slice(k * rows, (k + 1) * rows)
        value = tokens[k][:rows, :].astype(F32) + RESIDUAL * branch[part]
        if k % 2 == 0:
            mid_mine[(k // 2) * rows : (k // 2 + 1) * rows, :] = value
        unit, _ = normalize(value)
        normed[part, :] = (unit * vectors[2:3] + vectors[3:4]).astype(BF)
    hidden = dot(normed[...], fc[...]) + as_row(fc_bias)
    value, slope = gelu_terms(hidden)
    active[...] = value.astype(BF)
    g_hidden[...] = (dot_columns(g_output(extras, rows), out[...]) * slope).astype(BF)
    split_rows(dot_columns(g_hidden[...], fc[...]), rows, gn_mine, gn_other)


def fill_half(half, bit, kept, away, chunk):
    size = kept.shape[0] // half
    for i in range(half):
        into = slice(i * size, (i + 1) * size)
        kept[into, :] = chunk(bit * half + i)
        away[into, :] = chunk((1 - bit) * half + i).astype(BF)


def proj_grad(attended, g_branch):
    grad = dot_rows(attended[...], g_branch[...])
    return jnp.concatenate([grad[:128], grad[128 + HD :]], axis=0)


def proj_grad_body(rows, at, attended, g_branch, sums_in, grad, sums):
    grad[...] = proj_grad(attended, g_branch)
    sums[...] = sums_in[...]
    sums[4:5, :] = jnp.sum(g_branch[:rows, :].astype(F32), axis=0, keepdims=True)


def pack_wide(values, lanes):
    third = values.shape[0] // 3
    rest = values[:, lanes:]
    low = [rest[i * third : (i + 1) * third] for i in range(3)]
    low.append(jnp.zeros((third, lanes - 384), values.dtype))
    return jnp.concatenate([values[:, :lanes], jnp.concatenate(low, axis=1)], axis=0)


def out_partial_body(rows, at, active, out, mine, other):
    split_rows(dot(active[...], out[...]), rows, mine, other)


def out_weights_body(rows, step, at, active, sums_in, *refs):
    extras = refs[:-4]
    kept, away, sums, grad = refs[-4:]
    g_out = g_output(extras, rows)
    grad[...] = dot_rows(active[...], g_out)
    half = kept.shape[0]
    bit = (at[3] // step) % 2
    kept[...] = grad[rows_at(bit, half), :]
    away[...] = grad[rows_at(1 - bit, half), :].astype(BF)
    sums[...] = sums_in[...]
    sums[5:6, :] = jnp.sum(g_out[:rows].astype(F32), axis=0, keepdims=True)


def fc_weights_body(parts, half, step, at, normed, g_hidden, sums_in, kept, away, sums, grad):
    grad[...] = dot_rows(normed[...], g_hidden[...])
    size = grad.shape[0] // (parts * 2 * half)

    def chunk(i):
        blocks = [((at[2] ^ j) * 2 * half + i) * size for j in range(parts)]
        return jnp.concatenate([grad[pl.ds(pl.multiple_of(start, 8), size), :] for start in blocks], axis=0)

    fill_half(half, (at[3] // step) % 2, kept, away, chunk)
    sums[...] = sums_in[...]
    sums[6:7, :] = jnp.sum(g_hidden[...].astype(F32), axis=0, keepdims=True)


def plain_weights_body(rows, at, active, normed, g_hidden, sums_in, *refs):
    extras = refs[:-3]
    out_grad, fc_grad, sums = refs[-3:]
    g_out = g_output(extras, rows)
    out_grad[...] = dot_rows(active[...], g_out).astype(BF)
    fc_grad[...] = dot_rows(normed[...], g_hidden[...]).astype(BF)
    sums[...] = sums_in[...]
    sums[5:6, :] = jnp.sum(g_out[:rows].astype(F32), axis=0, keepdims=True)
    sums[6:7, :] = jnp.sum(g_hidden[...].astype(F32), axis=0, keepdims=True)


def second_norm_body(rows, at, chip_sum, arrived, mid, own_extra, x_extra, vectors, sums_in, g_branch, own_middle, sums):
    add = arrived[...].astype(F32)
    grad = chip_sum[...] + jnp.concatenate([add[rows:], add[:rows]], axis=0)
    unit, scale = normalize(mid[...])
    back = norm_back(grad, unit, scale, vectors[2:3])
    sums[...] = sums_in[...]
    sums[2:3, :] = jnp.sum(grad[:rows] * unit[:rows], axis=0, keepdims=True)
    sums[3:4, :] = jnp.sum(grad[:rows], axis=0, keepdims=True)
    g_own = back[:rows] + own_extra[:rows, :].astype(F32)
    own_middle[...] = g_own
    g_branch[:rows, :] = (RESIDUAL * g_own).astype(BF)
    g_branch[rows:, :] = (RESIDUAL * (back[rows:] + x_extra[:rows, :].astype(F32))).astype(BF)


def attended_grad_body(parts, rows, at, mine, other, proj, *refs):
    outs, (kept, g_all) = refs[:parts], refs[parts:]
    kept[:rows, :] = mine[:rows, :]
    kept[rows : 2 * rows, :] = other[:rows, :]
    kept[2 * rows : 3 * rows, :] = mine[rows:, :]
    kept[3 * rows :, :] = other[rows:, :]
    zero = jnp.zeros((HD, proj.shape[1]), BF)
    weight = jnp.concatenate([proj[:128, :], zero, proj[128:, :]], axis=0)
    g_all[...] = dot_columns(kept[...], weight).astype(BF)
    for k in range(parts):
        outs[k][...] = g_all[block_of(at, k, rows), :]


def merge_pieces_body(rows, at, dq, own, arrived, *outs):
    for k, out in enumerate(outs):
        part = rows_at(at[0] ^ k, rows)
        out[:, :256] = dq[part, :]
        out[:, 256:] = (own[part, :] + arrived[part, :].astype(F32)).astype(BF)


def first_grad_body(parts, rows, at, matrix, *refs):
    pieces, (mine, other, mixed) = refs[:-3], refs[-3:]
    for i in range(parts):
        if len(pieces) == 1:
            mixed[rows_at(at[2] ^ i, rows), :] = pieces[0][i * rows : (i + 1) * rows, :]
        else:
            mixed[block_of(at, i, rows), :] = pieces[i][...]
    split_rows(dot_columns(mixed[...], matrix[...]), rows, mine, other)


def attn_halves_body(parts, count, at, own, every, dq, dkv, proj, kept, away, sums, grad):
    grad[:, :256] = dot_rows(own[...], dq[...])
    grad[:, 256:] = dot_rows(every[...], dkv[...])
    owner_rows = grad.shape[0] // parts
    size = owner_rows // (2 * count)
    packed = size + size // 3
    start = 0
    for k in range(count):
        place = at[1] * count + (at[0] ^ k)
        other = (1 - at[1]) * count + (at[0] ^ k)
        for j in range(parts):
            base = (at[2] ^ j) * 2 * count
            kept[start : start + size, :] = grad[rows_at(base + place, size), :]
            away[start : start + size, :] = grad[rows_at(base + other, size), :].astype(BF)
            start += size
        kept[start : start + packed, :] = pack_wide(proj[rows_at(place, size), :], grad.shape[1])
        away[start : start + packed, :] = pack_wide(proj[rows_at(other, size), :], grad.shape[1]).astype(BF)
        start += packed
    sums[...] = jnp.zeros_like(sums)
    sums[0:1, :256] = jnp.sum(dq[...].astype(F32), axis=0, keepdims=True)
    sums[0:1, 256:] = jnp.sum(dkv[...].astype(F32), axis=0, keepdims=True)


def attn_pair_body(at, kept, arrived, *outs):
    size = outs[0].shape[0]
    for k, out in enumerate(outs):
        part = slice(k * size, (k + 1) * size)
        out[...] = (kept[part, :] + arrived[part, :].astype(F32)).astype(out.dtype)


def attn_fold_body(count, at, *refs):
    total = refs[0][...]
    for ref in refs[1:count]:
        total = total + ref[...].astype(F32)
    start = 0
    for out in refs[count:]:
        out[...] = total[start : start + out.shape[0]].astype(BF)
        start += out.shape[0]


def attn_place_body(parts, count, at, *refs):
    own, away, (out, proj, kept) = refs[:count], refs[count], refs[count + 1 :]
    features = proj.shape[1]
    width, lanes = features // parts, kept.shape[2]
    size = width // (2 * count)
    total = own[0].shape[0]
    for side in range(2):
        block = at[1] if side == 0 else 1 - at[1]
        for k in range(count):
            piece = own[k][...] if side == 0 else away[k * total : (k + 1) * total, :]
            piece = piece.astype(F32)
            rows = rows_at(block * count + (at[0] ^ k), size)
            for j in range(parts):
                kept[at[2] ^ j, rows, :] = piece[j * size : (j + 1) * size]
            start = parts * size
            proj[rows, :lanes] = piece[start : start + size]
            low = piece[start + size :]
            proj[rows, lanes:] = jnp.concatenate([low[:, i * 128 : (i + 1) * 128] for i in range(3)], axis=0)
    for g in range(parts):
        first = g * width
        out[:, first : first + width] = kept[g, :, :width]
        first += features
        out[:, first : first + width] = jnp.concatenate([kept[g, :, 256:384], kept[g, :, 512 : 512 + HD]], axis=1)
        first += features
        out[:, first : first + width] = jnp.concatenate([kept[g, :, 384:512], kept[g, :, 512 + HD :]], axis=1)


def attn_weights_body(parts, ways, at, own, every, dq, dkv, grads, sums):
    query = dot_rows(own[...], dq[...])
    pair = dot_rows(every[...], dkv[...])
    size = query.shape[0] // (parts * ways)
    for c in range(ways):
        for j in range(parts):
            at_row = (j * ways + c) * size
            grads[c * parts + j, :, :256] = query[at_row : at_row + size].astype(BF)
            grads[c * parts + j, :, 256:] = pair[at_row : at_row + size].astype(BF)
    sums[...] = jnp.zeros_like(sums)
    sums[0:1, :256] = jnp.sum(dq[...].astype(F32), axis=0, keepdims=True)
    sums[0:1, 256:] = jnp.sum(dkv[...].astype(F32), axis=0, keepdims=True)


def attn_sum_body(parts, ways, at, arrived, out):
    for j in range(parts):
        total = arrived[j].astype(F32)
        for c in range(1, ways):
            total = total + arrived[c * parts + j].astype(F32)
        total = total.astype(BF)
        for c in range(ways):
            out[c, j, :, :] = total


def attn_final_body(parts, ways, at, arrived, out):
    size = arrived.shape[2]
    width = size * ways
    features = out.shape[1] // 3
    for c in range(ways):
        rows = slice(c * size, (c + 1) * size)
        for g in range(parts):
            piece = arrived[c, g].astype(F32)
            first = g * width
            out[rows, first : first + width] = piece[:, :width]
            first += features
            out[rows, first : first + width] = jnp.concatenate([piece[:, 256:384], piece[:, 512 : 512 + HD]], axis=1)
            first += features
            out[rows, first : first + width] = jnp.concatenate([piece[:, 384:512], piece[:, 512 + HD :]], axis=1)


def first_norm_body(rows, at, own, core, arrived, tokens, own_middle, vectors, sums, attn, input_grad, shares):
    grad = own[:rows, :] + core[:rows, :] + arrived[...].astype(F32)
    unit, scale = normalize(tokens[...].astype(F32))
    back = norm_back(grad, unit, scale, vectors[0:1])
    input_grad[...] = (back + own_middle[...]).astype(BF)
    first = [jnp.sum(grad * unit, axis=0, keepdims=True), jnp.sum(grad, axis=0, keepdims=True)]
    whole = jnp.concatenate(first + [sums[2:6, :], jnp.zeros((2, grad.shape[1]), F32)], axis=0)
    parts = whole.shape[1] // HD // 3
    width = whole.shape[1] // parts
    part = sums.shape[1] // 4
    value = jnp.concatenate([attn[0:1, 384:512], attn[0:1, 512 + HD :]], axis=1)
    local = [sums[6:7, i * part : (i + 1) * part] for i in range(4)] + [attn[0:1, :width], value]
    local = jnp.concatenate(local + [jnp.zeros((2, width), F32)], axis=0)
    blank = jnp.zeros((8, 256 - width), F32)
    for j in range(parts):
        piece = jnp.concatenate([whole[:, j * width : (j + 1) * width], blank, local, blank], axis=1)
        for c in range(shares.shape[0] // parts):
            shares[c * parts + j, :, :] = piece


def vector_final_body(ways, parts, at, arrived, *outs):
    width, hidden = outs[0].shape[0], outs[8].shape[0]
    total, local = jnp.zeros((8, arrived.shape[2]), F32), jnp.zeros((8, arrived.shape[2]), F32)
    for i in range(ways * parts):
        total = total + arrived[i]
    for c in range(ways):
        local = local + arrived[c * parts + at[2]]
    for row in range(6):
        outs[row][...] = total[row : row + 1, :width].reshape(width)
    part = hidden // 4
    outs[8][...] = jnp.concatenate([local[i : i + 1, 256 : 256 + part] for i in range(4)], axis=1).reshape(hidden)
    outs[6][...] = local[4:5, 256 : 256 + width].reshape(width)
    outs[7][...] = local[5:6, 256 : 256 + width].reshape(width)


def halve_body(step, at, held, arrived, kept, away, total):
    total[...] = held[...] + arrived[...].astype(F32)
    half = kept.shape[0]
    bit = (at[3] // step) % 2
    kept[...] = total[pl.ds(pl.multiple_of(bit * half, 8), half), :]
    away[...] = total[pl.ds(pl.multiple_of((1 - bit) * half, 8), half), :].astype(BF)


def last_sum_body(at, held, arrived, *outs):
    total = held[...] + arrived[...].astype(F32)
    start = 0
    for out in outs:
        out[...] = total[start : start + out.shape[0]].astype(BF)
        start += out.shape[0]


def stack_rows_body(at, *refs):
    out = refs[-1]
    start = 0
    for ref in refs[:-1]:
        out[start : start + ref.shape[0], :] = ref[...]
        start += ref.shape[0]


def chunk_number(at, mask, steps):
    number = 0
    for step in steps:
        number = number * 2 + ((at[3] ^ mask) // step) % 2
    return number


def chunks_of(at, steps, refs):
    masks = [0]
    found = [(0, refs[0], 0)]
    for step, ref in zip(reversed(steps), refs[1:]):
        found += [(mask ^ step, ref, i) for i, mask in enumerate(masks)]
        masks = masks + [mask ^ step for mask in masks]
    size = refs[0].shape[0]
    for mask, ref, i in found:
        yield chunk_number(at, mask, steps), ref[i * size : (i + 1) * size, :].astype(F32)


def out_final_body(steps, at, *refs):
    for place, piece in chunks_of(at, steps, refs[:-1]):
        refs[-1][rows_at(place, piece.shape[0]), :] = piece


def fc_final_body(parts, steps, at, *refs):
    out = refs[-1]
    hidden = out.shape[1] // parts
    for place, piece in chunks_of(at, steps, refs[:-1]):
        size = piece.shape[0] // parts
        for j in range(parts):
            lanes = pl.ds(pl.multiple_of((at[2] ^ j) * hidden, 128), hidden)
            out[rows_at(place, size), lanes] = piece[j * size : (j + 1) * size]


class Values:
    pass


def shards(
    parts,
    ways,
    tokens,
    first_gain,
    first_bias,
    attn_weight,
    query_bias,
    value_bias,
    proj_weight,
    proj_bias,
    second_gain,
    second_bias,
    fc_weight,
    fc_bias,
    out_weight,
    out_bias,
    cotangent,
):
    rows, features = tokens.shape[1], tokens.shape[2]
    width = features // parts
    count = parts
    blocks = ways // count
    hidden = fc_weight.shape[1] // parts
    columns = 256 + 2 * width
    all_rows, half_rows = parts * rows, parts * rows // 2
    f = lax.axis_index("fsdp").astype(jnp.int32)
    c = lax.axis_index("ctx").astype(jnp.int32)
    at = jnp.stack([c // blocks, c % blocks, f, c])
    halved = ways == 8
    chunks, size = 4, width // 8
    packed = size + size // 3
    small_blocks = blocks * count * rows <= 1024
    last = []
    v = Values()

    def run(body, outs, *args, mib=16, scratch=()):
        task = v.task
        held = [] if task in v.free else last
        hooked = jax.tree.leaves(v.hooks[task]()) if task in v.hooks else []
        made = call(
            body,
            task.__name__,
            outs,
            at,
            *args,
            scratch=scratch,
            after=[*held, *hooked],
            us=v.costs.get(task, 1.0),
            mib=mib,
        )
        if task not in v.free:
            last[:] = [made[-1]]
        return made

    def over_fsdp(value, k):
        return lax.ppermute(value, "fsdp", [(i, i ^ k) for i in range(parts)])

    def over_ctx(value, k):
        return lax.ppermute(value, "ctx", [(i, i ^ k) for i in range(ways)])

    def spread(value):
        across = over_fsdp(value, 2)
        return [value, over_fsdp(value, 1), across, over_fsdp(across, 1)]

    def turn_fsdp(pieces):
        return [pieces[0]] + [over_fsdp(pieces[k], k) for k in range(1, parts)]

    def turn_ctx(pieces):
        return [pieces[0]] + [over_ctx(pieces[k], k * blocks) for k in range(1, count)]

    def halve(kept, arrived, step):
        half, lanes = kept.shape[0] // 2, kept.shape[1]
        outs = [shape((half, lanes), F32), shape((half, lanes), BF)]
        return run(partial(halve_body, step), outs, kept, arrived, scratch=[pltpu.VMEM((2 * half, lanes), F32)])

    def last_sum(kept, arrived, cuts):
        return run(last_sum_body, [shape((cut, kept.shape[1]), BF) for cut in cuts], kept, arrived)

    def stacked(pieces):
        total = sum(piece.shape[0] for piece in pieces)
        return run(stack_rows_body, [shape((total, pieces[0].shape[1]), BF)], *pieces)[0]

    v.sums = jnp.zeros((8, features), F32)

    def attn_columns():
        outs = [shape((width, columns), BF)] * parts
        v.attn_pieces = turn_fsdp(run(partial(attn_columns_body, parts), outs, attn_weight))
        v.attn_core = [v.attn_pieces[1]]

    def token_message():
        args = (tokens[0], first_gain, first_bias, second_gain, second_bias, proj_bias, out_bias)
        v.tokens = spread(run(token_message_body, [shape((rows + 8, features), BF)], *args)[0])

    def fc_columns():
        outs = [shape((width, hidden), BF)] * parts
        v.fc_columns = turn_fsdp(run(fc_columns_body, outs, fc_weight))
        v.fc_core = [v.fc_columns[1]]

    def mixed():
        made = run(
            partial(mixed_body, parts, count),
            [shape((all_rows, features), BF), shape((features, columns), BF), shape((8, features), F32)]
            + [shape((5 * rows // 2, 256), BF)] * count
            + [shape((rows, 384), BF)] * count,
            query_bias,
            value_bias,
            *v.tokens,
            *v.attn_pieces,
            scratch=[pltpu.VMEM((all_rows, columns), BF)],
        )
        v.attn_matrix, v.vectors = made[1:3]
        v.pairs = turn_ctx(made[3 + count :])
        v.queries = turn_ctx(made[3 : 3 + count])

    def stack_pairs():
        joined = stacked(v.pairs)
        v.partners = [over_ctx(joined, j) for j in range(1, blocks)]

    def join_fc():
        v.fc_matrix = run(join_body, [shape((features, hidden), BF)], *v.fc_columns)[0]

    def stack_extra():
        v.extra = spread(stacked([cotangent[0], proj_weight]))
        v.extra_across = [v.extra[2]]

    def attend():
        kept = run(
            partial(attend_body, count, blocks, rows),
            [shape((rows + rows // 2, 128), BF)] * count
            + [
                shape((count * rows, 256), F32),
                shape((count * rows, 128), F32),
                shape((count * rows, 256), BF),
                shape((count * blocks * rows, 384), BF),
            ],
            *v.queries,
            *v.pairs,
            *v.partners,
        )
        v.att_pieces, v.state = turn_ctx(kept[:count]), kept[count:]

    def plain_front():
        kept = plain_attend(count, blocks, rows, at, v.queries, v.pairs, v.partners)
        v.att_pieces, v.state = turn_ctx(kept[:count]), kept[count:]

    def normed_stack():
        outs = [shape((count * rows, features // 2), BF)]
        own = run(partial(normed_stack_body, rows), outs, *v.queries)[0]
        v.normed_across = [over_ctx(own, j) for j in range(1, blocks)]
        v.normed_sides = [own] + v.normed_across

    def middle():
        attended_all = lax.all_gather(jnp.concatenate(v.att_pieces, 0), "fsdp")
        gn_mine, gn_other, v.mid_mine, v.normed_two, v.active, v.g_hidden, v.attended = run(
            partial(middle_body, parts, rows),
            [shape((half_rows, features), F32)] * 3
            + [shape((all_rows, features), BF), shape((all_rows, hidden), BF), shape((all_rows, hidden), BF)]
            + [shape((all_rows, 256), BF)],
            attended_all,
            v.vectors,
            v.fc_matrix,
            fc_bias,
            out_weight,
            *v.tokens,
            *v.extra,
            scratch=[pltpu.VMEM((all_rows, parts * 256), BF), pltpu.VMEM((parts * 256, features), BF)],
            mib=24,
        )
        v.chip_sum = gn_mine + over_fsdp(gn_other, 1)
        v.chip_low = v.chip_sum.astype(BF)
        v.arrived = over_fsdp(v.chip_low, 2)


    def place():
        sides = v.normed_sides + [over_fsdp(side, 1) for side in v.normed_sides]
        v.every, v.own_rows = run(
            partial(normed_place_body, count, blocks, rows),
            [shape((count * blocks * rows, features), BF), shape((count * rows, features), BF)],
            *sides,
        )

    def fc_weights():
        v.fc_kept, away, v.sums = run(
            partial(fc_weights_body, parts, chunks, FC_STEPS[0]),
            [shape((features // 2, hidden), F32), shape((features // 2, hidden), BF), shape((8, features), F32)],
            v.normed_two,
            v.g_hidden,
            v.sums,
            scratch=[pltpu.VMEM((features, hidden), F32)],
        )
        v.fc_in = over_ctx(away, FC_STEPS[0])

    def out_weights():
        v.out_kept, away, v.sums = run(
            partial(out_weights_body, rows, OUT_STEPS[0]),
            [shape((hidden // 2, features), F32), shape((hidden // 2, features), BF), shape((8, features), F32)],
            v.active,
            v.sums,
            *v.extra,
            scratch=[pltpu.VMEM((hidden, features), F32)],
        )
        v.out_in = over_ctx(away, OUT_STEPS[0])

    def both_weights():
        v.out_grad, v.fc_grad, v.sums = run(
            partial(plain_weights_body, rows),
            [shape((hidden, features), BF), shape((features, hidden), BF), shape((8, features), F32)],
            v.active,
            v.normed_two,
            v.g_hidden,
            v.sums,
            *v.extra,
        )

    def second_norm():
        v.g_branch, v.own_middle, v.sums = run(
            partial(second_norm_body, rows),
            [shape((half_rows, features), BF), shape((rows, features), F32), shape((8, features), F32)],
            v.chip_sum,
            v.arrived,
            v.mid_mine,
            v.extra[0],
            v.extra[2],
            v.vectors,
            v.sums,
        )

    def attended_grad():
        grads = run(
            partial(attended_grad_body, parts, rows),
            [shape((rows, 256), BF)] * parts + [shape((all_rows, features), BF)],
            v.g_branch,
            over_fsdp(v.g_branch, 1),
            proj_weight,
            scratch=[pltpu.VMEM((all_rows, 256), BF)],
        )
        v.g_pieces, v.g_branch_all = turn_ctx(grads[:parts]), grads[parts]

    def proj_weights():
        v.proj, v.sums = run(
            partial(proj_grad_body, rows),
            [shape((width, features), F32), shape((8, features), F32)],
            v.attended,
            v.g_branch_all,
            v.sums,
        )

    def fc_one():
        v.fc_kept, away = halve(v.fc_kept, v.fc_in, FC_STEPS[1])
        v.fc_in = over_ctx(away, FC_STEPS[1])

    def fc_two():
        v.fc_kept, away = halve(v.fc_kept, v.fc_in, FC_STEPS[2])
        v.fc_in = over_ctx(away, FC_STEPS[2])

    def fc_sum():
        v.fc_parts = turn_fsdp(last_sum(v.fc_kept, v.fc_in, [size] * parts))

    def fc_turned():
        part = stacked(v.fc_parts)
        v.fc_pieces = [part, over_ctx(part, FC_STEPS[2])]

    def fc_double():
        v.fc_pieces.append(over_ctx(stacked(v.fc_pieces), FC_STEPS[1]))

    def fc_fourfold():
        v.fc_pieces.append(over_ctx(stacked(v.fc_pieces), FC_STEPS[0]))

    def fc_final():
        outs = [shape((width, parts * hidden), F32)]
        v.fc_weight_grad = run(partial(fc_final_body, parts, FC_STEPS), outs, *v.fc_pieces)[0]

    def out_one():
        v.out_kept, away = halve(v.out_kept, v.out_in, OUT_STEPS[1])
        v.out_in = over_ctx(away, OUT_STEPS[1])

    def out_two():
        v.out_kept, away = halve(v.out_kept, v.out_in, OUT_STEPS[2])
        v.out_in = over_ctx(away, OUT_STEPS[2])

    def out_sum():
        part = last_sum(v.out_kept, v.out_in, [hidden // 8])[0]
        v.out_pieces = [part, over_ctx(part, OUT_STEPS[2])]

    def out_double():
        v.out_pieces.append(over_ctx(stacked(v.out_pieces), OUT_STEPS[1]))

    def out_fourfold():
        v.out_pieces.append(over_ctx(stacked(v.out_pieces), OUT_STEPS[0]))

    def out_final():
        outs = [shape((hidden, features), F32)]
        v.out_weight_grad = run(partial(out_final_body, OUT_STEPS), outs, *v.out_pieces)[0]

    def attend_back():
        v.own, away, v.dq, v.dkv = run(
            partial(attend_back_body, count, blocks, rows),
            [
                shape((count * rows, 384), F32),
                shape(((blocks - 1) * count * rows, 384), BF),
                shape((count * rows, 256), BF),
                shape((count * blocks * rows, 384), BF),
            ],
            *v.g_pieces,
            v.state[2],
            v.state[3],
            *v.state[:2],
            scratch=[pltpu.VMEM((count * rows, 256), BF), pltpu.VMEM((count * blocks * rows, 384), F32)],
        )
        v.from_partners = [over_ctx(away, 1)]

    def plain_back():
        v.own, away, v.dq, v.dkv = plain_attend_back(
            count, blocks, rows, at, v.g_pieces, v.state[2], v.state[3], *v.state[:2]
        )
        stack = count * rows
        v.from_partners = [over_ctx(away[(j - 1) * stack : j * stack], j) for j in range(1, blocks)]

    def attn_weights():
        outs = [shape((count * (parts * size + packed), columns), kind) for kind in (F32, BF)]
        v.attn_kept, away, v.sums_attn = run(
            partial(attn_halves_body, parts, count),
            outs + [shape((8, columns), F32)],
            v.own_rows,
            v.every,
            v.dq,
            v.dkv,
            v.proj,
            scratch=[pltpu.VMEM((features, columns), F32)],
        )
        v.attn_in = over_ctx(away, 1)

    def attn_pair():
        outs = [shape((parts * size + packed, columns), kind) for kind in (F32, BF, BF, BF)]
        v.attn_sent = turn_ctx(run(attn_pair_body, outs, v.attn_kept, v.attn_in))

    def attn_fold():
        outs = [shape((size, columns), BF)] * parts + [shape((packed, columns), BF)]
        *attn_parts, v.proj = run(partial(attn_fold_body, count), outs, *v.attn_sent)
        v.attn_parts = turn_fsdp(attn_parts)

    def attn_turned():
        v.attn_pieces = turn_ctx([stacked([*v.attn_parts, v.proj])] * count)

    def attn_fourfold():
        v.attn_pieces.append(over_ctx(stacked(v.attn_pieces), 1))

    def attn_final():
        outs = [shape((width, 3 * features), F32), shape((width, features), F32)]
        v.attn_weight_grad, v.proj_weight_grad = run(
            partial(attn_place_body, parts, count),
            outs,
            *v.attn_pieces,
            scratch=[pltpu.VMEM((parts, width, columns), F32)],
        )

    def plain_attn_weights():
        attn_grads, v.sums_attn = run(
            partial(attn_weights_body, parts, ways),
            [shape((parts * ways, width // ways, columns), BF), shape((8, columns), F32)],
            v.own_rows,
            v.every,
            v.dq,
            v.dkv,
        )
        attn_in = lax.all_to_all(attn_grads, ("ctx", "fsdp"), split_axis=0, concat_axis=0, tiled=True)
        outs = [shape((ways, parts, width // ways, columns), BF)]
        attn_sum = run(partial(attn_sum_body, parts, ways), outs, attn_in)[0]
        attn_all = lax.all_to_all(attn_sum, "ctx", split_axis=0, concat_axis=0, tiled=True)
        outs = [shape((width, 3 * features), F32)]
        v.attn_weight_grad = run(partial(attn_final_body, parts, ways), outs, attn_all)[0]

    def merge():
        outs = [shape((count * rows, columns), BF)]
        if MERGE_PERMUTES and halved:
            outs = [shape((rows, columns), BF)] * count
            pieces = run(partial(merge_pieces_body, rows), outs, v.dq, v.own, *v.from_partners)
            v.g_mixed = turn_ctx(pieces)
            return
        made = run(merge_body, outs, v.dq, v.own, *v.from_partners)[0]
        groups = [[i * blocks + j for i in range(count)] for j in range(blocks)]
        v.g_mixed = lax.all_to_all(made, "ctx", split_axis=0, concat_axis=0, tiled=True, axis_index_groups=groups)

    def out_partial():
        outs = [shape((half_rows, features), F32)] * 2
        mine, other = run(partial(out_partial_body, rows), outs, v.active, out_weight)
        core = over_fsdp(other, 1)
        across = over_fsdp((mine[rows:] + core[rows:]).astype(BF), 2)
        output = mine[:rows] + core[:rows] + across.astype(F32) + v.vectors[5:6]
        v.block_out = (v.mid_mine[:rows] + RESIDUAL * output).astype(BF)

    def first_grad():
        mine, other = run(
            partial(first_grad_body, parts, rows),
            [shape((half_rows, features), F32)] * 2,
            v.attn_matrix,
            *(v.g_mixed if MERGE_PERMUTES and halved else [v.g_mixed]),
            scratch=[pltpu.VMEM((all_rows, columns), BF)],
        )
        arrived = over_fsdp(other, 1)
        v.first_own = (mine, arrived)
        v.first_in = over_fsdp((mine[rows:] + arrived[rows:]).astype(BF), 2)

    def first_norm():
        v.input_grad, shares = run(
            partial(first_norm_body, rows),
            [shape((rows, features), BF), shape((parts * ways, 8, 512), F32)],
            *v.first_own,
            v.first_in,
            tokens[0],
            v.own_middle,
            v.vectors,
            v.sums,
            v.sums_attn,
        )
        v.shares = lax.all_to_all(shares, ("ctx", "fsdp"), split_axis=0, concat_axis=0, tiled=True)

    def vector_final():
        outs = [shape((width,), F32)] * 8 + [shape((hidden,), F32)]
        v.vector_grads = run(partial(vector_final_body, ways, parts), outs, v.shares)

    def gather_rest():
        def over_all(value):
            part = lax.psum_scatter(value, "ctx", scatter_dimension=1, tiled=True)
            return lax.all_gather(part, "ctx", axis=1, tiled=True)

        v.out_weight_grad = over_all(v.out_grad).astype(F32)
        v.proj_weight_grad = over_all(v.proj.astype(BF)).astype(F32)
        fc_grad = over_all(v.fc_grad).reshape(parts, width, hidden)
        fc_grad = lax.all_to_all(fc_grad, "fsdp", split_axis=0, concat_axis=0)
        v.fc_weight_grad = fc_grad.transpose(1, 0, 2).reshape(width, parts * hidden).astype(F32)

    v.free = {
        attn_pair, fc_final, fc_fourfold, fc_weights, out_double, out_partial, vector_final,
    }
    v.hooks = {
        attend: lambda: [v.extra_across],
        fc_columns: lambda: [v.attn_core],
        fc_weights: lambda: [v.chip_low],
        middle: lambda: [v.normed_across],
        mixed: lambda: [v.fc_core],
        out_weights: lambda: [v.chip_low],
        place: lambda: [v.chip_low],
    }
    v.costs = {merge: 1.0, out_sum: 1000000.0}
    front = (attn_columns, token_message, fc_columns, mixed, stack_pairs, join_fc, stack_extra)
    if halved:
        order = (
            attn_columns, token_message, fc_columns, mixed, stack_pairs, join_fc, stack_extra, attend, normed_stack,
            middle, place, fc_weights, out_weights, second_norm, attended_grad, fc_one, proj_weights, out_one,
            attend_back, attn_weights, fc_two, out_two, fc_sum, merge, first_grad, attn_pair, fc_turned, out_sum,
            attn_fold, out_double, first_norm, fc_double, fc_fourfold, out_partial, out_fourfold, attn_turned,
            out_final, attn_fourfold, fc_final, vector_final, attn_final,
        )
    else:
        order = (*front, plain_front, normed_stack, middle, place, both_weights, second_norm, attended_grad)
        order += (proj_weights, plain_back, plain_attn_weights, merge, first_grad, out_partial, first_norm)
        order += (vector_final, gather_rest)
    for task in order:
        v.task = task
        task()
    first_gain_grad, first_bias_grad, second_gain_grad, second_bias_grad = v.vector_grads[:4]
    proj_bias_grad, out_bias_grad, query_bias_grad, value_bias_grad, fc_bias_grad = v.vector_grads[4:]
    return (
        v.block_out[None],
        v.input_grad[None],
        first_gain_grad,
        first_bias_grad,
        v.attn_weight_grad,
        query_bias_grad,
        value_bias_grad,
        v.proj_weight_grad,
        proj_bias_grad,
        second_gain_grad,
        second_bias_grad,
        v.fc_weight_grad,
        fc_bias_grad,
        v.out_weight_grad,
        out_bias_grad,
    )


def solution(mesh):
    rows, row, matrix = P("fsdp", "ctx", None), P("fsdp"), P("fsdp", None)
    return jax.shard_map(
        partial(shards, mesh.shape["fsdp"], mesh.shape["ctx"]),
        mesh=mesh,
        in_specs=(
            rows, row, row, matrix, row, row, matrix, row, row, row, matrix, row, matrix, row, rows,
        ),
        out_specs=(
            rows, rows, row, row, matrix, row, row, matrix, row, row, row, matrix, row, matrix, row,
        ),
        check_vma=False,
    )
```

```python
from functools import partial

import jax
import jax.numpy as jnp
from jax import lax
from jax.experimental import pallas as pl
from jax.experimental.pallas import tpu as pltpu
from jax.sharding import PartitionSpec as P

HD = 64
LAYERS = 12
EPSILON = 1e-05
BF = jnp.bfloat16
F32 = jnp.float32
RESIDUAL = LAYERS ** (-0.5)
SCORE = HD ** (-0.5)
NEVER = -1e30
OUT_STEPS, FC_STEPS = (1, 2, 4), (2, 1, 4)
MERGE_PERMUTES = True


def shape(dims, kind):
    return jax.ShapeDtypeStruct(dims, kind)


def call(body, name, outs, *args, scratch=(), after=(), us=1.0, mib=16):
    vmem = pl.BlockSpec(memory_space=pltpu.VMEM)
    smem = pl.BlockSpec(memory_space=pltpu.SMEM)
    held = pl.BlockSpec(memory_space=pl.ANY)
    count, waits = len(args), len(after)

    def run(*refs):
        body(*refs[:count], *refs[count + waits :])

    return pl.pallas_call(
        run,
        name=name,
        out_shape=outs,
        in_specs=[smem] + [vmem] * (count - 1) + [held] * waits,
        out_specs=[vmem] * len(outs),
        scratch_shapes=list(scratch),
        cost_estimate=pl.CostEstimate(flops=int(us * 1e3), transcendentals=0, bytes_accessed=int(us * 1e3)),
        compiler_params=pltpu.CompilerParams(vmem_limit_bytes=mib * 1024 * 1024),
    )(*args, *after)


def rows_at(index, size):
    return pl.ds(pl.multiple_of(index * size, size), size)


def dot(first, second):
    return jnp.dot(first, second, preferred_element_type=F32)


def dot_rows(first, second):
    return lax.dot_general(first, second, (((0,), (0,)), ((), ())), preferred_element_type=F32)


def dot_columns(first, second):
    return lax.dot_general(first, second, (((1,), (1,)), ((), ())), preferred_element_type=F32)


def normalize(values):
    center = jnp.mean(values, axis=-1, keepdims=True)
    centered = values - center
    spread = jnp.mean(centered * centered, axis=-1, keepdims=True)
    scale = lax.rsqrt(spread + EPSILON)
    return centered * scale, scale


def norm_back(grad, unit, scale, gain):
    inner = grad * gain
    mean_inner = jnp.mean(inner, axis=-1, keepdims=True)
    mean_along = jnp.mean(inner * unit, axis=-1, keepdims=True)
    return scale * (inner - mean_inner - unit * mean_along)


def join(at, pieces, whole):
    size = pieces[0].shape[0]
    for k, piece in enumerate(pieces):
        whole[rows_at(at[2] ^ k, size), :] = piece[...]


def as_row(ref):
    return ref[...].astype(F32).reshape(1, ref.shape[0])


def attn_columns_body(parts, at, attn, *pieces):
    features = attn.shape[1] // 3
    width = features // parts
    for owner in range(parts):

        @pl.when(at[2] == owner)
        def _():
            for k in range(parts):
                first = (owner ^ k) * width
                piece = pieces[k]
                piece[:, :width] = attn[:, first : first + width]
                piece[:, width:256] = jnp.zeros((width, 256 - width), BF)
                key = attn[:, features + first : features + first + width]
                value = attn[:, 2 * features + first : 2 * features + first + width]
                piece[:, 256:384] = key[:, :128]
                piece[:, 384:512] = value[:, :128]
                piece[:, 512 : 512 + HD] = key[:, 128:]
                piece[:, 512 + HD :] = value[:, 128:]


def token_message_body(at, tokens, *refs):
    vectors, out = refs[:-1], refs[-1]
    rows, width = tokens.shape[0], vectors[0].shape[0]
    out[:rows, :] = tokens[...]
    small = jnp.concatenate([as_row(ref) for ref in vectors] + [jnp.zeros((8 - len(vectors), width), F32)], axis=0)
    rest = jnp.zeros((8, tokens.shape[1] - width), F32)
    out[rows:, :] = jnp.concatenate([small, rest], axis=1).astype(BF)


def fc_columns_body(at, fc, *pieces):
    for k, piece in enumerate(pieces):
        hidden = piece.shape[1]
        piece[...] = fc[:, pl.ds(pl.multiple_of((at[2] ^ k) * hidden, 128), hidden)]


def join_body(at, *refs):
    join(at, refs[:-1], refs[-1])


def block_of(at, k, rows):
    return rows_at(at[2] ^ at[0] ^ k, rows)


def mixed_body(parts, count, at, query_bias, value_bias, *refs):
    tokens, weights = refs[:parts], refs[parts : 2 * parts]
    normed, matrix, vectors, *outs, kept = refs[2 * parts :]
    rows = tokens[0].shape[0] - 8
    join(at, weights, matrix)
    columns = matrix.shape[1]
    width = weights[0].shape[0]
    for owner in range(parts):

        @pl.when(at[2] == owner)
        def _():
            for k in range(parts):
                lanes = slice((owner ^ k) * width, ((owner ^ k) + 1) * width)
                vectors[:, lanes] = tokens[k][rows:, :width].astype(F32)

    small = vectors[...]
    for k in range(parts):
        unit, _ = normalize(tokens[k][:rows, :].astype(F32))
        normed[k * rows : (k + 1) * rows, :] = (unit * small[0:1] + small[1:2]).astype(BF)
    query, value = as_row(query_bias), as_row(value_bias)
    none = jnp.zeros((1, 128), F32)
    bias = [query, none[:, :HD], none, value[:, :128], none[:, :HD], value[:, 128:]]
    bias = jnp.concatenate(bias, axis=1)
    kept[...] = (dot(normed[...], matrix[...]) + bias).astype(BF)
    half = rows // 2
    third = normed.shape[1] // 6
    first = (at[2] % 2) * 3 * third
    for k in range(count):
        block = block_of(at, k, rows)
        outs[k][:rows, :] = kept[block, :256]
        part = normed[block, pl.ds(pl.multiple_of(first, 128), 3 * third)]
        outs[k][rows : 2 * rows, :] = part[:, : 2 * third]
        outs[k][2 * rows :, :third] = part[:half, 2 * third :]
        outs[k][2 * rows :, third:] = part[half:, 2 * third :]
        outs[count + k][...] = kept[block, 256:]


def normed_stack_body(rows, at, *refs):
    half = rows // 2
    out = refs[-1]
    third = out.shape[1] // 3
    for k, ref in enumerate(refs[:-1]):
        part = slice(k * rows, (k + 1) * rows)
        out[part, : 2 * third] = ref[rows : 2 * rows, :]
        out[k * rows : k * rows + half, 2 * third :] = ref[2 * rows :, :third]
        out[k * rows + half : (k + 1) * rows, 2 * third :] = ref[2 * rows :, third:]


def normed_place_body(count, blocks, rows, at, *refs):
    sides, (every, own) = refs[:-2], refs[-2:]
    lanes = sides[0].shape[1]
    core = at[2] % 2
    for side in range(2):
        part = pl.ds(pl.multiple_of((core if side == 0 else 1 - core) * lanes, 128), lanes)
        for j in range(blocks):
            ref = sides[side * blocks + j]
            for k in range(count):
                row = at[0] ^ k
                piece = ref[k * rows : (k + 1) * rows, :]
                every[rows_at(row * blocks + (at[1] ^ j), rows), part] = piece
                if j == 0:
                    own[rows_at(row, rows), part] = piece


def place(at, count, blocks, rows, queries, pairs, partners, q_all, kv_all):
    for k in range(count):
        row = at[0] ^ k
        q_all[rows_at(row, rows), :] = queries[k][:rows, :]
        kv_all[rows_at(row * blocks + at[1], rows), :] = pairs[k][...]
        for j, partner in enumerate(partners):
            side = row * blocks + (at[1] ^ (j + 1))
            kv_all[rows_at(side, rows), :] = partner[k * rows : (k + 1) * rows, :]


def head_views(tile_one, tile_two, scale):
    low = lax.broadcasted_iota(jnp.int32, tile_one.shape, 1) < HD
    zero = jnp.zeros_like(tile_one)
    tile_one = tile_one * scale if scale is not None else tile_one
    tile_two = tile_two * scale if scale is not None else tile_two
    return (jnp.where(low, tile_one, zero), jnp.where(low, zero, tile_one), tile_two)


def visible_keys(at, i, blocks, rows, keys):
    query = (i * blocks + at[1]) * rows + lax.broadcasted_iota(jnp.int32, (rows, keys), 0)
    return lax.broadcasted_iota(jnp.int32, (rows, keys), 1) <= query


def attend_body(count, blocks, rows, at, *refs):
    queries, pairs = refs[:count], refs[count : 2 * count]
    partners = refs[2 * count : 2 * count + blocks - 1]
    outs = refs[2 * count + blocks - 1 :]
    pieces, (exact, totals, q_all, kv_all) = outs[:count], outs[count:]
    place(at, count, blocks, rows, queries, pairs, partners, q_all, kv_all)
    low = lax.broadcasted_iota(jnp.int32, (rows, 128), 1) < HD
    for i in range(count):
        keys = (i + 1) * blocks * rows
        mine = slice(i * rows, (i + 1) * rows)
        heads = head_views(q_all[mine, :128], q_all[mine, 128:], SCORE)
        seen = visible_keys(at, i, blocks, rows, keys)
        found = []
        for h, query in enumerate(heads):
            key_cols = slice(0, 128) if h < 2 else slice(256, 384)
            value_cols = slice(128, 256) if h < 2 else slice(256, 384)
            scores = jnp.where(seen, dot_columns(query, kv_all[:keys, key_cols]), NEVER)
            highest = jnp.max(scores, axis=-1, keepdims=True)
            weights = jnp.exp(scores - highest)
            total = jnp.sum(weights, axis=-1, keepdims=True)
            totals[mine, h : h + 1] = highest + jnp.log(total)
            weights = (weights * (1.0 / total)).astype(BF)
            found.append(dot(weights, kv_all[:keys, value_cols]))
        exact[mine, :128] = jnp.where(low, found[0], found[1])
        exact[mine, 128:] = jnp.where(low, 0.0, found[2])
    half = rows // 2
    for k in range(count):
        block = rows_at(at[0] ^ k, rows)
        pieces[k][:rows, :] = exact[block, :128].astype(BF)
        last = exact[block, 128:]
        pair = jnp.where(low[:half], pltpu.roll(last[:half], HD, 1), last[half:])
        pieces[k][rows:, :] = pair.astype(BF)


def attend_back_body(count, blocks, rows, at, *refs):
    grads, (q_all, kv_all, exact, totals) = refs[:count], refs[count : count + 4]
    outs = refs[count + 4 :]
    own, away, dq_all, summed, g_all, acc = outs
    for k in range(count):
        g_all[rows_at(at[0] ^ k, rows), :] = grads[k][...]
    acc[...] = jnp.zeros_like(acc)
    low = lax.broadcasted_iota(jnp.int32, (rows, 128), 1) < HD
    for i in range(count):
        keys = (i + 1) * blocks * rows
        mine = slice(i * rows, (i + 1) * rows)
        q_heads = head_views(q_all[mine, :128], q_all[mine, 128:], SCORE)
        g_heads = head_views(g_all[mine, :128], g_all[mine, 128:], None)
        seen = visible_keys(at, i, blocks, rows, keys)
        found = []
        for h in range(3):
            key_cols = slice(0, 128) if h < 2 else slice(256, 384)
            value_cols = slice(128, 256) if h < 2 else slice(256, 384)
            kept = exact[mine, :128] if h < 2 else exact[mine, 128:]
            delta = jnp.sum(g_heads[h].astype(F32) * kept, axis=-1, keepdims=True)
            scores = dot_columns(q_heads[h], kv_all[:keys, key_cols]) - totals[mine, h : h + 1]
            weights = jnp.exp(jnp.where(seen, scores, NEVER))
            g_weights = dot_columns(g_heads[h], kv_all[:keys, value_cols])
            g_scores = (weights * (g_weights - delta)).astype(BF)
            found.append(dot(g_scores, kv_all[:keys, key_cols]))
            acc[:keys, key_cols] += dot_rows(g_scores, q_heads[h])
            acc[:keys, value_cols] += dot_rows(weights.astype(BF), g_heads[h])
        dq_all[mine, :128] = (jnp.where(low, found[0], found[1]) * SCORE).astype(BF)
        dq_all[mine, 128:] = (jnp.where(low, found[2], 0.0) * SCORE).astype(BF)
    summed[...] = acc[...].astype(BF)
    for i in range(count):
        into = slice(i * rows, (i + 1) * rows)
        own[into, :] = acc[rows_at(i * blocks + at[1], rows), :]
        for j in range(1, blocks):
            from_rows = slice(((j - 1) * count + i) * rows, ((j - 1) * count + i + 1) * rows)
            away[from_rows, :] = acc[rows_at(i * blocks + (at[1] ^ j), rows), :].astype(BF)


def plain_heads(values):
    zero = jnp.zeros_like(values[:, :HD])
    first = jnp.concatenate([values[:, :HD], zero], 1)
    second = jnp.concatenate([zero, values[:, HD:128]], 1)
    return (first, second, values[:, 128:])


def plain_terms(at, count, blocks, rows):
    q_pos = (jnp.arange(count)[:, None] * blocks + at[1]) * rows + jnp.arange(rows)[None]
    k_pos = jnp.arange(count * blocks * rows)
    return k_pos[None] <= q_pos.reshape(-1)[:, None]


def plain_attend(count, blocks, rows, at, queries, pairs, partners):
    width = pairs[0].shape[1]
    q_all = jnp.zeros((count, rows, queries[0].shape[1]), BF)
    kv_all = jnp.zeros((count, blocks, rows, width), BF)
    for k in range(count):
        row = at[0] ^ k
        q_all = q_all.at[row].set(queries[k][:rows])
        kv_all = kv_all.at[row, at[1]].set(pairs[k])
        for j, partner in enumerate(partners):
            kv_all = kv_all.at[row, at[1] ^ (j + 1)].set(partner[k * rows : (k + 1) * rows])
    q_all, kv_all = q_all.reshape(count * rows, -1), kv_all.reshape(-1, width)
    seen = plain_terms(at, count, blocks, rows)
    found, totals = [], []
    for h, query in enumerate(plain_heads(q_all)):
        key = kv_all[:, :128] if h < 2 else kv_all[:, 256:]
        value = kv_all[:, 128:256] if h < 2 else kv_all[:, 256:]
        scores = jnp.where(seen, dot_columns(query, key) * SCORE, NEVER)
        total = jax.nn.logsumexp(scores, axis=-1, keepdims=True)
        found.append(dot(jnp.exp(scores - total).astype(BF), value))
        totals.append(total)
    exact = jnp.concatenate([found[0][:, :HD], found[1][:, HD:], jnp.zeros_like(found[2][:, :HD]), found[2][:, HD:]], 1)
    grid = exact.astype(BF).reshape(count, rows, -1)
    half = rows // 2
    pair = jnp.concatenate([grid[:, :half, 128 + HD :], grid[:, half:, 128 + HD :]], 2)
    grid = jnp.concatenate([grid[:, :, :128], pair], 1)
    pieces = [grid[at[0] ^ k] for k in range(count)]
    totals = jnp.concatenate(totals + [jnp.zeros((count * rows, 125), F32)], 1)
    return (*pieces, exact, totals, q_all, kv_all)


def plain_attend_back(count, blocks, rows, at, grads, q_all, kv_all, exact, totals):
    g_all = jnp.zeros((count, rows, grads[0].shape[1]), BF)
    for k in range(count):
        g_all = g_all.at[at[0] ^ k].set(grads[k])
    g_all = g_all.reshape(count * rows, -1)
    seen = plain_terms(at, count, blocks, rows)
    dq, parts = [], []
    for h, (query, grad, kept) in enumerate(zip(plain_heads(q_all), plain_heads(g_all), plain_heads(exact))):
        key = kv_all[:, :128] if h < 2 else kv_all[:, 256:]
        value = kv_all[:, 128:256] if h < 2 else kv_all[:, 256:]
        delta = jnp.sum(grad.astype(F32) * kept, axis=-1, keepdims=True)
        scores = dot_columns(query, key) * SCORE - totals[:, h : h + 1]
        weights = jnp.exp(jnp.where(seen, scores, NEVER))
        g_scores = (weights * (dot_columns(grad, value) - delta)).astype(BF)
        dq.append(dot(g_scores, key) * SCORE)
        parts.append((dot_rows(g_scores, query) * SCORE, dot_rows(weights.astype(BF), grad)))
    dq = jnp.concatenate([dq[0][:, :HD], dq[1][:, HD:], dq[2][:, :HD], jnp.zeros_like(dq[2][:, :HD])], 1)
    dq = dq.astype(BF).reshape(count, rows, -1)
    acc = jnp.concatenate([parts[0][0] + parts[1][0], parts[0][1] + parts[1][1], parts[2][0] + parts[2][1]], 1)
    acc = acc.reshape(count, blocks, rows, -1)
    dq_all, summed = dq.reshape(count * rows, -1), acc.reshape(-1, acc.shape[-1]).astype(BF)
    own = jnp.concatenate([acc[i, at[1]] for i in range(count)], 0)
    away = [acc[i, at[1] ^ j].astype(BF) for j in range(1, blocks) for i in range(count)]
    return (own, jnp.concatenate(away, 0), dq_all, summed)


def merge_body(at, dq, own, *refs):
    arrived, out = refs[:-1], refs[-1]
    total = own[...]
    for ref in arrived:
        total = total + ref[...].astype(F32)
    out[:, :256] = dq[...]
    out[:, 256:] = total.astype(BF)


def gelu_terms(hidden):
    root = 0.7978845608028654
    square = hidden * hidden
    bend = jnp.tanh(root * hidden * (1.0 + 0.044715 * square))
    half = 0.5 * (1.0 + bend)
    slope = half + 0.5 * hidden * (1.0 - bend * bend) * root * (1.0 + 3.0 * 0.044715 * square)
    return hidden * half, slope


def g_output(extras, rows):
    return jnp.concatenate([(RESIDUAL * ref[:rows, :].astype(F32)).astype(BF) for ref in extras], axis=0)


def split_rows(values, rows, mine, other):
    mine[:rows, :] = values[:rows]
    mine[rows:, :] = values[2 * rows : 3 * rows]
    other[:rows, :] = values[rows : 2 * rows]
    other[rows:, :] = values[3 * rows :]


def middle_body(parts, rows, at, attended, vectors, fc, fc_bias, out, *refs):
    tokens, extras = refs[:parts], refs[parts : 2 * parts]
    gn_mine, gn_other, mid_mine, normed, active, g_hidden, own, att_all, proj = refs[2 * parts :]
    zero = jnp.zeros((HD, proj.shape[1]), BF)
    half = rows // 2
    low = lax.broadcasted_iota(jnp.int32, (half, 128), 1) < HD
    for k in range(parts):
        weight = extras[k][rows:, :]
        owner = at[2] ^ k
        packed = jnp.concatenate([weight[:128], zero, weight[128:]], axis=0)
        proj[rows_at(owner, 256), :] = packed
    size = rows + half
    for j in range(parts):
        for k in range(parts):
            piece = attended[j, k * size : (k + 1) * size, :]
            pair = piece[rows:].astype(F32)
            upper = jnp.where(low, 0.0, pltpu.roll(pair, HD, 1)).astype(BF)
            lower = jnp.where(low, 0.0, pair).astype(BF)
            block = block_of(at, k, rows)
            att_all[block, j * 256 : j * 256 + 128] = piece[:rows]
            att_all[block, j * 256 + 128 : (j + 1) * 256] = jnp.concatenate([upper, lower], axis=0)
    own[...] = att_all[:, pl.ds(pl.multiple_of(at[2] * 256, 256), 256)]
    branch = dot(att_all[...], proj[...]) + vectors[4:5]
    for k in range(parts):
        part = slice(k * rows, (k + 1) * rows)
        value = tokens[k][:rows, :].astype(F32) + RESIDUAL * branch[part]
        if k % 2 == 0:
            mid_mine[(k // 2) * rows : (k // 2 + 1) * rows, :] = value
        unit, _ = normalize(value)
        normed[part, :] = (unit * vectors[2:3] + vectors[3:4]).astype(BF)
    hidden = dot(normed[...], fc[...]) + as_row(fc_bias)
    value, slope = gelu_terms(hidden)
    active[...] = value.astype(BF)
    g_hidden[...] = (dot_columns(g_output(extras, rows), out[...]) * slope).astype(BF)
    split_rows(dot_columns(g_hidden[...], fc[...]), rows, gn_mine, gn_other)


def fill_half(half, bit, kept, away, chunk):
    size = kept.shape[0] // half
    for i in range(half):
        into = slice(i * size, (i + 1) * size)
        kept[into, :] = chunk(bit * half + i)
        away[into, :] = chunk((1 - bit) * half + i).astype(BF)


def proj_grad(attended, g_branch):
    grad = dot_rows(attended[...], g_branch[...])
    return jnp.concatenate([grad[:128], grad[128 + HD :]], axis=0)


def proj_grad_body(rows, at, attended, g_branch, sums_in, grad, sums):
    grad[...] = proj_grad(attended, g_branch)
    sums[...] = sums_in[...]
    sums[4:5, :] = jnp.sum(g_branch[:rows, :].astype(F32), axis=0, keepdims=True)


def pack_wide(values, lanes):
    third = values.shape[0] // 3
    rest = values[:, lanes:]
    low = [rest[i * third : (i + 1) * third] for i in range(3)]
    low.append(jnp.zeros((third, lanes - 384), values.dtype))
    return jnp.concatenate([values[:, :lanes], jnp.concatenate(low, axis=1)], axis=0)


def out_partial_body(rows, at, active, out, mine, other):
    split_rows(dot(active[...], out[...]), rows, mine, other)


def out_weights_body(rows, step, at, active, sums_in, *refs):
    extras = refs[:-4]
    kept, away, sums, grad = refs[-4:]
    g_out = g_output(extras, rows)
    grad[...] = dot_rows(active[...], g_out)
    half = kept.shape[0]
    bit = (at[3] // step) % 2
    kept[...] = grad[rows_at(bit, half), :]
    away[...] = grad[rows_at(1 - bit, half), :].astype(BF)
    sums[...] = sums_in[...]
    sums[5:6, :] = jnp.sum(g_out[:rows].astype(F32), axis=0, keepdims=True)


def fc_weights_body(parts, half, step, at, normed, g_hidden, sums_in, kept, away, sums, grad):
    grad[...] = dot_rows(normed[...], g_hidden[...])
    size = grad.shape[0] // (parts * 2 * half)

    def chunk(i):
        blocks = [((at[2] ^ j) * 2 * half + i) * size for j in range(parts)]
        return jnp.concatenate([grad[pl.ds(pl.multiple_of(start, 8), size), :] for start in blocks], axis=0)

    fill_half(half, (at[3] // step) % 2, kept, away, chunk)
    sums[...] = sums_in[...]
    sums[6:7, :] = jnp.sum(g_hidden[...].astype(F32), axis=0, keepdims=True)


def plain_weights_body(rows, at, active, normed, g_hidden, sums_in, *refs):
    extras = refs[:-3]
    out_grad, fc_grad, sums = refs[-3:]
    g_out = g_output(extras, rows)
    out_grad[...] = dot_rows(active[...], g_out).astype(BF)
    fc_grad[...] = dot_rows(normed[...], g_hidden[...]).astype(BF)
    sums[...] = sums_in[...]
    sums[5:6, :] = jnp.sum(g_out[:rows].astype(F32), axis=0, keepdims=True)
    sums[6:7, :] = jnp.sum(g_hidden[...].astype(F32), axis=0, keepdims=True)


def second_norm_body(rows, at, chip_sum, arrived, mid, own_extra, x_extra, vectors, sums_in, g_branch, own_middle, sums):
    add = arrived[...].astype(F32)
    grad = chip_sum[...] + jnp.concatenate([add[rows:], add[:rows]], axis=0)
    unit, scale = normalize(mid[...])
    back = norm_back(grad, unit, scale, vectors[2:3])
    sums[...] = sums_in[...]
    sums[2:3, :] = jnp.sum(grad[:rows] * unit[:rows], axis=0, keepdims=True)
    sums[3:4, :] = jnp.sum(grad[:rows], axis=0, keepdims=True)
    g_own = back[:rows] + own_extra[:rows, :].astype(F32)
    own_middle[...] = g_own
    g_branch[:rows, :] = (RESIDUAL * g_own).astype(BF)
    g_branch[rows:, :] = (RESIDUAL * (back[rows:] + x_extra[:rows, :].astype(F32))).astype(BF)


def attended_grad_body(parts, rows, at, mine, other, proj, *refs):
    outs, (kept, g_all) = refs[:parts], refs[parts:]
    kept[:rows, :] = mine[:rows, :]
    kept[rows : 2 * rows, :] = other[:rows, :]
    kept[2 * rows : 3 * rows, :] = mine[rows:, :]
    kept[3 * rows :, :] = other[rows:, :]
    zero = jnp.zeros((HD, proj.shape[1]), BF)
    weight = jnp.concatenate([proj[:128, :], zero, proj[128:, :]], axis=0)
    g_all[...] = dot_columns(kept[...], weight).astype(BF)
    for k in range(parts):
        outs[k][...] = g_all[block_of(at, k, rows), :]


def merge_pieces_body(rows, at, dq, own, arrived, *outs):
    for k, out in enumerate(outs):
        part = rows_at(at[0] ^ k, rows)
        out[:, :256] = dq[part, :]
        out[:, 256:] = (own[part, :] + arrived[part, :].astype(F32)).astype(BF)


def first_grad_body(parts, rows, at, matrix, *refs):
    pieces, (mine, other, mixed) = refs[:-3], refs[-3:]
    for i in range(parts):
        if len(pieces) == 1:
            mixed[rows_at(at[2] ^ i, rows), :] = pieces[0][i * rows : (i + 1) * rows, :]
        else:
            mixed[block_of(at, i, rows), :] = pieces[i][...]
    split_rows(dot_columns(mixed[...], matrix[...]), rows, mine, other)


def attn_halves_body(parts, count, at, own, every, dq, dkv, proj, kept, away, sums, grad):
    grad[:, :256] = dot_rows(own[...], dq[...])
    grad[:, 256:] = dot_rows(every[...], dkv[...])
    owner_rows = grad.shape[0] // parts
    size = owner_rows // (2 * count)
    packed = size + size // 3
    start = 0
    for k in range(count):
        place = at[1] * count + (at[0] ^ k)
        other = (1 - at[1]) * count + (at[0] ^ k)
        for j in range(parts):
            base = (at[2] ^ j) * 2 * count
            kept[start : start + size, :] = grad[rows_at(base + place, size), :]
            away[start : start + size, :] = grad[rows_at(base + other, size), :].astype(BF)
            start += size
        kept[start : start + packed, :] = pack_wide(proj[rows_at(place, size), :], grad.shape[1])
        away[start : start + packed, :] = pack_wide(proj[rows_at(other, size), :], grad.shape[1]).astype(BF)
        start += packed
    sums[...] = jnp.zeros_like(sums)
    sums[0:1, :256] = jnp.sum(dq[...].astype(F32), axis=0, keepdims=True)
    sums[0:1, 256:] = jnp.sum(dkv[...].astype(F32), axis=0, keepdims=True)


def attn_pair_body(at, kept, arrived, *outs):
    size = outs[0].shape[0]
    for k, out in enumerate(outs):
        part = slice(k * size, (k + 1) * size)
        out[...] = (kept[part, :] + arrived[part, :].astype(F32)).astype(out.dtype)


def attn_fold_body(count, at, *refs):
    total = refs[0][...]
    for ref in refs[1:count]:
        total = total + ref[...].astype(F32)
    start = 0
    for out in refs[count:]:
        out[...] = total[start : start + out.shape[0]].astype(BF)
        start += out.shape[0]


def attn_place_body(parts, count, at, *refs):
    own, away, (out, proj, kept) = refs[:count], refs[count], refs[count + 1 :]
    features = proj.shape[1]
    width, lanes = features // parts, kept.shape[2]
    size = width // (2 * count)
    total = own[0].shape[0]
    for side in range(2):
        block = at[1] if side == 0 else 1 - at[1]
        for k in range(count):
            piece = own[k][...] if side == 0 else away[k * total : (k + 1) * total, :]
            piece = piece.astype(F32)
            rows = rows_at(block * count + (at[0] ^ k), size)
            for j in range(parts):
                kept[at[2] ^ j, rows, :] = piece[j * size : (j + 1) * size]
            start = parts * size
            proj[rows, :lanes] = piece[start : start + size]
            low = piece[start + size :]
            proj[rows, lanes:] = jnp.concatenate([low[:, i * 128 : (i + 1) * 128] for i in range(3)], axis=0)
    for g in range(parts):
        first = g * width
        out[:, first : first + width] = kept[g, :, :width]
        first += features
        out[:, first : first + width] = jnp.concatenate([kept[g, :, 256:384], kept[g, :, 512 : 512 + HD]], axis=1)
        first += features
        out[:, first : first + width] = jnp.concatenate([kept[g, :, 384:512], kept[g, :, 512 + HD :]], axis=1)


def attn_weights_body(parts, ways, at, own, every, dq, dkv, grads, sums):
    query = dot_rows(own[...], dq[...])
    pair = dot_rows(every[...], dkv[...])
    size = query.shape[0] // (parts * ways)
    for c in range(ways):
        for j in range(parts):
            at_row = (j * ways + c) * size
            grads[c * parts + j, :, :256] = query[at_row : at_row + size].astype(BF)
            grads[c * parts + j, :, 256:] = pair[at_row : at_row + size].astype(BF)
    sums[...] = jnp.zeros_like(sums)
    sums[0:1, :256] = jnp.sum(dq[...].astype(F32), axis=0, keepdims=True)
    sums[0:1, 256:] = jnp.sum(dkv[...].astype(F32), axis=0, keepdims=True)


def attn_sum_body(parts, ways, at, arrived, out):
    for j in range(parts):
        total = arrived[j].astype(F32)
        for c in range(1, ways):
            total = total + arrived[c * parts + j].astype(F32)
        total = total.astype(BF)
        for c in range(ways):
            out[c, j, :, :] = total


def attn_final_body(parts, ways, at, arrived, out):
    size = arrived.shape[2]
    width = size * ways
    features = out.shape[1] // 3
    for c in range(ways):
        rows = slice(c * size, (c + 1) * size)
        for g in range(parts):
            piece = arrived[c, g].astype(F32)
            first = g * width
            out[rows, first : first + width] = piece[:, :width]
            first += features
            out[rows, first : first + width] = jnp.concatenate([piece[:, 256:384], piece[:, 512 : 512 + HD]], axis=1)
            first += features
            out[rows, first : first + width] = jnp.concatenate([piece[:, 384:512], piece[:, 512 + HD :]], axis=1)


def first_norm_body(rows, at, own, core, arrived, tokens, own_middle, vectors, sums, attn, input_grad, shares):
    grad = own[:rows, :] + core[:rows, :] + arrived[...].astype(F32)
    unit, scale = normalize(tokens[...].astype(F32))
    back = norm_back(grad, unit, scale, vectors[0:1])
    input_grad[...] = (back + own_middle[...]).astype(BF)
    first = [jnp.sum(grad * unit, axis=0, keepdims=True), jnp.sum(grad, axis=0, keepdims=True)]
    whole = jnp.concatenate(first + [sums[2:6, :], jnp.zeros((2, grad.shape[1]), F32)], axis=0)
    parts = whole.shape[1] // HD // 3
    width = whole.shape[1] // parts
    part = sums.shape[1] // 4
    value = jnp.concatenate([attn[0:1, 384:512], attn[0:1, 512 + HD :]], axis=1)
    local = [sums[6:7, i * part : (i + 1) * part] for i in range(4)] + [attn[0:1, :width], value]
    local = jnp.concatenate(local + [jnp.zeros((2, width), F32)], axis=0)
    blank = jnp.zeros((8, 256 - width), F32)
    for j in range(parts):
        piece = jnp.concatenate([whole[:, j * width : (j + 1) * width], blank, local, blank], axis=1)
        for c in range(shares.shape[0] // parts):
            shares[c * parts + j, :, :] = piece


def vector_final_body(ways, parts, at, arrived, *outs):
    width, hidden = outs[0].shape[0], outs[8].shape[0]
    total, local = jnp.zeros((8, arrived.shape[2]), F32), jnp.zeros((8, arrived.shape[2]), F32)
    for i in range(ways * parts):
        total = total + arrived[i]
    for c in range(ways):
        local = local + arrived[c * parts + at[2]]
    for row in range(6):
        outs[row][...] = total[row : row + 1, :width].reshape(width)
    part = hidden // 4
    outs[8][...] = jnp.concatenate([local[i : i + 1, 256 : 256 + part] for i in range(4)], axis=1).reshape(hidden)
    outs[6][...] = local[4:5, 256 : 256 + width].reshape(width)
    outs[7][...] = local[5:6, 256 : 256 + width].reshape(width)


def halve_body(step, at, held, arrived, kept, away, total):
    total[...] = held[...] + arrived[...].astype(F32)
    half = kept.shape[0]
    bit = (at[3] // step) % 2
    kept[...] = total[pl.ds(pl.multiple_of(bit * half, 8), half), :]
    away[...] = total[pl.ds(pl.multiple_of((1 - bit) * half, 8), half), :].astype(BF)


def last_sum_body(at, held, arrived, *outs):
    total = held[...] + arrived[...].astype(F32)
    start = 0
    for out in outs:
        out[...] = total[start : start + out.shape[0]].astype(BF)
        start += out.shape[0]


def stack_rows_body(at, *refs):
    out = refs[-1]
    start = 0
    for ref in refs[:-1]:
        out[start : start + ref.shape[0], :] = ref[...]
        start += ref.shape[0]


def chunk_number(at, mask, steps):
    number = 0
    for step in steps:
        number = number * 2 + ((at[3] ^ mask) // step) % 2
    return number


def chunks_of(at, steps, refs):
    masks = [0]
    found = [(0, refs[0], 0)]
    for step, ref in zip(reversed(steps), refs[1:]):
        found += [(mask ^ step, ref, i) for i, mask in enumerate(masks)]
        masks = masks + [mask ^ step for mask in masks]
    size = refs[0].shape[0]
    for mask, ref, i in found:
        yield chunk_number(at, mask, steps), ref[i * size : (i + 1) * size, :].astype(F32)


def out_final_body(steps, at, *refs):
    for place, piece in chunks_of(at, steps, refs[:-1]):
        refs[-1][rows_at(place, piece.shape[0]), :] = piece


def fc_final_body(parts, steps, at, *refs):
    out = refs[-1]
    hidden = out.shape[1] // parts
    for place, piece in chunks_of(at, steps, refs[:-1]):
        size = piece.shape[0] // parts
        for j in range(parts):
            lanes = pl.ds(pl.multiple_of((at[2] ^ j) * hidden, 128), hidden)
            out[rows_at(place, size), lanes] = piece[j * size : (j + 1) * size]


class Values:
    pass


def shards(
    parts,
    ways,
    tokens,
    first_gain,
    first_bias,
    attn_weight,
    query_bias,
    value_bias,
    proj_weight,
    proj_bias,
    second_gain,
    second_bias,
    fc_weight,
    fc_bias,
    out_weight,
    out_bias,
    cotangent,
):
    rows, features = tokens.shape[1], tokens.shape[2]
    width = features // parts
    count = parts
    blocks = ways // count
    hidden = fc_weight.shape[1] // parts
    columns = 256 + 2 * width
    all_rows, half_rows = parts * rows, parts * rows // 2
    f = lax.axis_index("fsdp").astype(jnp.int32)
    c = lax.axis_index("ctx").astype(jnp.int32)
    at = jnp.stack([c // blocks, c % blocks, f, c])
    halved = ways == 8
    chunks, size = 4, width // 8
    packed = size + size // 3
    small_blocks = blocks * count * rows <= 1024
    last = []
    v = Values()

    def run(body, outs, *args, mib=16, scratch=()):
        task = v.task
        held = [] if task in v.free else last
        hooked = jax.tree.leaves(v.hooks[task]()) if task in v.hooks else []
        made = call(
            body,
            task.__name__,
            outs,
            at,
            *args,
            scratch=scratch,
            after=[*held, *hooked],
            us=v.costs.get(task, 1.0),
            mib=mib,
        )
        if task not in v.free:
            last[:] = [made[-1]]
        return made

    def over_fsdp(value, k):
        return lax.ppermute(value, "fsdp", [(i, i ^ k) for i in range(parts)])

    def over_ctx(value, k):
        return lax.ppermute(value, "ctx", [(i, i ^ k) for i in range(ways)])

    def spread(value):
        across = over_fsdp(value, 2)
        return [value, over_fsdp(value, 1), across, over_fsdp(across, 1)]

    def turn_fsdp(pieces):
        return [pieces[0]] + [over_fsdp(pieces[k], k) for k in range(1, parts)]

    def turn_ctx(pieces):
        return [pieces[0]] + [over_ctx(pieces[k], k * blocks) for k in range(1, count)]

    def halve(kept, arrived, step):
        half, lanes = kept.shape[0] // 2, kept.shape[1]
        outs = [shape((half, lanes), F32), shape((half, lanes), BF)]
        return run(partial(halve_body, step), outs, kept, arrived, scratch=[pltpu.VMEM((2 * half, lanes), F32)])

    def last_sum(kept, arrived, cuts):
        return run(last_sum_body, [shape((cut, kept.shape[1]), BF) for cut in cuts], kept, arrived)

    def stacked(pieces):
        total = sum(piece.shape[0] for piece in pieces)
        return run(stack_rows_body, [shape((total, pieces[0].shape[1]), BF)], *pieces)[0]

    v.sums = jnp.zeros((8, features), F32)

    def attn_columns():
        outs = [shape((width, columns), BF)] * parts
        v.attn_pieces = turn_fsdp(run(partial(attn_columns_body, parts), outs, attn_weight))
        v.attn_core = [v.attn_pieces[1]]

    def token_message():
        args = (tokens[0], first_gain, first_bias, second_gain, second_bias, proj_bias, out_bias)
        v.tokens = spread(run(token_message_body, [shape((rows + 8, features), BF)], *args)[0])

    def fc_columns():
        outs = [shape((width, hidden), BF)] * parts
        v.fc_columns = turn_fsdp(run(fc_columns_body, outs, fc_weight))
        v.fc_core = [v.fc_columns[1]]

    def mixed():
        made = run(
            partial(mixed_body, parts, count),
            [shape((all_rows, features), BF), shape((features, columns), BF), shape((8, features), F32)]
            + [shape((5 * rows // 2, 256), BF)] * count
            + [shape((rows, 384), BF)] * count,
            query_bias,
            value_bias,
            *v.tokens,
            *v.attn_pieces,
            scratch=[pltpu.VMEM((all_rows, columns), BF)],
        )
        v.attn_matrix, v.vectors = made[1:3]
        v.pairs = turn_ctx(made[3 + count :])
        v.queries = turn_ctx(made[3 : 3 + count])

    def stack_pairs():
        joined = stacked(v.pairs)
        v.partners = [over_ctx(joined, j) for j in range(1, blocks)]

    def join_fc():
        v.fc_matrix = run(join_body, [shape((features, hidden), BF)], *v.fc_columns)[0]

    def stack_extra():
        v.extra = spread(stacked([cotangent[0], proj_weight]))
        v.extra_across = [v.extra[2]]

    def attend():
        kept = run(
            partial(attend_body, count, blocks, rows),
            [shape((rows + rows // 2, 128), BF)] * count
            + [
                shape((count * rows, 256), F32),
                shape((count * rows, 128), F32),
                shape((count * rows, 256), BF),
                shape((count * blocks * rows, 384), BF),
            ],
            *v.queries,
            *v.pairs,
            *v.partners,
        )
        v.att_pieces, v.state = turn_ctx(kept[:count]), kept[count:]

    def plain_front():
        kept = plain_attend(count, blocks, rows, at, v.queries, v.pairs, v.partners)
        v.att_pieces, v.state = turn_ctx(kept[:count]), kept[count:]

    def normed_stack():
        outs = [shape((count * rows, features // 2), BF)]
        own = run(partial(normed_stack_body, rows), outs, *v.queries)[0]
        v.normed_across = [over_ctx(own, j) for j in range(1, blocks)]
        v.normed_sides = [own] + v.normed_across

    def middle():
        attended_all = lax.all_gather(jnp.concatenate(v.att_pieces, 0), "fsdp")
        gn_mine, gn_other, v.mid_mine, v.normed_two, v.active, v.g_hidden, v.attended = run(
            partial(middle_body, parts, rows),
            [shape((half_rows, features), F32)] * 3
            + [shape((all_rows, features), BF), shape((all_rows, hidden), BF), shape((all_rows, hidden), BF)]
            + [shape((all_rows, 256), BF)],
            attended_all,
            v.vectors,
            v.fc_matrix,
            fc_bias,
            out_weight,
            *v.tokens,
            *v.extra,
            scratch=[pltpu.VMEM((all_rows, parts * 256), BF), pltpu.VMEM((parts * 256, features), BF)],
            mib=24,
        )
        v.chip_sum = gn_mine + over_fsdp(gn_other, 1)
        v.chip_low = v.chip_sum.astype(BF)
        v.arrived = over_fsdp(v.chip_low, 2)


    def place():
        sides = v.normed_sides + [over_fsdp(side, 1) for side in v.normed_sides]
        v.every, v.own_rows = run(
            partial(normed_place_body, count, blocks, rows),
            [shape((count * blocks * rows, features), BF), shape((count * rows, features), BF)],
            *sides,
        )

    def fc_weights():
        v.fc_kept, away, v.sums = run(
            partial(fc_weights_body, parts, chunks, FC_STEPS[0]),
            [shape((features // 2, hidden), F32), shape((features // 2, hidden), BF), shape((8, features), F32)],
            v.normed_two,
            v.g_hidden,
            v.sums,
            scratch=[pltpu.VMEM((features, hidden), F32)],
        )
        v.fc_in = over_ctx(away, FC_STEPS[0])

    def out_weights():
        v.out_kept, away, v.sums = run(
            partial(out_weights_body, rows, OUT_STEPS[0]),
            [shape((hidden // 2, features), F32), shape((hidden // 2, features), BF), shape((8, features), F32)],
            v.active,
            v.sums,
            *v.extra,
            scratch=[pltpu.VMEM((hidden, features), F32)],
        )
        v.out_in = over_ctx(away, OUT_STEPS[0])

    def both_weights():
        v.out_grad, v.fc_grad, v.sums = run(
            partial(plain_weights_body, rows),
            [shape((hidden, features), BF), shape((features, hidden), BF), shape((8, features), F32)],
            v.active,
            v.normed_two,
            v.g_hidden,
            v.sums,
            *v.extra,
        )

    def second_norm():
        v.g_branch, v.own_middle, v.sums = run(
            partial(second_norm_body, rows),
            [shape((half_rows, features), BF), shape((rows, features), F32), shape((8, features), F32)],
            v.chip_sum,
            v.arrived,
            v.mid_mine,
            v.extra[0],
            v.extra[2],
            v.vectors,
            v.sums,
        )

    def attended_grad():
        grads = run(
            partial(attended_grad_body, parts, rows),
            [shape((rows, 256), BF)] * parts + [shape((all_rows, features), BF)],
            v.g_branch,
            over_fsdp(v.g_branch, 1),
            proj_weight,
            scratch=[pltpu.VMEM((all_rows, 256), BF)],
        )
        v.g_pieces, v.g_branch_all = turn_ctx(grads[:parts]), grads[parts]

    def proj_weights():
        v.proj, v.sums = run(
            partial(proj_grad_body, rows),
            [shape((width, features), F32), shape((8, features), F32)],
            v.attended,
            v.g_branch_all,
            v.sums,
        )

    def fc_one():
        v.fc_kept, away = halve(v.fc_kept, v.fc_in, FC_STEPS[1])
        v.fc_in = over_ctx(away, FC_STEPS[1])

    def fc_two():
        v.fc_kept, away = halve(v.fc_kept, v.fc_in, FC_STEPS[2])
        v.fc_in = over_ctx(away, FC_STEPS[2])

    def fc_sum():
        v.fc_parts = turn_fsdp(last_sum(v.fc_kept, v.fc_in, [size] * parts))

    def fc_turned():
        part = stacked(v.fc_parts)
        v.fc_pieces = [part, over_ctx(part, FC_STEPS[2])]

    def fc_double():
        v.fc_pieces.append(over_ctx(stacked(v.fc_pieces), FC_STEPS[1]))

    def fc_fourfold():
        v.fc_pieces.append(over_ctx(stacked(v.fc_pieces), FC_STEPS[0]))

    def fc_final():
        outs = [shape((width, parts * hidden), F32)]
        v.fc_weight_grad = run(partial(fc_final_body, parts, FC_STEPS), outs, *v.fc_pieces)[0]

    def out_one():
        v.out_kept, away = halve(v.out_kept, v.out_in, OUT_STEPS[1])
        v.out_in = over_ctx(away, OUT_STEPS[1])

    def out_two():
        v.out_kept, away = halve(v.out_kept, v.out_in, OUT_STEPS[2])
        v.out_in = over_ctx(away, OUT_STEPS[2])

    def out_sum():
        part = last_sum(v.out_kept, v.out_in, [hidden // 8])[0]
        v.out_pieces = [part, over_ctx(part, OUT_STEPS[2])]

    def out_double():
        v.out_pieces.append(over_ctx(stacked(v.out_pieces), OUT_STEPS[1]))

    def out_fourfold():
        v.out_pieces.append(over_ctx(stacked(v.out_pieces), OUT_STEPS[0]))

    def out_final():
        outs = [shape((hidden, features), F32)]
        v.out_weight_grad = run(partial(out_final_body, OUT_STEPS), outs, *v.out_pieces)[0]

    def attend_back():
        v.own, away, v.dq, v.dkv = run(
            partial(attend_back_body, count, blocks, rows),
            [
                shape((count * rows, 384), F32),
                shape(((blocks - 1) * count * rows, 384), BF),
                shape((count * rows, 256), BF),
                shape((count * blocks * rows, 384), BF),
            ],
            *v.g_pieces,
            v.state[2],
            v.state[3],
            *v.state[:2],
            scratch=[pltpu.VMEM((count * rows, 256), BF), pltpu.VMEM((count * blocks * rows, 384), F32)],
        )
        v.from_partners = [over_ctx(away, 1)]

    def plain_back():
        v.own, away, v.dq, v.dkv = plain_attend_back(
            count, blocks, rows, at, v.g_pieces, v.state[2], v.state[3], *v.state[:2]
        )
        stack = count * rows
        v.from_partners = [over_ctx(away[(j - 1) * stack : j * stack], j) for j in range(1, blocks)]

    def attn_weights():
        outs = [shape((count * (parts * size + packed), columns), kind) for kind in (F32, BF)]
        v.attn_kept, away, v.sums_attn = run(
            partial(attn_halves_body, parts, count),
            outs + [shape((8, columns), F32)],
            v.own_rows,
            v.every,
            v.dq,
            v.dkv,
            v.proj,
            scratch=[pltpu.VMEM((features, columns), F32)],
        )
        v.attn_in = over_ctx(away, 1)

    def attn_pair():
        outs = [shape((parts * size + packed, columns), kind) for kind in (F32, BF, BF, BF)]
        v.attn_sent = turn_ctx(run(attn_pair_body, outs, v.attn_kept, v.attn_in))

    def attn_fold():
        outs = [shape((size, columns), BF)] * parts + [shape((packed, columns), BF)]
        *attn_parts, v.proj = run(partial(attn_fold_body, count), outs, *v.attn_sent)
        v.attn_parts = turn_fsdp(attn_parts)

    def attn_turned():
        v.attn_pieces = turn_ctx([stacked([*v.attn_parts, v.proj])] * count)

    def attn_fourfold():
        v.attn_pieces.append(over_ctx(stacked(v.attn_pieces), 1))

    def attn_final():
        outs = [shape((width, 3 * features), F32), shape((width, features), F32)]
        v.attn_weight_grad, v.proj_weight_grad = run(
            partial(attn_place_body, parts, count),
            outs,
            *v.attn_pieces,
            scratch=[pltpu.VMEM((parts, width, columns), F32)],
        )

    def plain_attn_weights():
        attn_grads, v.sums_attn = run(
            partial(attn_weights_body, parts, ways),
            [shape((parts * ways, width // ways, columns), BF), shape((8, columns), F32)],
            v.own_rows,
            v.every,
            v.dq,
            v.dkv,
        )
        attn_in = lax.all_to_all(attn_grads, ("ctx", "fsdp"), split_axis=0, concat_axis=0, tiled=True)
        outs = [shape((ways, parts, width // ways, columns), BF)]
        attn_sum = run(partial(attn_sum_body, parts, ways), outs, attn_in)[0]
        attn_all = lax.all_to_all(attn_sum, "ctx", split_axis=0, concat_axis=0, tiled=True)
        outs = [shape((width, 3 * features), F32)]
        v.attn_weight_grad = run(partial(attn_final_body, parts, ways), outs, attn_all)[0]

    def merge():
        outs = [shape((count * rows, columns), BF)]
        if MERGE_PERMUTES and halved:
            outs = [shape((rows, columns), BF)] * count
            pieces = run(partial(merge_pieces_body, rows), outs, v.dq, v.own, *v.from_partners)
            v.g_mixed = turn_ctx(pieces)
            return
        made = run(merge_body, outs, v.dq, v.own, *v.from_partners)[0]
        groups = [[i * blocks + j for i in range(count)] for j in range(blocks)]
        v.g_mixed = lax.all_to_all(made, "ctx", split_axis=0, concat_axis=0, tiled=True, axis_index_groups=groups)

    def out_partial():
        outs = [shape((half_rows, features), F32)] * 2
        mine, other = run(partial(out_partial_body, rows), outs, v.active, out_weight)
        core = over_fsdp(other, 1)
        across = over_fsdp((mine[rows:] + core[rows:]).astype(BF), 2)
        output = mine[:rows] + core[:rows] + across.astype(F32) + v.vectors[5:6]
        v.block_out = (v.mid_mine[:rows] + RESIDUAL * output).astype(BF)

    def first_grad():
        mine, other = run(
            partial(first_grad_body, parts, rows),
            [shape((half_rows, features), F32)] * 2,
            v.attn_matrix,
            *(v.g_mixed if MERGE_PERMUTES and halved else [v.g_mixed]),
            scratch=[pltpu.VMEM((all_rows, columns), BF)],
        )
        arrived = over_fsdp(other, 1)
        v.first_own = (mine, arrived)
        v.first_in = over_fsdp((mine[rows:] + arrived[rows:]).astype(BF), 2)

    def first_norm():
        v.input_grad, shares = run(
            partial(first_norm_body, rows),
            [shape((rows, features), BF), shape((parts * ways, 8, 512), F32)],
            *v.first_own,
            v.first_in,
            tokens[0],
            v.own_middle,
            v.vectors,
            v.sums,
            v.sums_attn,
        )
        v.shares = lax.all_to_all(shares, ("ctx", "fsdp"), split_axis=0, concat_axis=0, tiled=True)

    def vector_final():
        outs = [shape((width,), F32)] * 8 + [shape((hidden,), F32)]
        v.vector_grads = run(partial(vector_final_body, ways, parts), outs, v.shares)

    def gather_rest():
        def over_all(value):
            part = lax.psum_scatter(value, "ctx", scatter_dimension=1, tiled=True)
            return lax.all_gather(part, "ctx", axis=1, tiled=True)

        v.out_weight_grad = over_all(v.out_grad).astype(F32)
        v.proj_weight_grad = over_all(v.proj.astype(BF)).astype(F32)
        fc_grad = over_all(v.fc_grad).reshape(parts, width, hidden)
        fc_grad = lax.all_to_all(fc_grad, "fsdp", split_axis=0, concat_axis=0)
        v.fc_weight_grad = fc_grad.transpose(1, 0, 2).reshape(width, parts * hidden).astype(F32)

    v.free = {
        attn_pair, fc_final, fc_fourfold, fc_one, fc_two, out_double, out_final, out_partial, out_sum, place,
        vector_final,
    }
    v.hooks = {
        attend: lambda: [v.extra_across],
        attn_fourfold: lambda: [v.out_pieces],
        attn_pair: lambda: [v.from_partners],
        fc_columns: lambda: [v.attn_core],
        fc_weights: lambda: [v.chip_low],
        middle: lambda: [v.normed_across],
        mixed: lambda: [v.fc_core],
        out_partial: lambda: [v.queries],
        out_weights: lambda: [v.chip_low],
        place: lambda: [v.chip_low],
    }
    v.costs = {merge: 1.0, out_sum: 1000000.0}
    front = (attn_columns, token_message, fc_columns, mixed, stack_pairs, join_fc, stack_extra)
    if halved:
        order = (
            attn_columns, token_message, fc_columns, mixed, stack_pairs, join_fc, stack_extra, attend, normed_stack,
            middle, fc_weights, out_weights, second_norm, attended_grad, fc_one, place, proj_weights, out_one,
            attend_back, attn_weights, fc_two, out_two, fc_sum, merge, fc_turned, first_grad, attn_pair, out_sum,
            first_norm, out_double, fc_double, attn_fold, out_partial, out_fourfold, attn_turned, attn_fourfold,
            out_final, fc_fourfold, vector_final, fc_final, attn_final,
        )
    else:
        order = (*front, plain_front, normed_stack, middle, place, both_weights, second_norm, attended_grad)
        order += (proj_weights, plain_back, plain_attn_weights, merge, first_grad, out_partial, first_norm)
        order += (vector_final, gather_rest)
    for task in order:
        v.task = task
        task()
    first_gain_grad, first_bias_grad, second_gain_grad, second_bias_grad = v.vector_grads[:4]
    proj_bias_grad, out_bias_grad, query_bias_grad, value_bias_grad, fc_bias_grad = v.vector_grads[4:]
    return (
        v.block_out[None],
        v.input_grad[None],
        first_gain_grad,
        first_bias_grad,
        v.attn_weight_grad,
        query_bias_grad,
        value_bias_grad,
        v.proj_weight_grad,
        proj_bias_grad,
        second_gain_grad,
        second_bias_grad,
        v.fc_weight_grad,
        fc_bias_grad,
        v.out_weight_grad,
        out_bias_grad,
    )


def solution(mesh):
    rows, row, matrix = P("fsdp", "ctx", None), P("fsdp"), P("fsdp", None)
    return jax.shard_map(
        partial(shards, mesh.shape["fsdp"], mesh.shape["ctx"]),
        mesh=mesh,
        in_specs=(
            rows, row, row, matrix, row, row, matrix, row, row, row, matrix, row, matrix, row, rows,
        ),
        out_specs=(
            rows, rows, row, row, matrix, row, row, matrix, row, row, row, matrix, row, matrix, row,
        ),
        check_vma=False,
    )
```

```python
from functools import partial

import jax
import jax.numpy as jnp
from jax import lax
from jax.experimental import pallas as pl
from jax.experimental.pallas import tpu as pltpu
from jax.sharding import PartitionSpec as P

HD = 64
LAYERS = 12
EPSILON = 1e-05
BF = jnp.bfloat16
F32 = jnp.float32
RESIDUAL = LAYERS ** (-0.5)
SCORE = HD ** (-0.5)
NEVER = -1e30
OUT_STEPS, FC_STEPS = (1, 2, 4), (2, 1, 4)
MERGE_PERMUTES = True


def shape(dims, kind):
    return jax.ShapeDtypeStruct(dims, kind)


def call(body, name, outs, *args, scratch=(), after=(), us=1.0, mib=16):
    vmem = pl.BlockSpec(memory_space=pltpu.VMEM)
    smem = pl.BlockSpec(memory_space=pltpu.SMEM)
    held = pl.BlockSpec(memory_space=pl.ANY)
    count, waits = len(args), len(after)

    def run(*refs):
        body(*refs[:count], *refs[count + waits :])

    return pl.pallas_call(
        run,
        name=name,
        out_shape=outs,
        in_specs=[smem] + [vmem] * (count - 1) + [held] * waits,
        out_specs=[vmem] * len(outs),
        scratch_shapes=list(scratch),
        cost_estimate=pl.CostEstimate(flops=int(us * 1e3), transcendentals=0, bytes_accessed=int(us * 1e3)),
        compiler_params=pltpu.CompilerParams(vmem_limit_bytes=mib * 1024 * 1024),
    )(*args, *after)


def rows_at(index, size):
    return pl.ds(pl.multiple_of(index * size, size), size)


def dot(first, second):
    return jnp.dot(first, second, preferred_element_type=F32)


def dot_rows(first, second):
    return lax.dot_general(first, second, (((0,), (0,)), ((), ())), preferred_element_type=F32)


def dot_columns(first, second):
    return lax.dot_general(first, second, (((1,), (1,)), ((), ())), preferred_element_type=F32)


def normalize(values):
    center = jnp.mean(values, axis=-1, keepdims=True)
    centered = values - center
    spread = jnp.mean(centered * centered, axis=-1, keepdims=True)
    scale = lax.rsqrt(spread + EPSILON)
    return centered * scale, scale


def norm_back(grad, unit, scale, gain):
    inner = grad * gain
    mean_inner = jnp.mean(inner, axis=-1, keepdims=True)
    mean_along = jnp.mean(inner * unit, axis=-1, keepdims=True)
    return scale * (inner - mean_inner - unit * mean_along)


def join(at, pieces, whole):
    size = pieces[0].shape[0]
    for k, piece in enumerate(pieces):
        whole[rows_at(at[2] ^ k, size), :] = piece[...]


def as_row(ref):
    return ref[...].astype(F32).reshape(1, ref.shape[0])


def attn_columns_body(parts, at, attn, *pieces):
    features = attn.shape[1] // 3
    width = features // parts
    for owner in range(parts):

        @pl.when(at[2] == owner)
        def _():
            for k in range(parts):
                first = (owner ^ k) * width
                piece = pieces[k]
                piece[:, :width] = attn[:, first : first + width]
                piece[:, width:256] = jnp.zeros((width, 256 - width), BF)
                key = attn[:, features + first : features + first + width]
                value = attn[:, 2 * features + first : 2 * features + first + width]
                piece[:, 256:384] = key[:, :128]
                piece[:, 384:512] = value[:, :128]
                piece[:, 512 : 512 + HD] = key[:, 128:]
                piece[:, 512 + HD :] = value[:, 128:]


def token_message_body(at, tokens, *refs):
    vectors, out = refs[:-1], refs[-1]
    rows, width = tokens.shape[0], vectors[0].shape[0]
    out[:rows, :] = tokens[...]
    small = jnp.concatenate([as_row(ref) for ref in vectors] + [jnp.zeros((8 - len(vectors), width), F32)], axis=0)
    rest = jnp.zeros((8, tokens.shape[1] - width), F32)
    out[rows:, :] = jnp.concatenate([small, rest], axis=1).astype(BF)


def fc_columns_body(at, fc, *pieces):
    for k, piece in enumerate(pieces):
        hidden = piece.shape[1]
        piece[...] = fc[:, pl.ds(pl.multiple_of((at[2] ^ k) * hidden, 128), hidden)]


def join_body(at, *refs):
    join(at, refs[:-1], refs[-1])


def block_of(at, k, rows):
    return rows_at(at[2] ^ at[0] ^ k, rows)


def mixed_body(parts, count, at, query_bias, value_bias, *refs):
    tokens, weights = refs[:parts], refs[parts : 2 * parts]
    normed, matrix, vectors, *outs, kept = refs[2 * parts :]
    rows = tokens[0].shape[0] - 8
    join(at, weights, matrix)
    columns = matrix.shape[1]
    width = weights[0].shape[0]
    for owner in range(parts):

        @pl.when(at[2] == owner)
        def _():
            for k in range(parts):
                lanes = slice((owner ^ k) * width, ((owner ^ k) + 1) * width)
                vectors[:, lanes] = tokens[k][rows:, :width].astype(F32)

    small = vectors[...]
    for k in range(parts):
        unit, _ = normalize(tokens[k][:rows, :].astype(F32))
        normed[k * rows : (k + 1) * rows, :] = (unit * small[0:1] + small[1:2]).astype(BF)
    query, value = as_row(query_bias), as_row(value_bias)
    none = jnp.zeros((1, 128), F32)
    bias = [query, none[:, :HD], none, value[:, :128], none[:, :HD], value[:, 128:]]
    bias = jnp.concatenate(bias, axis=1)
    kept[...] = (dot(normed[...], matrix[...]) + bias).astype(BF)
    half = rows // 2
    third = normed.shape[1] // 6
    first = (at[2] % 2) * 3 * third
    for k in range(count):
        block = block_of(at, k, rows)
        outs[k][:rows, :] = kept[block, :256]
        part = normed[block, pl.ds(pl.multiple_of(first, 128), 3 * third)]
        outs[k][rows : 2 * rows, :] = part[:, : 2 * third]
        outs[k][2 * rows :, :third] = part[:half, 2 * third :]
        outs[k][2 * rows :, third:] = part[half:, 2 * third :]
        outs[count + k][...] = kept[block, 256:]


def normed_stack_body(rows, at, *refs):
    half = rows // 2
    out = refs[-1]
    third = out.shape[1] // 3
    for k, ref in enumerate(refs[:-1]):
        part = slice(k * rows, (k + 1) * rows)
        out[part, : 2 * third] = ref[rows : 2 * rows, :]
        out[k * rows : k * rows + half, 2 * third :] = ref[2 * rows :, :third]
        out[k * rows + half : (k + 1) * rows, 2 * third :] = ref[2 * rows :, third:]


def normed_place_body(count, blocks, rows, at, *refs):
    sides, (every, own) = refs[:-2], refs[-2:]
    lanes = sides[0].shape[1]
    core = at[2] % 2
    for side in range(2):
        part = pl.ds(pl.multiple_of((core if side == 0 else 1 - core) * lanes, 128), lanes)
        for j in range(blocks):
            ref = sides[side * blocks + j]
            for k in range(count):
                row = at[0] ^ k
                piece = ref[k * rows : (k + 1) * rows, :]
                every[rows_at(row * blocks + (at[1] ^ j), rows), part] = piece
                if j == 0:
                    own[rows_at(row, rows), part] = piece


def place(at, count, blocks, rows, queries, pairs, partners, q_all, kv_all):
    for k in range(count):
        row = at[0] ^ k
        q_all[rows_at(row, rows), :] = queries[k][:rows, :]
        kv_all[rows_at(row * blocks + at[1], rows), :] = pairs[k][...]
        for j, partner in enumerate(partners):
            side = row * blocks + (at[1] ^ (j + 1))
            kv_all[rows_at(side, rows), :] = partner[k * rows : (k + 1) * rows, :]


def head_views(tile_one, tile_two, scale):
    low = lax.broadcasted_iota(jnp.int32, tile_one.shape, 1) < HD
    zero = jnp.zeros_like(tile_one)
    tile_one = tile_one * scale if scale is not None else tile_one
    tile_two = tile_two * scale if scale is not None else tile_two
    return (jnp.where(low, tile_one, zero), jnp.where(low, zero, tile_one), tile_two)


def visible_keys(at, i, blocks, rows, keys):
    query = (i * blocks + at[1]) * rows + lax.broadcasted_iota(jnp.int32, (rows, keys), 0)
    return lax.broadcasted_iota(jnp.int32, (rows, keys), 1) <= query


def attend_body(count, blocks, rows, at, *refs):
    queries, pairs = refs[:count], refs[count : 2 * count]
    partners = refs[2 * count : 2 * count + blocks - 1]
    outs = refs[2 * count + blocks - 1 :]
    pieces, (exact, totals, q_all, kv_all) = outs[:count], outs[count:]
    place(at, count, blocks, rows, queries, pairs, partners, q_all, kv_all)
    low = lax.broadcasted_iota(jnp.int32, (rows, 128), 1) < HD
    for i in range(count):
        keys = (i + 1) * blocks * rows
        mine = slice(i * rows, (i + 1) * rows)
        heads = head_views(q_all[mine, :128], q_all[mine, 128:], SCORE)
        seen = visible_keys(at, i, blocks, rows, keys)
        found = []
        for h, query in enumerate(heads):
            key_cols = slice(0, 128) if h < 2 else slice(256, 384)
            value_cols = slice(128, 256) if h < 2 else slice(256, 384)
            scores = jnp.where(seen, dot_columns(query, kv_all[:keys, key_cols]), NEVER)
            highest = jnp.max(scores, axis=-1, keepdims=True)
            weights = jnp.exp(scores - highest)
            total = jnp.sum(weights, axis=-1, keepdims=True)
            totals[mine, h : h + 1] = highest + jnp.log(total)
            weights = (weights * (1.0 / total)).astype(BF)
            found.append(dot(weights, kv_all[:keys, value_cols]))
        exact[mine, :128] = jnp.where(low, found[0], found[1])
        exact[mine, 128:] = jnp.where(low, 0.0, found[2])
    half = rows // 2
    for k in range(count):
        block = rows_at(at[0] ^ k, rows)
        pieces[k][:rows, :] = exact[block, :128].astype(BF)
        last = exact[block, 128:]
        pair = jnp.where(low[:half], pltpu.roll(last[:half], HD, 1), last[half:])
        pieces[k][rows:, :] = pair.astype(BF)


def attend_back_body(count, blocks, rows, at, *refs):
    grads, (q_all, kv_all, exact, totals) = refs[:count], refs[count : count + 4]
    outs = refs[count + 4 :]
    own, away, dq_all, summed, g_all, acc = outs
    for k in range(count):
        g_all[rows_at(at[0] ^ k, rows), :] = grads[k][...]
    acc[...] = jnp.zeros_like(acc)
    low = lax.broadcasted_iota(jnp.int32, (rows, 128), 1) < HD
    for i in range(count):
        keys = (i + 1) * blocks * rows
        mine = slice(i * rows, (i + 1) * rows)
        q_heads = head_views(q_all[mine, :128], q_all[mine, 128:], SCORE)
        g_heads = head_views(g_all[mine, :128], g_all[mine, 128:], None)
        seen = visible_keys(at, i, blocks, rows, keys)
        found = []
        for h in range(3):
            key_cols = slice(0, 128) if h < 2 else slice(256, 384)
            value_cols = slice(128, 256) if h < 2 else slice(256, 384)
            kept = exact[mine, :128] if h < 2 else exact[mine, 128:]
            delta = jnp.sum(g_heads[h].astype(F32) * kept, axis=-1, keepdims=True)
            scores = dot_columns(q_heads[h], kv_all[:keys, key_cols]) - totals[mine, h : h + 1]
            weights = jnp.exp(jnp.where(seen, scores, NEVER))
            g_weights = dot_columns(g_heads[h], kv_all[:keys, value_cols])
            g_scores = (weights * (g_weights - delta)).astype(BF)
            found.append(dot(g_scores, kv_all[:keys, key_cols]))
            acc[:keys, key_cols] += dot_rows(g_scores, q_heads[h])
            acc[:keys, value_cols] += dot_rows(weights.astype(BF), g_heads[h])
        dq_all[mine, :128] = (jnp.where(low, found[0], found[1]) * SCORE).astype(BF)
        dq_all[mine, 128:] = (jnp.where(low, found[2], 0.0) * SCORE).astype(BF)
    summed[...] = acc[...].astype(BF)
    for i in range(count):
        into = slice(i * rows, (i + 1) * rows)
        own[into, :] = acc[rows_at(i * blocks + at[1], rows), :]
        for j in range(1, blocks):
            from_rows = slice(((j - 1) * count + i) * rows, ((j - 1) * count + i + 1) * rows)
            away[from_rows, :] = acc[rows_at(i * blocks + (at[1] ^ j), rows), :].astype(BF)


def plain_heads(values):
    zero = jnp.zeros_like(values[:, :HD])
    first = jnp.concatenate([values[:, :HD], zero], 1)
    second = jnp.concatenate([zero, values[:, HD:128]], 1)
    return (first, second, values[:, 128:])


def plain_terms(at, count, blocks, rows):
    q_pos = (jnp.arange(count)[:, None] * blocks + at[1]) * rows + jnp.arange(rows)[None]
    k_pos = jnp.arange(count * blocks * rows)
    return k_pos[None] <= q_pos.reshape(-1)[:, None]


def plain_attend(count, blocks, rows, at, queries, pairs, partners):
    width = pairs[0].shape[1]
    q_all = jnp.zeros((count, rows, queries[0].shape[1]), BF)
    kv_all = jnp.zeros((count, blocks, rows, width), BF)
    for k in range(count):
        row = at[0] ^ k
        q_all = q_all.at[row].set(queries[k][:rows])
        kv_all = kv_all.at[row, at[1]].set(pairs[k])
        for j, partner in enumerate(partners):
            kv_all = kv_all.at[row, at[1] ^ (j + 1)].set(partner[k * rows : (k + 1) * rows])
    q_all, kv_all = q_all.reshape(count * rows, -1), kv_all.reshape(-1, width)
    seen = plain_terms(at, count, blocks, rows)
    found, totals = [], []
    for h, query in enumerate(plain_heads(q_all)):
        key = kv_all[:, :128] if h < 2 else kv_all[:, 256:]
        value = kv_all[:, 128:256] if h < 2 else kv_all[:, 256:]
        scores = jnp.where(seen, dot_columns(query, key) * SCORE, NEVER)
        total = jax.nn.logsumexp(scores, axis=-1, keepdims=True)
        found.append(dot(jnp.exp(scores - total).astype(BF), value))
        totals.append(total)
    exact = jnp.concatenate([found[0][:, :HD], found[1][:, HD:], jnp.zeros_like(found[2][:, :HD]), found[2][:, HD:]], 1)
    grid = exact.astype(BF).reshape(count, rows, -1)
    half = rows // 2
    pair = jnp.concatenate([grid[:, :half, 128 + HD :], grid[:, half:, 128 + HD :]], 2)
    grid = jnp.concatenate([grid[:, :, :128], pair], 1)
    pieces = [grid[at[0] ^ k] for k in range(count)]
    totals = jnp.concatenate(totals + [jnp.zeros((count * rows, 125), F32)], 1)
    return (*pieces, exact, totals, q_all, kv_all)


def plain_attend_back(count, blocks, rows, at, grads, q_all, kv_all, exact, totals):
    g_all = jnp.zeros((count, rows, grads[0].shape[1]), BF)
    for k in range(count):
        g_all = g_all.at[at[0] ^ k].set(grads[k])
    g_all = g_all.reshape(count * rows, -1)
    seen = plain_terms(at, count, blocks, rows)
    dq, parts = [], []
    for h, (query, grad, kept) in enumerate(zip(plain_heads(q_all), plain_heads(g_all), plain_heads(exact))):
        key = kv_all[:, :128] if h < 2 else kv_all[:, 256:]
        value = kv_all[:, 128:256] if h < 2 else kv_all[:, 256:]
        delta = jnp.sum(grad.astype(F32) * kept, axis=-1, keepdims=True)
        scores = dot_columns(query, key) * SCORE - totals[:, h : h + 1]
        weights = jnp.exp(jnp.where(seen, scores, NEVER))
        g_scores = (weights * (dot_columns(grad, value) - delta)).astype(BF)
        dq.append(dot(g_scores, key) * SCORE)
        parts.append((dot_rows(g_scores, query) * SCORE, dot_rows(weights.astype(BF), grad)))
    dq = jnp.concatenate([dq[0][:, :HD], dq[1][:, HD:], dq[2][:, :HD], jnp.zeros_like(dq[2][:, :HD])], 1)
    dq = dq.astype(BF).reshape(count, rows, -1)
    acc = jnp.concatenate([parts[0][0] + parts[1][0], parts[0][1] + parts[1][1], parts[2][0] + parts[2][1]], 1)
    acc = acc.reshape(count, blocks, rows, -1)
    dq_all, summed = dq.reshape(count * rows, -1), acc.reshape(-1, acc.shape[-1]).astype(BF)
    own = jnp.concatenate([acc[i, at[1]] for i in range(count)], 0)
    away = [acc[i, at[1] ^ j].astype(BF) for j in range(1, blocks) for i in range(count)]
    return (own, jnp.concatenate(away, 0), dq_all, summed)


def merge_body(at, dq, own, *refs):
    arrived, out = refs[:-1], refs[-1]
    total = own[...]
    for ref in arrived:
        total = total + ref[...].astype(F32)
    out[:, :256] = dq[...]
    out[:, 256:] = total.astype(BF)


def gelu_terms(hidden):
    root = 0.7978845608028654
    square = hidden * hidden
    bend = jnp.tanh(root * hidden * (1.0 + 0.044715 * square))
    half = 0.5 * (1.0 + bend)
    slope = half + 0.5 * hidden * (1.0 - bend * bend) * root * (1.0 + 3.0 * 0.044715 * square)
    return hidden * half, slope


def g_output(extras, rows):
    return jnp.concatenate([(RESIDUAL * ref[:rows, :].astype(F32)).astype(BF) for ref in extras], axis=0)


def split_rows(values, rows, mine, other):
    mine[:rows, :] = values[:rows]
    mine[rows:, :] = values[2 * rows : 3 * rows]
    other[:rows, :] = values[rows : 2 * rows]
    other[rows:, :] = values[3 * rows :]


def middle_body(parts, rows, at, attended, vectors, fc, fc_bias, out, *refs):
    tokens, extras = refs[:parts], refs[parts : 2 * parts]
    gn_mine, gn_other, mid_mine, normed, active, g_hidden, own, att_all, proj = refs[2 * parts :]
    zero = jnp.zeros((HD, proj.shape[1]), BF)
    half = rows // 2
    low = lax.broadcasted_iota(jnp.int32, (half, 128), 1) < HD
    for k in range(parts):
        weight = extras[k][rows:, :]
        owner = at[2] ^ k
        packed = jnp.concatenate([weight[:128], zero, weight[128:]], axis=0)
        proj[rows_at(owner, 256), :] = packed
    size = rows + half
    for j in range(parts):
        for k in range(parts):
            piece = attended[j, k * size : (k + 1) * size, :]
            pair = piece[rows:].astype(F32)
            upper = jnp.where(low, 0.0, pltpu.roll(pair, HD, 1)).astype(BF)
            lower = jnp.where(low, 0.0, pair).astype(BF)
            block = block_of(at, k, rows)
            att_all[block, j * 256 : j * 256 + 128] = piece[:rows]
            att_all[block, j * 256 + 128 : (j + 1) * 256] = jnp.concatenate([upper, lower], axis=0)
    own[...] = att_all[:, pl.ds(pl.multiple_of(at[2] * 256, 256), 256)]
    branch = dot(att_all[...], proj[...]) + vectors[4:5]
    for k in range(parts):
        part = slice(k * rows, (k + 1) * rows)
        value = tokens[k][:rows, :].astype(F32) + RESIDUAL * branch[part]
        if k % 2 == 0:
            mid_mine[(k // 2) * rows : (k // 2 + 1) * rows, :] = value
        unit, _ = normalize(value)
        normed[part, :] = (unit * vectors[2:3] + vectors[3:4]).astype(BF)
    hidden = dot(normed[...], fc[...]) + as_row(fc_bias)
    value, slope = gelu_terms(hidden)
    active[...] = value.astype(BF)
    g_hidden[...] = (dot_columns(g_output(extras, rows), out[...]) * slope).astype(BF)
    split_rows(dot_columns(g_hidden[...], fc[...]), rows, gn_mine, gn_other)


def fill_half(half, bit, kept, away, chunk):
    size = kept.shape[0] // half
    for i in range(half):
        into = slice(i * size, (i + 1) * size)
        kept[into, :] = chunk(bit * half + i)
        away[into, :] = chunk((1 - bit) * half + i).astype(BF)


def proj_grad(attended, g_branch):
    grad = dot_rows(attended[...], g_branch[...])
    return jnp.concatenate([grad[:128], grad[128 + HD :]], axis=0)


def proj_grad_body(rows, at, attended, g_branch, sums_in, grad, sums):
    grad[...] = proj_grad(attended, g_branch)
    sums[...] = sums_in[...]
    sums[4:5, :] = jnp.sum(g_branch[:rows, :].astype(F32), axis=0, keepdims=True)


def pack_wide(values, lanes):
    third = values.shape[0] // 3
    rest = values[:, lanes:]
    low = [rest[i * third : (i + 1) * third] for i in range(3)]
    low.append(jnp.zeros((third, lanes - 384), values.dtype))
    return jnp.concatenate([values[:, :lanes], jnp.concatenate(low, axis=1)], axis=0)


def out_partial_body(rows, at, active, out, mine, other):
    split_rows(dot(active[...], out[...]), rows, mine, other)


def out_weights_body(rows, step, at, active, sums_in, *refs):
    extras = refs[:-4]
    kept, away, sums, grad = refs[-4:]
    g_out = g_output(extras, rows)
    grad[...] = dot_rows(active[...], g_out)
    half = kept.shape[0]
    bit = (at[3] // step) % 2
    kept[...] = grad[rows_at(bit, half), :]
    away[...] = grad[rows_at(1 - bit, half), :].astype(BF)
    sums[...] = sums_in[...]
    sums[5:6, :] = jnp.sum(g_out[:rows].astype(F32), axis=0, keepdims=True)


def fc_weights_body(parts, half, step, at, normed, g_hidden, sums_in, kept, away, sums, grad):
    grad[...] = dot_rows(normed[...], g_hidden[...])
    size = grad.shape[0] // (parts * 2 * half)

    def chunk(i):
        blocks = [((at[2] ^ j) * 2 * half + i) * size for j in range(parts)]
        return jnp.concatenate([grad[pl.ds(pl.multiple_of(start, 8), size), :] for start in blocks], axis=0)

    fill_half(half, (at[3] // step) % 2, kept, away, chunk)
    sums[...] = sums_in[...]
    sums[6:7, :] = jnp.sum(g_hidden[...].astype(F32), axis=0, keepdims=True)


def plain_weights_body(rows, at, active, normed, g_hidden, sums_in, *refs):
    extras = refs[:-3]
    out_grad, fc_grad, sums = refs[-3:]
    g_out = g_output(extras, rows)
    out_grad[...] = dot_rows(active[...], g_out).astype(BF)
    fc_grad[...] = dot_rows(normed[...], g_hidden[...]).astype(BF)
    sums[...] = sums_in[...]
    sums[5:6, :] = jnp.sum(g_out[:rows].astype(F32), axis=0, keepdims=True)
    sums[6:7, :] = jnp.sum(g_hidden[...].astype(F32), axis=0, keepdims=True)


def second_norm_body(rows, at, chip_sum, arrived, mid, own_extra, x_extra, vectors, sums_in, g_branch, own_middle, sums):
    add = arrived[...].astype(F32)
    grad = chip_sum[...] + jnp.concatenate([add[rows:], add[:rows]], axis=0)
    unit, scale = normalize(mid[...])
    back = norm_back(grad, unit, scale, vectors[2:3])
    sums[...] = sums_in[...]
    sums[2:3, :] = jnp.sum(grad[:rows] * unit[:rows], axis=0, keepdims=True)
    sums[3:4, :] = jnp.sum(grad[:rows], axis=0, keepdims=True)
    g_own = back[:rows] + own_extra[:rows, :].astype(F32)
    own_middle[...] = g_own
    g_branch[:rows, :] = (RESIDUAL * g_own).astype(BF)
    g_branch[rows:, :] = (RESIDUAL * (back[rows:] + x_extra[:rows, :].astype(F32))).astype(BF)


def attended_grad_body(parts, rows, at, mine, other, proj, *refs):
    outs, (kept, g_all) = refs[:parts], refs[parts:]
    kept[:rows, :] = mine[:rows, :]
    kept[rows : 2 * rows, :] = other[:rows, :]
    kept[2 * rows : 3 * rows, :] = mine[rows:, :]
    kept[3 * rows :, :] = other[rows:, :]
    zero = jnp.zeros((HD, proj.shape[1]), BF)
    weight = jnp.concatenate([proj[:128, :], zero, proj[128:, :]], axis=0)
    g_all[...] = dot_columns(kept[...], weight).astype(BF)
    for k in range(parts):
        outs[k][...] = g_all[block_of(at, k, rows), :]


def merge_pieces_body(rows, at, dq, own, arrived, *outs):
    for k, out in enumerate(outs):
        part = rows_at(at[0] ^ k, rows)
        out[:, :256] = dq[part, :]
        out[:, 256:] = (own[part, :] + arrived[part, :].astype(F32)).astype(BF)


def first_grad_body(parts, rows, at, matrix, *refs):
    pieces, (mine, other, mixed) = refs[:-3], refs[-3:]
    for i in range(parts):
        if len(pieces) == 1:
            mixed[rows_at(at[2] ^ i, rows), :] = pieces[0][i * rows : (i + 1) * rows, :]
        else:
            mixed[block_of(at, i, rows), :] = pieces[i][...]
    split_rows(dot_columns(mixed[...], matrix[...]), rows, mine, other)


def attn_halves_body(parts, count, at, own, every, dq, dkv, proj, kept, away, sums, grad):
    grad[:, :256] = dot_rows(own[...], dq[...])
    grad[:, 256:] = dot_rows(every[...], dkv[...])
    owner_rows = grad.shape[0] // parts
    size = owner_rows // (2 * count)
    packed = size + size // 3
    start = 0
    for k in range(count):
        place = at[1] * count + (at[0] ^ k)
        other = (1 - at[1]) * count + (at[0] ^ k)
        for j in range(parts):
            base = (at[2] ^ j) * 2 * count
            kept[start : start + size, :] = grad[rows_at(base + place, size), :]
            away[start : start + size, :] = grad[rows_at(base + other, size), :].astype(BF)
            start += size
        kept[start : start + packed, :] = pack_wide(proj[rows_at(place, size), :], grad.shape[1])
        away[start : start + packed, :] = pack_wide(proj[rows_at(other, size), :], grad.shape[1]).astype(BF)
        start += packed
    sums[...] = jnp.zeros_like(sums)
    sums[0:1, :256] = jnp.sum(dq[...].astype(F32), axis=0, keepdims=True)
    sums[0:1, 256:] = jnp.sum(dkv[...].astype(F32), axis=0, keepdims=True)


def attn_pair_body(at, kept, arrived, *outs):
    size = outs[0].shape[0]
    for k, out in enumerate(outs):
        part = slice(k * size, (k + 1) * size)
        out[...] = (kept[part, :] + arrived[part, :].astype(F32)).astype(out.dtype)


def attn_fold_body(count, at, *refs):
    total = refs[0][...]
    for ref in refs[1:count]:
        total = total + ref[...].astype(F32)
    start = 0
    for out in refs[count:]:
        out[...] = total[start : start + out.shape[0]].astype(BF)
        start += out.shape[0]


def attn_place_body(parts, count, at, *refs):
    own, away, (out, proj, kept) = refs[:count], refs[count], refs[count + 1 :]
    features = proj.shape[1]
    width, lanes = features // parts, kept.shape[2]
    size = width // (2 * count)
    total = own[0].shape[0]
    for side in range(2):
        block = at[1] if side == 0 else 1 - at[1]
        for k in range(count):
            piece = own[k][...] if side == 0 else away[k * total : (k + 1) * total, :]
            piece = piece.astype(F32)
            rows = rows_at(block * count + (at[0] ^ k), size)
            for j in range(parts):
                kept[at[2] ^ j, rows, :] = piece[j * size : (j + 1) * size]
            start = parts * size
            proj[rows, :lanes] = piece[start : start + size]
            low = piece[start + size :]
            proj[rows, lanes:] = jnp.concatenate([low[:, i * 128 : (i + 1) * 128] for i in range(3)], axis=0)
    for g in range(parts):
        first = g * width
        out[:, first : first + width] = kept[g, :, :width]
        first += features
        out[:, first : first + width] = jnp.concatenate([kept[g, :, 256:384], kept[g, :, 512 : 512 + HD]], axis=1)
        first += features
        out[:, first : first + width] = jnp.concatenate([kept[g, :, 384:512], kept[g, :, 512 + HD :]], axis=1)


def attn_weights_body(parts, ways, at, own, every, dq, dkv, grads, sums):
    query = dot_rows(own[...], dq[...])
    pair = dot_rows(every[...], dkv[...])
    size = query.shape[0] // (parts * ways)
    for c in range(ways):
        for j in range(parts):
            at_row = (j * ways + c) * size
            grads[c * parts + j, :, :256] = query[at_row : at_row + size].astype(BF)
            grads[c * parts + j, :, 256:] = pair[at_row : at_row + size].astype(BF)
    sums[...] = jnp.zeros_like(sums)
    sums[0:1, :256] = jnp.sum(dq[...].astype(F32), axis=0, keepdims=True)
    sums[0:1, 256:] = jnp.sum(dkv[...].astype(F32), axis=0, keepdims=True)


def attn_sum_body(parts, ways, at, arrived, out):
    for j in range(parts):
        total = arrived[j].astype(F32)
        for c in range(1, ways):
            total = total + arrived[c * parts + j].astype(F32)
        total = total.astype(BF)
        for c in range(ways):
            out[c, j, :, :] = total


def attn_final_body(parts, ways, at, arrived, out):
    size = arrived.shape[2]
    width = size * ways
    features = out.shape[1] // 3
    for c in range(ways):
        rows = slice(c * size, (c + 1) * size)
        for g in range(parts):
            piece = arrived[c, g].astype(F32)
            first = g * width
            out[rows, first : first + width] = piece[:, :width]
            first += features
            out[rows, first : first + width] = jnp.concatenate([piece[:, 256:384], piece[:, 512 : 512 + HD]], axis=1)
            first += features
            out[rows, first : first + width] = jnp.concatenate([piece[:, 384:512], piece[:, 512 + HD :]], axis=1)


def first_norm_body(rows, at, own, core, arrived, tokens, own_middle, vectors, sums, attn, input_grad, shares):
    grad = own[:rows, :] + core[:rows, :] + arrived[...].astype(F32)
    unit, scale = normalize(tokens[...].astype(F32))
    back = norm_back(grad, unit, scale, vectors[0:1])
    input_grad[...] = (back + own_middle[...]).astype(BF)
    first = [jnp.sum(grad * unit, axis=0, keepdims=True), jnp.sum(grad, axis=0, keepdims=True)]
    whole = jnp.concatenate(first + [sums[2:6, :], jnp.zeros((2, grad.shape[1]), F32)], axis=0)
    parts = whole.shape[1] // HD // 3
    width = whole.shape[1] // parts
    part = sums.shape[1] // 4
    value = jnp.concatenate([attn[0:1, 384:512], attn[0:1, 512 + HD :]], axis=1)
    local = [sums[6:7, i * part : (i + 1) * part] for i in range(4)] + [attn[0:1, :width], value]
    local = jnp.concatenate(local + [jnp.zeros((2, width), F32)], axis=0)
    blank = jnp.zeros((8, 256 - width), F32)
    for j in range(parts):
        piece = jnp.concatenate([whole[:, j * width : (j + 1) * width], blank, local, blank], axis=1)
        for c in range(shares.shape[0] // parts):
            shares[c * parts + j, :, :] = piece


def vector_final_body(ways, parts, at, arrived, *outs):
    width, hidden = outs[0].shape[0], outs[8].shape[0]
    total, local = jnp.zeros((8, arrived.shape[2]), F32), jnp.zeros((8, arrived.shape[2]), F32)
    for i in range(ways * parts):
        total = total + arrived[i]
    for c in range(ways):
        local = local + arrived[c * parts + at[2]]
    for row in range(6):
        outs[row][...] = total[row : row + 1, :width].reshape(width)
    part = hidden // 4
    outs[8][...] = jnp.concatenate([local[i : i + 1, 256 : 256 + part] for i in range(4)], axis=1).reshape(hidden)
    outs[6][...] = local[4:5, 256 : 256 + width].reshape(width)
    outs[7][...] = local[5:6, 256 : 256 + width].reshape(width)


def halve_body(step, at, held, arrived, kept, away, total):
    total[...] = held[...] + arrived[...].astype(F32)
    half = kept.shape[0]
    bit = (at[3] // step) % 2
    kept[...] = total[pl.ds(pl.multiple_of(bit * half, 8), half), :]
    away[...] = total[pl.ds(pl.multiple_of((1 - bit) * half, 8), half), :].astype(BF)


def last_sum_body(at, held, arrived, *outs):
    total = held[...] + arrived[...].astype(F32)
    start = 0
    for out in outs:
        out[...] = total[start : start + out.shape[0]].astype(BF)
        start += out.shape[0]


def stack_rows_body(at, *refs):
    out = refs[-1]
    start = 0
    for ref in refs[:-1]:
        out[start : start + ref.shape[0], :] = ref[...]
        start += ref.shape[0]


def chunk_number(at, mask, steps):
    number = 0
    for step in steps:
        number = number * 2 + ((at[3] ^ mask) // step) % 2
    return number


def chunks_of(at, steps, refs):
    masks = [0]
    found = [(0, refs[0], 0)]
    for step, ref in zip(reversed(steps), refs[1:]):
        found += [(mask ^ step, ref, i) for i, mask in enumerate(masks)]
        masks = masks + [mask ^ step for mask in masks]
    size = refs[0].shape[0]
    for mask, ref, i in found:
        yield chunk_number(at, mask, steps), ref[i * size : (i + 1) * size, :].astype(F32)


def out_final_body(steps, at, *refs):
    for place, piece in chunks_of(at, steps, refs[:-1]):
        refs[-1][rows_at(place, piece.shape[0]), :] = piece


def fc_final_body(parts, steps, at, *refs):
    out = refs[-1]
    hidden = out.shape[1] // parts
    for place, piece in chunks_of(at, steps, refs[:-1]):
        size = piece.shape[0] // parts
        for j in range(parts):
            lanes = pl.ds(pl.multiple_of((at[2] ^ j) * hidden, 128), hidden)
            out[rows_at(place, size), lanes] = piece[j * size : (j + 1) * size]


class Values:
    pass


def shards(
    parts,
    ways,
    tokens,
    first_gain,
    first_bias,
    attn_weight,
    query_bias,
    value_bias,
    proj_weight,
    proj_bias,
    second_gain,
    second_bias,
    fc_weight,
    fc_bias,
    out_weight,
    out_bias,
    cotangent,
):
    rows, features = tokens.shape[1], tokens.shape[2]
    width = features // parts
    count = parts
    blocks = ways // count
    hidden = fc_weight.shape[1] // parts
    columns = 256 + 2 * width
    all_rows, half_rows = parts * rows, parts * rows // 2
    f = lax.axis_index("fsdp").astype(jnp.int32)
    c = lax.axis_index("ctx").astype(jnp.int32)
    at = jnp.stack([c // blocks, c % blocks, f, c])
    halved = ways == 8
    chunks, size = 4, width // 8
    packed = size + size // 3
    small_blocks = blocks * count * rows <= 1024
    last = []
    v = Values()

    def run(body, outs, *args, mib=16, scratch=()):
        task = v.task
        held = [] if task in v.free else last
        hooked = jax.tree.leaves(v.hooks[task]()) if task in v.hooks else []
        made = call(
            body,
            task.__name__,
            outs,
            at,
            *args,
            scratch=scratch,
            after=[*held, *hooked],
            us=v.costs.get(task, 1.0),
            mib=mib,
        )
        if task not in v.free:
            last[:] = [made[-1]]
        return made

    def over_fsdp(value, k):
        return lax.ppermute(value, "fsdp", [(i, i ^ k) for i in range(parts)])

    def over_ctx(value, k):
        return lax.ppermute(value, "ctx", [(i, i ^ k) for i in range(ways)])

    def spread(value):
        across = over_fsdp(value, 2)
        return [value, over_fsdp(value, 1), across, over_fsdp(across, 1)]

    def turn_fsdp(pieces):
        return [pieces[0]] + [over_fsdp(pieces[k], k) for k in range(1, parts)]

    def turn_ctx(pieces):
        return [pieces[0]] + [over_ctx(pieces[k], k * blocks) for k in range(1, count)]

    def halve(kept, arrived, step):
        half, lanes = kept.shape[0] // 2, kept.shape[1]
        outs = [shape((half, lanes), F32), shape((half, lanes), BF)]
        return run(partial(halve_body, step), outs, kept, arrived, scratch=[pltpu.VMEM((2 * half, lanes), F32)])

    def last_sum(kept, arrived, cuts):
        return run(last_sum_body, [shape((cut, kept.shape[1]), BF) for cut in cuts], kept, arrived)

    def stacked(pieces):
        total = sum(piece.shape[0] for piece in pieces)
        return run(stack_rows_body, [shape((total, pieces[0].shape[1]), BF)], *pieces)[0]

    v.sums = jnp.zeros((8, features), F32)

    def attn_columns():
        outs = [shape((width, columns), BF)] * parts
        v.attn_pieces = turn_fsdp(run(partial(attn_columns_body, parts), outs, attn_weight))
        v.attn_core = [v.attn_pieces[1]]

    def token_message():
        args = (tokens[0], first_gain, first_bias, second_gain, second_bias, proj_bias, out_bias)
        v.tokens = spread(run(token_message_body, [shape((rows + 8, features), BF)], *args)[0])

    def fc_columns():
        outs = [shape((width, hidden), BF)] * parts
        v.fc_columns = turn_fsdp(run(fc_columns_body, outs, fc_weight))
        v.fc_core = [v.fc_columns[1]]

    def mixed():
        made = run(
            partial(mixed_body, parts, count),
            [shape((all_rows, features), BF), shape((features, columns), BF), shape((8, features), F32)]
            + [shape((5 * rows // 2, 256), BF)] * count
            + [shape((rows, 384), BF)] * count,
            query_bias,
            value_bias,
            *v.tokens,
            *v.attn_pieces,
            scratch=[pltpu.VMEM((all_rows, columns), BF)],
        )
        v.attn_matrix, v.vectors = made[1:3]
        v.pairs = turn_ctx(made[3 + count :])
        v.queries = turn_ctx(made[3 : 3 + count])

    def stack_pairs():
        joined = stacked(v.pairs)
        v.partners = [over_ctx(joined, j) for j in range(1, blocks)]

    def join_fc():
        v.fc_matrix = run(join_body, [shape((features, hidden), BF)], *v.fc_columns)[0]

    def stack_extra():
        v.extra = spread(stacked([cotangent[0], proj_weight]))
        v.extra_across = [v.extra[2]]

    def attend():
        kept = run(
            partial(attend_body, count, blocks, rows),
            [shape((rows + rows // 2, 128), BF)] * count
            + [
                shape((count * rows, 256), F32),
                shape((count * rows, 128), F32),
                shape((count * rows, 256), BF),
                shape((count * blocks * rows, 384), BF),
            ],
            *v.queries,
            *v.pairs,
            *v.partners,
        )
        v.att_pieces, v.state = turn_ctx(kept[:count]), kept[count:]

    def plain_front():
        kept = plain_attend(count, blocks, rows, at, v.queries, v.pairs, v.partners)
        v.att_pieces, v.state = turn_ctx(kept[:count]), kept[count:]

    def normed_stack():
        outs = [shape((count * rows, features // 2), BF)]
        own = run(partial(normed_stack_body, rows), outs, *v.queries)[0]
        v.normed_across = [over_ctx(own, j) for j in range(1, blocks)]
        v.normed_sides = [own] + v.normed_across

    def middle():
        attended_all = lax.all_gather(jnp.concatenate(v.att_pieces, 0), "fsdp")
        gn_mine, gn_other, v.mid_mine, v.normed_two, v.active, v.g_hidden, v.attended = run(
            partial(middle_body, parts, rows),
            [shape((half_rows, features), F32)] * 3
            + [shape((all_rows, features), BF), shape((all_rows, hidden), BF), shape((all_rows, hidden), BF)]
            + [shape((all_rows, 256), BF)],
            attended_all,
            v.vectors,
            v.fc_matrix,
            fc_bias,
            out_weight,
            *v.tokens,
            *v.extra,
            scratch=[pltpu.VMEM((all_rows, parts * 256), BF), pltpu.VMEM((parts * 256, features), BF)],
            mib=24,
        )
        v.chip_sum = gn_mine + over_fsdp(gn_other, 1)
        v.chip_low = v.chip_sum.astype(BF)
        v.arrived = over_fsdp(v.chip_low, 2)


    def place():
        sides = v.normed_sides + [over_fsdp(side, 1) for side in v.normed_sides]
        v.every, v.own_rows = run(
            partial(normed_place_body, count, blocks, rows),
            [shape((count * blocks * rows, features), BF), shape((count * rows, features), BF)],
            *sides,
        )

    def fc_weights():
        v.fc_kept, away, v.sums = run(
            partial(fc_weights_body, parts, chunks, FC_STEPS[0]),
            [shape((features // 2, hidden), F32), shape((features // 2, hidden), BF), shape((8, features), F32)],
            v.normed_two,
            v.g_hidden,
            v.sums,
            scratch=[pltpu.VMEM((features, hidden), F32)],
        )
        v.fc_in = over_ctx(away, FC_STEPS[0])

    def out_weights():
        v.out_kept, away, v.sums = run(
            partial(out_weights_body, rows, OUT_STEPS[0]),
            [shape((hidden // 2, features), F32), shape((hidden // 2, features), BF), shape((8, features), F32)],
            v.active,
            v.sums,
            *v.extra,
            scratch=[pltpu.VMEM((hidden, features), F32)],
        )
        v.out_in = over_ctx(away, OUT_STEPS[0])

    def both_weights():
        v.out_grad, v.fc_grad, v.sums = run(
            partial(plain_weights_body, rows),
            [shape((hidden, features), BF), shape((features, hidden), BF), shape((8, features), F32)],
            v.active,
            v.normed_two,
            v.g_hidden,
            v.sums,
            *v.extra,
        )

    def second_norm():
        v.g_branch, v.own_middle, v.sums = run(
            partial(second_norm_body, rows),
            [shape((half_rows, features), BF), shape((rows, features), F32), shape((8, features), F32)],
            v.chip_sum,
            v.arrived,
            v.mid_mine,
            v.extra[0],
            v.extra[2],
            v.vectors,
            v.sums,
        )

    def attended_grad():
        grads = run(
            partial(attended_grad_body, parts, rows),
            [shape((rows, 256), BF)] * parts + [shape((all_rows, features), BF)],
            v.g_branch,
            over_fsdp(v.g_branch, 1),
            proj_weight,
            scratch=[pltpu.VMEM((all_rows, 256), BF)],
        )
        v.g_pieces, v.g_branch_all = turn_ctx(grads[:parts]), grads[parts]

    def proj_weights():
        v.proj, v.sums = run(
            partial(proj_grad_body, rows),
            [shape((width, features), F32), shape((8, features), F32)],
            v.attended,
            v.g_branch_all,
            v.sums,
        )

    def fc_one():
        v.fc_kept, away = halve(v.fc_kept, v.fc_in, FC_STEPS[1])
        v.fc_in = over_ctx(away, FC_STEPS[1])

    def fc_two():
        v.fc_kept, away = halve(v.fc_kept, v.fc_in, FC_STEPS[2])
        v.fc_in = over_ctx(away, FC_STEPS[2])

    def fc_sum():
        v.fc_parts = turn_fsdp(last_sum(v.fc_kept, v.fc_in, [size] * parts))

    def fc_turned():
        part = stacked(v.fc_parts)
        v.fc_pieces = [part, over_ctx(part, FC_STEPS[2])]

    def fc_double():
        v.fc_pieces.append(over_ctx(stacked(v.fc_pieces), FC_STEPS[1]))

    def fc_fourfold():
        v.fc_pieces.append(over_ctx(stacked(v.fc_pieces), FC_STEPS[0]))

    def fc_final():
        outs = [shape((width, parts * hidden), F32)]
        v.fc_weight_grad = run(partial(fc_final_body, parts, FC_STEPS), outs, *v.fc_pieces)[0]

    def out_one():
        v.out_kept, away = halve(v.out_kept, v.out_in, OUT_STEPS[1])
        v.out_in = over_ctx(away, OUT_STEPS[1])

    def out_two():
        v.out_kept, away = halve(v.out_kept, v.out_in, OUT_STEPS[2])
        v.out_in = over_ctx(away, OUT_STEPS[2])

    def out_sum():
        part = last_sum(v.out_kept, v.out_in, [hidden // 8])[0]
        v.out_pieces = [part, over_ctx(part, OUT_STEPS[2])]

    def out_double():
        v.out_pieces.append(over_ctx(stacked(v.out_pieces), OUT_STEPS[1]))

    def out_fourfold():
        v.out_pieces.append(over_ctx(stacked(v.out_pieces), OUT_STEPS[0]))

    def out_final():
        outs = [shape((hidden, features), F32)]
        v.out_weight_grad = run(partial(out_final_body, OUT_STEPS), outs, *v.out_pieces)[0]

    def attend_back():
        v.own, away, v.dq, v.dkv = run(
            partial(attend_back_body, count, blocks, rows),
            [
                shape((count * rows, 384), F32),
                shape(((blocks - 1) * count * rows, 384), BF),
                shape((count * rows, 256), BF),
                shape((count * blocks * rows, 384), BF),
            ],
            *v.g_pieces,
            v.state[2],
            v.state[3],
            *v.state[:2],
            scratch=[pltpu.VMEM((count * rows, 256), BF), pltpu.VMEM((count * blocks * rows, 384), F32)],
        )
        v.from_partners = [over_ctx(away, 1)]

    def plain_back():
        v.own, away, v.dq, v.dkv = plain_attend_back(
            count, blocks, rows, at, v.g_pieces, v.state[2], v.state[3], *v.state[:2]
        )
        stack = count * rows
        v.from_partners = [over_ctx(away[(j - 1) * stack : j * stack], j) for j in range(1, blocks)]

    def attn_weights():
        outs = [shape((count * (parts * size + packed), columns), kind) for kind in (F32, BF)]
        v.attn_kept, away, v.sums_attn = run(
            partial(attn_halves_body, parts, count),
            outs + [shape((8, columns), F32)],
            v.own_rows,
            v.every,
            v.dq,
            v.dkv,
            v.proj,
            scratch=[pltpu.VMEM((features, columns), F32)],
        )
        v.attn_in = over_ctx(away, 1)

    def attn_pair():
        outs = [shape((parts * size + packed, columns), kind) for kind in (F32, BF, BF, BF)]
        v.attn_sent = turn_ctx(run(attn_pair_body, outs, v.attn_kept, v.attn_in))

    def attn_fold():
        outs = [shape((size, columns), BF)] * parts + [shape((packed, columns), BF)]
        *attn_parts, v.proj = run(partial(attn_fold_body, count), outs, *v.attn_sent)
        v.attn_parts = turn_fsdp(attn_parts)

    def attn_turned():
        v.attn_pieces = turn_ctx([stacked([*v.attn_parts, v.proj])] * count)

    def attn_fourfold():
        v.attn_pieces.append(over_ctx(stacked(v.attn_pieces), 1))

    def attn_final():
        outs = [shape((width, 3 * features), F32), shape((width, features), F32)]
        v.attn_weight_grad, v.proj_weight_grad = run(
            partial(attn_place_body, parts, count),
            outs,
            *v.attn_pieces,
            scratch=[pltpu.VMEM((parts, width, columns), F32)],
        )

    def plain_attn_weights():
        attn_grads, v.sums_attn = run(
            partial(attn_weights_body, parts, ways),
            [shape((parts * ways, width // ways, columns), BF), shape((8, columns), F32)],
            v.own_rows,
            v.every,
            v.dq,
            v.dkv,
        )
        attn_in = lax.all_to_all(attn_grads, ("ctx", "fsdp"), split_axis=0, concat_axis=0, tiled=True)
        outs = [shape((ways, parts, width // ways, columns), BF)]
        attn_sum = run(partial(attn_sum_body, parts, ways), outs, attn_in)[0]
        attn_all = lax.all_to_all(attn_sum, "ctx", split_axis=0, concat_axis=0, tiled=True)
        outs = [shape((width, 3 * features), F32)]
        v.attn_weight_grad = run(partial(attn_final_body, parts, ways), outs, attn_all)[0]

    def merge():
        outs = [shape((count * rows, columns), BF)]
        if MERGE_PERMUTES and halved:
            outs = [shape((rows, columns), BF)] * count
            pieces = run(partial(merge_pieces_body, rows), outs, v.dq, v.own, *v.from_partners)
            v.g_mixed = turn_ctx(pieces)
            return
        made = run(merge_body, outs, v.dq, v.own, *v.from_partners)[0]
        groups = [[i * blocks + j for i in range(count)] for j in range(blocks)]
        v.g_mixed = lax.all_to_all(made, "ctx", split_axis=0, concat_axis=0, tiled=True, axis_index_groups=groups)

    def out_partial():
        outs = [shape((half_rows, features), F32)] * 2
        mine, other = run(partial(out_partial_body, rows), outs, v.active, out_weight)
        core = over_fsdp(other, 1)
        across = over_fsdp((mine[rows:] + core[rows:]).astype(BF), 2)
        output = mine[:rows] + core[:rows] + across.astype(F32) + v.vectors[5:6]
        v.block_out = (v.mid_mine[:rows] + RESIDUAL * output).astype(BF)

    def first_grad():
        mine, other = run(
            partial(first_grad_body, parts, rows),
            [shape((half_rows, features), F32)] * 2,
            v.attn_matrix,
            *(v.g_mixed if MERGE_PERMUTES and halved else [v.g_mixed]),
            scratch=[pltpu.VMEM((all_rows, columns), BF)],
        )
        arrived = over_fsdp(other, 1)
        v.first_own = (mine, arrived)
        v.first_in = over_fsdp((mine[rows:] + arrived[rows:]).astype(BF), 2)

    def first_norm():
        v.input_grad, shares = run(
            partial(first_norm_body, rows),
            [shape((rows, features), BF), shape((parts * ways, 8, 512), F32)],
            *v.first_own,
            v.first_in,
            tokens[0],
            v.own_middle,
            v.vectors,
            v.sums,
            v.sums_attn,
        )
        v.shares = lax.all_to_all(shares, ("ctx", "fsdp"), split_axis=0, concat_axis=0, tiled=True)

    def vector_final():
        outs = [shape((width,), F32)] * 8 + [shape((hidden,), F32)]
        v.vector_grads = run(partial(vector_final_body, ways, parts), outs, v.shares)

    def gather_rest():
        def over_all(value):
            part = lax.psum_scatter(value, "ctx", scatter_dimension=1, tiled=True)
            return lax.all_gather(part, "ctx", axis=1, tiled=True)

        v.out_weight_grad = over_all(v.out_grad).astype(F32)
        v.proj_weight_grad = over_all(v.proj.astype(BF)).astype(F32)
        fc_grad = over_all(v.fc_grad).reshape(parts, width, hidden)
        fc_grad = lax.all_to_all(fc_grad, "fsdp", split_axis=0, concat_axis=0)
        v.fc_weight_grad = fc_grad.transpose(1, 0, 2).reshape(width, parts * hidden).astype(F32)

    v.free = {
        attn_pair, fc_final, fc_fourfold, fc_one, fc_two, out_double, out_final, out_partial, out_sum, vector_final,
    }
    v.hooks = {
        attend: lambda: [v.extra_across],
        attn_pair: lambda: [v.from_partners],
        fc_columns: lambda: [v.attn_core],
        fc_weights: lambda: [v.chip_low],
        middle: lambda: [v.normed_across],
        mixed: lambda: [v.fc_core],
        normed_stack: lambda: [v.attn_core],
        out_partial: lambda: [v.queries],
        out_weights: lambda: [v.chip_low],
        place: lambda: [v.chip_low],
    }
    v.costs = {merge: 1.0, out_sum: 1000000.0}
    front = (attn_columns, token_message, fc_columns, mixed, stack_pairs, join_fc, stack_extra)
    if halved:
        order = (
            attn_columns, token_message, fc_columns, mixed, stack_pairs, join_fc, stack_extra, attend, normed_stack,
            middle, fc_weights, out_weights, second_norm, attended_grad, fc_one, proj_weights, place, out_one,
            attend_back, attn_weights, fc_two, out_two, fc_sum, merge, fc_turned, first_grad, attn_pair, out_sum,
            first_norm, out_double, fc_double, attn_fold, out_partial, out_fourfold, attn_turned, attn_fourfold,
            out_final, fc_fourfold, vector_final, fc_final, attn_final,
        )
    else:
        order = (*front, plain_front, normed_stack, middle, place, both_weights, second_norm, attended_grad)
        order += (proj_weights, plain_back, plain_attn_weights, merge, first_grad, out_partial, first_norm)
        order += (vector_final, gather_rest)
    for task in order:
        v.task = task
        task()
    first_gain_grad, first_bias_grad, second_gain_grad, second_bias_grad = v.vector_grads[:4]
    proj_bias_grad, out_bias_grad, query_bias_grad, value_bias_grad, fc_bias_grad = v.vector_grads[4:]
    return (
        v.block_out[None],
        v.input_grad[None],
        first_gain_grad,
        first_bias_grad,
        v.attn_weight_grad,
        query_bias_grad,
        value_bias_grad,
        v.proj_weight_grad,
        proj_bias_grad,
        second_gain_grad,
        second_bias_grad,
        v.fc_weight_grad,
        fc_bias_grad,
        v.out_weight_grad,
        out_bias_grad,
    )


def solution(mesh):
    rows, row, matrix = P("fsdp", "ctx", None), P("fsdp"), P("fsdp", None)
    return jax.shard_map(
        partial(shards, mesh.shape["fsdp"], mesh.shape["ctx"]),
        mesh=mesh,
        in_specs=(
            rows, row, row, matrix, row, row, matrix, row, row, row, matrix, row, matrix, row, rows,
        ),
        out_specs=(
            rows, rows, row, row, matrix, row, row, matrix, row, row, row, matrix, row, matrix, row,
        ),
        check_vma=False,
    )
```
